256 devices in a mesh: kz: 16 (over y_hi, x, core), ky: 16 (over z, y_lo).
Axes of the slice: x: 4, y: 4 (y_hi: 2, y_lo: 2; y = y_hi * 2 + y_lo), z: 8, core: 2. Of those that a mesh axis runs over, the one named last changes fastest.
Arguments:
- slice_re: bfloat16 [256, 512, 512], P('kz', 'ky'), may hold values from -6 to 6
- slice_im: bfloat16 [256, 512, 512], P('kz', 'ky'), may hold values from -6 to 6
- slice_ctf: bfloat16 [256, 512, 512], P('kz', 'ky'), may hold values from -1 to 1
- slice_dest: int32 [256, 1], P('kz'), may hold values from 0 to 15; in each aligned block of 16 rows (0 to 15, 16 to 31, ...) at most 4 rows name the same one
- slice_plane: int32 [256], P('kz'), may hold values from 0 to 3
- helix_index: int32 [256], P('kz'), may hold values from 0 to 7
- slice_tilt: bfloat16 [256], P('kz'), may hold values from -2 to 2
- slice_shift: bfloat16 [2, 256], P(None, 'kz'), may hold values from 0 to 1
Outputs:
- folded: float32 [3, 64, 1024, 1024], P(None, 'kz', 'ky')
The draws below stay inside these ranges and needn't reach their ends.
Inputs may be any that keep to these rules, and one draw needn't show every extreme that they name: `slice_dest`: within each aligned block of 16 slices (the slices of one kz slab), at most 4 name the same slab, a bound that some block reaches of them.
All inputs are finite; a program needn't handle non-finite values.
Results may differ from the reference program's by a relative error of at most 0.0049.
Values may be sent and summed in bfloat16 or wider, within the bound.
A program may use at most 128 MiB of HBM per device.

```python
import math
import jax
import jax.numpy as jnp
import numpy as np
from jax import lax

SL = 512
SLK = 16
ZD = 4
MZ = 4
HSYM = 8
CAP = 4
NSL = 256
NZ = 64
NY = 1024
NX = 1024
ZE = 12
N_KZ = 16


def touch_ends(drawn, key, low, high):
    dims = drawn.shape
    spot = [jax.random.randint(jax.random.fold_in(key, axis), (), 0, dims[axis]) for axis in range(len(dims))]
    drawn = drawn.at[tuple(spot)].set(low)
    longest = dims.index(max(dims))
    spot[longest] = (spot[longest] + 1) % dims[longest]
    return drawn.at[tuple(spot)].set(high)


def level_of(own_key, extent, pieces, least, top_value):
    factor_of, own = 1.0, jax.random.fold_in(own_key, 6)
    for dim, parts in pieces:
        draws = jnp.exp(jax.random.uniform(jax.random.fold_in(own, dim), (parts,), jnp.float32, least / len(pieces), top_value / len(pieces)))
        factor_of = factor_of * jnp.repeat(draws, extent[dim] // parts).reshape([-1 if axis == dim else 1 for axis in range(len(extent))])
    return factor_of


def shared_out(own_key, own, number, rows, count, top, reach, slope):
    ranking = jax.random.permutation(own_key, count)
    crowded, common = shares(count, rows * top, reach, slope, True), shares(count, rows * top, reach, slope, False)
    places = jnp.arange(count)

    def named(lengths, turn):
        used = int((lengths > 0).sum())
        fixed = max(1, used // 4)
        shifted = fixed + (places - fixed + turn * (used - fixed)) % max(1, count - fixed)
        return jnp.zeros((count,), jnp.int32).at[ranking[jnp.where(places < fixed, places, shifted)]].set(jnp.asarray(lengths, jnp.int32))

    lengths = jnp.where(number % 4 == 0, named(crowded, number // 4), named(common, number - number // 4 - 1))
    mixed = jax.random.permutation(jax.random.fold_in(own, 3), count)
    source_of, receiver = mixed[0:count // 2 * 2:2], mixed[1:count // 2 * 2:2]
    margin = jnp.minimum(lengths[source_of] - 1, reach - lengths[receiver]) // 2
    margin = jnp.where((source_of == ranking[0]) | (receiver == ranking[0]) | (lengths[receiver] == 0), 0, jnp.maximum(margin, 0))
    shifted = jax.random.randint(jax.random.fold_in(own, 4), (count // 2,), 0, 1 << 20) % (margin + 1)
    lengths = lengths.at[source_of].add(-shifted).at[receiver].add(shifted)
    members = jnp.searchsorted(jnp.cumsum(lengths), jnp.arange(rows * top), side="right").astype(jnp.int32)
    table = members.reshape(top, rows).T
    table = table[jax.random.permutation(jax.random.fold_in(own, 1), rows)]
    turn = jax.random.randint(jax.random.fold_in(own, 2), (rows, 1), 0, top)
    return jnp.take_along_axis(table, (jnp.arange(top)[None, :] + turn) % top, axis=1)


def shares(amount, total, reach, skew, full):
    weights = [(1 << 20) // math.isqrt(rank ** skew) + 1 for rank in range(1, amount + 1)]
    largest = reach if full else min(reach, max(-(-total // amount), total * weights[0] // sum(weights)))
    least = 1 if total - largest >= amount - 1 else 0
    holding, rest = [largest] + [least] * (amount - 1), total - largest - least * (amount - 1)
    while rest > 0:
        free = [i for i in range(1, amount) if holding[i] < largest] or [i for i in range(1, amount) if holding[i] < reach]
        whole, budget = sum([weights[i] for i in free]), rest
        for i in free:
            addition = min(reach - holding[i], max(1, budget * weights[i] // whole), rest)
            holding[i] = holding[i] + addition
            rest = rest - addition
    return np.array(holding)


def gaussian(stream_key, dims, scale, limit, pieces=(), kind=jnp.bfloat16):
    values = scale * jax.random.normal(stream_key, dims, jnp.float32)
    if pieces:
        values = values * level_of(stream_key, dims, pieces, -0.22, 0.18)
    return jnp.clip(values, -limit, limit).astype(kind)


def setup_inputs(seed: int = 0) -> dict:
    streams_of = jax.random.split(jax.random.key(seed), 9)
    slice_re = gaussian(streams_of[0], (NSL, SL, SL), 1.0, 6.0, ((0, 16), (1, 16)))
    slice_im = gaussian(streams_of[1], (NSL, SL, SL), 1.0, 6.0, ((0, 16), (1, 16)))
    slice_ctf = jnp.clip(jax.random.uniform(streams_of[2], (NSL, SL, SL), jnp.float32, -1.0, 1.0) * level_of(streams_of[2], (NSL, SL, SL), ((0, 16), (1, 16)), -0.4, 0.0), -1.0, 1.0).astype(jnp.bfloat16)
    slice_dest_keys = jax.random.split(jax.random.fold_in(streams_of[3], 1), NSL // SLK)
    slice_dest_turns = jax.random.permutation(jax.random.fold_in(streams_of[3], 3), NSL // SLK)
    slice_dest = jax.vmap(lambda own, number: shared_out(jax.random.fold_in(streams_of[3], 2), own, number, SLK, N_KZ, 1, CAP, 2))(slice_dest_keys, slice_dest_turns).reshape((NSL, 1))
    slice_plane = touch_ends(jax.random.randint(streams_of[4], (NSL,), 0, ZD), jax.random.fold_in(streams_of[4], 1), 0, ZD - 1).astype(jnp.int32)
    helix_index = touch_ends(jax.random.randint(streams_of[5], (NSL,), 0, HSYM), jax.random.fold_in(streams_of[5], 1), 0, HSYM - 1).astype(jnp.int32)
    slice_tilt = jnp.clip(jax.random.uniform(streams_of[6], (NSL,), jnp.float32, -2.0, 2.0) * level_of(streams_of[6], (NSL,), ((0, 16),), -0.4, 0.0), -2.0, 2.0).astype(jnp.bfloat16)
    slice_shift = jnp.clip(1.0 * jax.random.uniform(streams_of[7], (2, NSL), jnp.float32) ** level_of(streams_of[7], (2, NSL), ((1, 16),), -0.2, 0.2), 0.0, 1.0).astype(jnp.bfloat16)
    return dict(slice_re=slice_re, slice_im=slice_im, slice_ctf=slice_ctf, slice_dest=slice_dest, slice_plane=slice_plane, helix_index=helix_index, slice_tilt=slice_tilt, slice_shift=slice_shift)


kernel_beta = 7.4
kernel_reach = 2.0
twist_step = 0.37

def bessel_zero(value):
    quarter = value * value * 0.25
    term = jnp.ones_like(value)
    total = term
    for order in range(1, 26):
        term = term * quarter / float(order * order)
        total = total + term
    return total

def kaiser(distance):
    inside = jnp.clip(1.0 - (distance / kernel_reach) ** 2, 0.0, 1.0)
    scale = bessel_zero(jnp.asarray(kernel_beta, distance.dtype)) - 1.0
    return (bessel_zero(kernel_beta * jnp.sqrt(inside)) - 1.0) / scale

def rounded(value):
    return lax.optimization_barrier(value.astype(jnp.bfloat16)).astype(jnp.float32)

def reference(slice_re, slice_im, slice_ctf, slice_dest, slice_plane, helix_index, slice_tilt, slice_shift):
    xcoord = jnp.arange(NX)
    ycoord = jnp.arange(NY)
    plane_ids = jnp.arange(ZE) - MZ

    def insert(index, volume):
        ctf = slice_ctf[index].astype(jnp.float32)
        data = rounded(jnp.stack([ctf * slice_re[index].astype(jnp.float32), ctf * slice_im[index].astype(jnp.float32), ctf * ctf]))
        offset_y = slice_shift[0, index].astype(jnp.float32)
        offset_x = slice_shift[1, index].astype(jnp.float32)
        spread = jnp.zeros((3, SL, NX), jnp.float32)
        for tap_index in range(3):
            column = (xcoord // 2 - 1 + tap_index) % SL
            delta = ((xcoord - 2 * column + NX // 2) % NX - NX // 2).astype(jnp.float32) - offset_x
            spread = spread + data[:, :, column] * rounded(kaiser(delta))
        spread = rounded(spread)
        target = slice_dest[index, 0]
        plane = slice_plane[index].astype(jnp.float32)
        tilt = slice_tilt[index].astype(jnp.float32)
        global_plane = target * ZD + plane_ids
        angle = twist_step * (helix_index[index] * global_plane).astype(jnp.float32)
        cosine = jnp.cos(angle)[:, None]
        sine = jnp.sin(angle)[:, None]
        contrib = jnp.zeros((3, ZE, NY, NX), jnp.float32)
        for tap_index in range(3):
            row = (ycoord // 2 - 1 + tap_index) % SL
            centre = plane + tilt * (row - SL // 2).astype(jnp.float32) / (SL // 2)
            along_z = kaiser(plane_ids.astype(jnp.float32)[:, None] - centre[None, :])
            lag_y = ((ycoord - 2 * row + NY // 2) % NY - NY // 2).astype(jnp.float32) - offset_y
            joint = along_z * kaiser(lag_y)[None, :]
            kreal = rounded(joint * cosine)[:, :, None]
            kimag = rounded(joint * sine)[:, :, None]
            kweight = rounded(joint)[:, :, None]
            picked = spread[:, row, :]
            contrib = contrib + jnp.stack([kreal * picked[0] - kimag * picked[1], kreal * picked[1] + kimag * picked[0], kweight * picked[2]])
        start = (target * ZD).astype(jnp.int32)
        zero = jnp.zeros((), jnp.int32)
        old = lax.dynamic_slice(volume, (zero, start, zero, zero), (3, ZE, NY, NX))
        return lax.dynamic_update_slice(volume, old + contrib, (zero, start, zero, zero))
    volume = jnp.zeros((3, NZ + 2 * MZ, NY, NX), jnp.float32)
    volume = lax.fori_loop(0, NSL, insert, volume)
    half = rounded(volume[:, MZ:MZ + NZ])
    mirror = half[:, ::-1, ::-1, ::-1]
    signs = jnp.array([1.0, -1.0, 1.0], jnp.float32)[:, None, None, None]
    return half + signs * mirror
```

```python
import functools
import math

import jax
import jax.numpy as jnp
from jax import lax
from jax.experimental import pallas as pl
from jax.experimental.pallas import tpu as pltpu
from jax.sharding import PartitionSpec as P

ZD = 4
MZ = 4
ZE = 12
CAP = 4
SLABS = 16
SLOTS = SLABS * CAP
SLICE = 512
GRID = 1024
STRIP = 32
LINES = 64
HALF = 16
KC = SLOTS * HALF
MAIN = ZE * 32
MROWS = MAIN + 32

kernel_beta = 7.4
kernel_reach = 2.0
twist_step = 0.37

MESH = pl.DeviceIdType.MESH


def series(quarter):
    total = jnp.full_like(quarter, 1.0 / math.factorial(25) ** 2)
    for order in range(24, 0, -1):
        total = total * quarter + 1.0 / math.factorial(order) ** 2
    return total * quarter


SCALE = sum((kernel_beta * kernel_beta / 4) ** m / math.factorial(m) ** 2 for m in range(1, 26))


def kaiser(distance):
    inside = jnp.maximum(1.0 - distance * distance * 0.25, 0.0)
    return series(inside * (kernel_beta * kernel_beta * 0.25)) * (1.0 / SCALE)


def insert_kernel(w_ref, g_ref, cs_ref, pay_ref, mid_ref, up_ref, dn_ref, halo_ref, bc, bw, ac, aw):
    row_index = lax.axis_index("ky")

    @pl.loop(0, SLOTS)
    def _(n):
        wa, wb, wc, wd = w_ref[n, 0], w_ref[n, 1], w_ref[n, 2], w_ref[n, 3]
        for c in range(3):
            d = pay_ref[n, c].astype(jnp.float32)
            before = pltpu.roll(d, 1, 1)
            after = pltpu.roll(d, SLICE - 1, 1)
            even = (wa * d + wb * before).astype(jnp.bfloat16)
            odd = (wc * d + wd * after).astype(jnp.bfloat16)
            for q in range(2):
                if c < 2:
                    rows = pl.ds(pl.multiple_of(c * KC + n * HALF, HALF), HALF)
                    target = bc
                else:
                    rows = pl.ds(pl.multiple_of(n * HALF, HALF), HALF)
                    target = bw
                target[q, rows, 0:SLICE] = even[q * HALF : (q + 1) * HALF]
                target[q, rows, SLICE:GRID] = odd[q * HALF : (q + 1) * HALF]

    plane, live, tilt, shift = g_ref[0:1], g_ref[2:3], g_ref[3:4], g_ref[4:5]
    local = lax.broadcasted_iota(jnp.int32, (1, KC), 1) % HALF
    level = (lax.broadcasted_iota(jnp.int32, (16, 1), 0) - MZ).astype(jnp.float32)
    line = lax.broadcasted_iota(jnp.int32, (32, 1), 0)
    main_y = kaiser((line - 2 * local).astype(jnp.float32) - shift)
    low_y = kaiser((-1 - 2 * local).astype(jnp.float32) - shift)
    high_y = kaiser((32 - 2 * local).astype(jnp.float32) - shift)
    for q in range(2):
        row = row_index * STRIP + q * HALF + local - SLICE // 2
        centre = plane + tilt * row.astype(jnp.float32) / (SLICE // 2)
        along = kaiser(level - centre) * live
        real, imag = along * cs_ref[0:16], along * cs_ref[16:32]
        for part, value_y in ((0, low_y), (16, high_y)):
            rows = slice(MAIN + part, MAIN + part + 16)
            again = slice(MROWS + MAIN + part, MROWS + MAIN + part + 16)
            kr = (real * value_y).astype(jnp.bfloat16)
            ki = imag * value_y
            ac[q, rows, 0:KC] = kr
            ac[q, rows, KC : 2 * KC] = (-ki).astype(jnp.bfloat16)
            ac[q, again, 0:KC] = ki.astype(jnp.bfloat16)
            ac[q, again, KC : 2 * KC] = kr
            aw[q, rows, :] = (along * value_y).astype(jnp.bfloat16)
        for z in range(ZE):
            rows = slice(z * 32, z * 32 + 32)
            again = slice(MROWS + z * 32, MROWS + z * 32 + 32)
            kr = (real[z : z + 1] * main_y).astype(jnp.bfloat16)
            ki = imag[z : z + 1] * main_y
            ac[q, rows, 0:KC] = kr
            ac[q, rows, KC : 2 * KC] = (-ki).astype(jnp.bfloat16)
            ac[q, again, 0:KC] = ki.astype(jnp.bfloat16)
            ac[q, again, KC : 2 * KC] = kr
            aw[q, rows, :] = (along[z : z + 1] * main_y).astype(jnp.bfloat16)

    lines = lax.broadcasted_iota(jnp.int32, (1, 32, 1), 1)

    @pl.loop(0, GRID // 256)
    def _(tile):
        cols = pl.ds(pl.multiple_of(tile * 256, 256), 256)
        for c in range(3):
            if c < 2:
                parts = [
                    jnp.dot(
                        ac[q, c * MROWS : (c + 1) * MROWS, :],
                        bc[q, :, cols],
                        preferred_element_type=jnp.float32,
                    )
                    for q in range(2)
                ]
            else:
                parts = [
                    jnp.dot(aw[q], bw[q, :, cols], preferred_element_type=jnp.float32)
                    for q in range(2)
                ]
            low = [part[MAIN : MAIN + ZE] for part in parts]
            high = [part[MAIN + 16 : MAIN + 16 + ZE] for part in parts]
            main = [part[:MAIN].reshape(ZE, 32, 256) for part in parts]
            main[0] = main[0] + jnp.where(lines == 31, low[1][:, None, :], 0.0)
            main[1] = main[1] + jnp.where(lines == 0, high[0][:, None, :], 0.0)
            for q in range(2):
                span = slice(q * 32, q * 32 + 32)
                dn_ref[c, :, span, cols] = main[q][0:MZ].astype(jnp.bfloat16)
                mid_ref[c, :, span, cols] = main[q][MZ : MZ + ZD]
                up_ref[c, :, span, cols] = main[q][MZ + ZD :].astype(jnp.bfloat16)
            for j in range(3):
                halo_ref[j, c * ZD : (c + 1) * ZD, cols] = low[0][j * 4 : j * 4 + 4]
                halo_ref[3 + j, c * ZD : (c + 1) * ZD, cols] = high[1][j * 4 : j * 4 + 4]


def insert(weights, geometry, phases, payload):
    vmem = pl.BlockSpec(memory_space=pltpu.VMEM)
    return pl.pallas_call(
        insert_kernel,
        out_shape=(
            jax.ShapeDtypeStruct((3, ZD, LINES, GRID), jnp.float32),
            jax.ShapeDtypeStruct((3, ZD, LINES, GRID), jnp.bfloat16),
            jax.ShapeDtypeStruct((3, ZD, LINES, GRID), jnp.bfloat16),
            jax.ShapeDtypeStruct((6, 16, GRID), jnp.float32),
        ),
        in_specs=[pl.BlockSpec(memory_space=pltpu.SMEM), vmem, vmem, vmem],
        out_specs=(vmem, vmem, vmem, vmem),
        scratch_shapes=[
            pltpu.VMEM((2, 2 * KC, GRID), jnp.bfloat16),
            pltpu.VMEM((2, KC, GRID), jnp.bfloat16),
            pltpu.VMEM((2, 2 * MROWS, 2 * KC), jnp.bfloat16),
            pltpu.VMEM((2, MROWS, KC), jnp.bfloat16),
        ],
        compiler_params=pltpu.CompilerParams(vmem_limit_bytes=60 << 20),
        name="insert",
    )(weights, geometry, phases, payload)


def exchange_kernel(
    mid_ref, up_ref, dn_ref, halo_ref, out_ref,
    from_low, from_high, halos, half, mirror, perm, back, send, recv,
):
    kz, ky = lax.axis_index("kz"), lax.axis_index("ky")
    above, below = lax.rem(kz + 1, 16), lax.rem(kz + 15, 16)
    after, before = lax.rem(ky + 1, 16), lax.rem(ky + 15, 16)
    partner = {"kz": 15 - kz, "ky": 15 - ky}
    slabs = (below, kz, above)
    peers = [{"kz": above, "ky": ky}, {"kz": below, "ky": ky}]
    peers += [{"kz": s, "ky": r} for s in slabs for r in (before, after)]
    peers += [partner]
    barrier = pltpu.get_barrier_semaphore()
    for peer in peers:
        pl.semaphore_signal(barrier, inc=1, device_id=peer, device_id_type=MESH)
    pl.semaphore_wait(barrier, len(peers))

    def copy(source, target, number, peer):
        return pltpu.make_async_remote_copy(
            src_ref=source, dst_ref=target, send_sem=send.at[number], recv_sem=recv.at[number],
            device_id=peer, device_id_type=MESH,
        )

    first = [copy(up_ref, from_low, 0, peers[0]), copy(dn_ref, from_high, 1, peers[1])]
    for j in range(3):
        for side, target in ((0, before), (1, after)):
            number = side * 3 + j
            first.append(
                copy(
                    halo_ref.at[number], halos.at[number], 2 + number,
                    {"kz": slabs[j], "ky": target},
                )
            )
    for item in first:
        item.start()

    @pl.loop(0, GRID // 128)
    def _(tile):
        rows = pl.multiple_of(tile * 128, 128)
        k = lax.broadcasted_iota(jnp.int32, (128, GRID), 0) + rows
        x = lax.broadcasted_iota(jnp.int32, (128, GRID), 1)
        wanted = jnp.where(k < SLICE, 2 * k, 2 * (k - SLICE) + 1)
        perm[pl.ds(rows, 128), :] = (x == wanted).astype(jnp.float32).astype(jnp.bfloat16)
        back[pl.ds(rows, 128), :] = (GRID - 1 - x == wanted).astype(jnp.float32).astype(jnp.bfloat16)

    for item in first:
        item.wait()

    lower = jnp.where(kz > 0, 1.0, 0.0)
    upper = jnp.where(kz < 15, 1.0, 0.0)
    lines = lax.broadcasted_iota(jnp.int32, (LINES, 1), 0)
    copies = []
    for c in range(3):

        @pl.loop(0, ZD)
        def _(p):
            row = pl.ds(c * ZD + p, 1)
            total = mid_ref[c, p] + lower * from_low[c, p].astype(jnp.float32)
            total = total + upper * from_high[c, p].astype(jnp.float32)
            last = upper * halos[0, row, :] + halos[1, row, :] + lower * halos[2, row, :]
            start = upper * halos[3, row, :] + halos[4, row, :] + lower * halos[5, row, :]
            total = total + jnp.where(lines == LINES - 1, last, 0.0)
            total = total + jnp.where(lines == 0, start, 0.0)
            half[c, pl.ds(pl.multiple_of(p * LINES, LINES), LINES), :] = total.astype(jnp.bfloat16)

        item = copy(half.at[c], mirror.at[c], 8 + c, partner)
        item.start()
        copies.append(item)

    for c in range(3):

        @pl.loop(0, GRID // 256)
        def _(tile):
            cols = pl.ds(pl.multiple_of(tile * 256, 256), 256)
            out_ref[c, :, cols] = jnp.dot(
                half[c], perm[:, cols], preferred_element_type=jnp.float32
            )

    i = lax.broadcasted_iota(jnp.int32, (256, 256), 0)
    j = lax.broadcasted_iota(jnp.int32, (256, 256), 1)
    flip = (i + j == 255).astype(jnp.float32).astype(jnp.bfloat16)
    for c, sign in ((0, 1.0), (1, -1.0), (2, 1.0)):
        copies[c].wait()
        turned = jnp.dot(flip, mirror[c], preferred_element_type=jnp.float32)
        mirror[c] = turned.astype(jnp.bfloat16)

        @pl.loop(0, GRID // 256)
        def _(tile):
            cols = pl.ds(pl.multiple_of(tile * 256, 256), 256)
            out_ref[c, :, cols] += sign * jnp.dot(
                mirror[c], back[:, cols], preferred_element_type=jnp.float32
            )


def exchange(mid, up, dn, halo):
    vmem = pl.BlockSpec(memory_space=pltpu.VMEM)
    return pl.pallas_call(
        exchange_kernel,
        out_shape=jax.ShapeDtypeStruct((3, ZD * LINES, GRID), jnp.float32),
        in_specs=[vmem] * 4,
        out_specs=vmem,
        scratch_shapes=[
            pltpu.VMEM((3, ZD, LINES, GRID), jnp.bfloat16),
            pltpu.VMEM((3, ZD, LINES, GRID), jnp.bfloat16),
            pltpu.VMEM((6, 16, GRID), jnp.float32),
            pltpu.VMEM((3, ZD * LINES, GRID), jnp.bfloat16),
            pltpu.VMEM((3, ZD * LINES, GRID), jnp.bfloat16),
            pltpu.VMEM((GRID, GRID), jnp.bfloat16),
            pltpu.VMEM((GRID, GRID), jnp.bfloat16),
            pltpu.SemaphoreType.DMA((11,)),
            pltpu.SemaphoreType.DMA((11,)),
        ],
        compiler_params=pltpu.CompilerParams(
            collective_id=1, has_side_effects=True, vmem_limit_bytes=60 << 20
        ),
        name="exchange",
    )(mid, up, dn, halo)


def per_device(
    slice_re, slice_im, slice_ctf, slice_dest, slice_plane, helix_index, slice_tilt, slice_shift
):
    slab_index = lax.axis_index("kz")
    held_count = slice_re.shape[0]
    ctf = slice_ctf.astype(jnp.float32)
    data = jnp.stack(
        [ctf * slice_re.astype(jnp.float32), ctf * slice_im.astype(jnp.float32), ctf * ctf], axis=1
    ).astype(jnp.bfloat16)
    ones = jnp.ones((held_count,), jnp.float32)
    zeros = jnp.zeros((held_count,), jnp.float32)
    geometry = jnp.stack(
        [
            slice_plane.astype(jnp.float32),
            helix_index.astype(jnp.float32),
            ones,
            slice_tilt.astype(jnp.float32),
            slice_shift[0].astype(jnp.float32),
            slice_shift[1].astype(jnp.float32),
            zeros,
            zeros,
        ],
        axis=1,
    ).astype(jnp.bfloat16)
    target = slice_dest[:, 0]
    onehot = (target[:, None] == jnp.arange(SLABS)[None, :]).astype(jnp.int32)
    ranking = jnp.sum((jnp.cumsum(onehot, axis=0) - 1) * onehot, axis=1)
    position = target * CAP + ranking
    matches = (jnp.arange(SLOTS)[:, None] == position[None, :]).astype(jnp.int32)
    occupied = jnp.sum(matches, axis=1) > 0
    source_row = jnp.sum(matches * jnp.arange(held_count)[None, :], axis=1)
    payload = lax.all_to_all(
        jnp.take(data, source_row, axis=0), "kz", split_axis=0, concat_axis=0, tiled=True
    )
    slots = jnp.where(occupied[:, None], jnp.take(geometry, source_row, axis=0), 0)
    arrived = lax.all_to_all(slots, "kz", split_axis=0, concat_axis=0, tiled=True)
    arrived = arrived.astype(jnp.float32)
    offset = arrived[:, 5:6]
    weights = kaiser(jnp.array([[0.0, 2.0, 1.0, -1.0]]) - offset)
    weights = weights.astype(jnp.bfloat16).astype(jnp.float32)
    band = slab_index * ZD + jnp.arange(16) - MZ
    angle = twist_step * (arrived[:, 1].astype(jnp.int32)[None, :] * band[:, None]).astype(
        jnp.float32
    )
    phases = jnp.repeat(jnp.concatenate([jnp.cos(angle), jnp.sin(angle)], axis=0), HALF, axis=1)
    spread = jnp.repeat(arrived.T, HALF, axis=1)
    mid, up, dn, halo = insert(weights, spread, phases, payload)
    out = exchange(mid, up, dn, halo)
    return out.reshape(3, ZD, LINES, GRID)


def solution(mesh):
    placed = (
        P("kz", "ky", None),
        P("kz", "ky", None),
        P("kz", "ky", None),
        P("kz", None),
        P("kz"),
        P("kz"),
        P("kz"),
        P(None, "kz"),
    )
    return jax.shard_map(
        per_device, mesh=mesh, in_specs=placed, out_specs=P(None, "kz", "ky", None), check_vma=False
    )
```

```python
import functools
import math

import jax
import jax.numpy as jnp
from jax import lax
from jax.experimental import pallas as pl
from jax.experimental.pallas import tpu as pltpu
from jax.sharding import PartitionSpec as P

ZD = 4
MZ = 4
ZE = 12
CAP = 4
SLABS = 16
SLOTS = SLABS * CAP
SLICE = 512
GRID = 1024
SPARE = 4
ALL = SLABS * (1 + SPARE)
KA = ALL * 16
STRIP = 32
LINES = 64
HALF = 16
KC = SLOTS * HALF
MAIN = ZE * 32
MROWS = MAIN + 32

kernel_beta = 7.4
kernel_reach = 2.0
twist_step = 0.37

MESH = pl.DeviceIdType.MESH


def series(quarter):
    total = jnp.full_like(quarter, 1.0 / math.factorial(25) ** 2)
    for order in range(24, 0, -1):
        total = total * quarter + 1.0 / math.factorial(order) ** 2
    return total * quarter


SCALE = sum((kernel_beta * kernel_beta / 4) ** m / math.factorial(m) ** 2 for m in range(1, 26))


def kaiser(distance):
    inside = jnp.maximum(1.0 - distance * distance * 0.25, 0.0)
    return series(inside * (kernel_beta * kernel_beta * 0.25)) * (1.0 / SCALE)


def insert_kernel(count, w_ref, g_ref, cs_ref, pay_ref, mid_ref, up_ref, dn_ref, halo_ref, b, a):
    row_index = lax.axis_index("ky")

    @pl.loop(0, SLOTS)
    def _(n):
        wa, wb, wc, wd = w_ref[n, 0], w_ref[n, 1], w_ref[n, 2], w_ref[n, 3]
        for c in range(count):
            d = pay_ref[n, c].astype(jnp.float32)
            before = pltpu.roll(d, 1, 1)
            after = pltpu.roll(d, SLICE - 1, 1)
            even = (wa * d + wb * before).astype(jnp.bfloat16)
            odd = (wc * d + wd * after).astype(jnp.bfloat16)
            rows = pl.ds(pl.multiple_of(c * KC + n * HALF, HALF), HALF)
            for q in range(2):
                b[q, rows, 0:SLICE] = even[q * HALF : (q + 1) * HALF]
                b[q, rows, SLICE:GRID] = odd[q * HALF : (q + 1) * HALF]

    plane, live, tilt, shift = g_ref[0:1], g_ref[2:3], g_ref[3:4], g_ref[4:5]
    local = lax.broadcasted_iota(jnp.int32, (1, KC), 1) % HALF
    level = (lax.broadcasted_iota(jnp.int32, (16, 1), 0) - MZ).astype(jnp.float32)
    line = lax.broadcasted_iota(jnp.int32, (32, 1), 0)
    main_y = kaiser((line - 2 * local).astype(jnp.float32) - shift)
    low_y = kaiser((-1 - 2 * local).astype(jnp.float32) - shift)
    high_y = kaiser((32 - 2 * local).astype(jnp.float32) - shift)
    for q in range(2):
        row = row_index * STRIP + q * HALF + local - SLICE // 2
        centre = plane + tilt * row.astype(jnp.float32) / (SLICE // 2)
        along = kaiser(level - centre) * live
        parts = [(MAIN, slice(0, 16), low_y), (MAIN + 16, slice(0, 16), high_y)]
        parts += [(z * 32, slice(z, z + 1), main_y) for z in range(ZE)]
        if count == 2:
            real, imag = along * cs_ref[0:16], along * cs_ref[16:32]
        for first, levels, value_y in parts:
            size = 16 if first >= MAIN else 32
            rows = slice(first, first + size)
            again = slice(MROWS + first, MROWS + first + size)
            if count == 2:
                kr = (real[levels] * value_y).astype(jnp.bfloat16)
                ki = imag[levels] * value_y
                a[q, rows, 0:KC] = kr
                a[q, rows, KC : 2 * KC] = (-ki).astype(jnp.bfloat16)
                a[q, again, 0:KC] = ki.astype(jnp.bfloat16)
                a[q, again, KC : 2 * KC] = kr
            else:
                a[q, rows, :] = (along[levels] * value_y).astype(jnp.bfloat16)

    lines = lax.broadcasted_iota(jnp.int32, (1, 32, 1), 1)

    @pl.loop(0, GRID // 256)
    def _(tile):
        cols = pl.ds(pl.multiple_of(tile * 256, 256), 256)
        for c in range(count):
            parts = [
                jnp.dot(
                    a[q, c * MROWS : (c + 1) * MROWS, :],
                    b[q, :, cols],
                    preferred_element_type=jnp.float32,
                )
                for q in range(2)
            ]
            low = [part[MAIN : MAIN + ZE] for part in parts]
            high = [part[MAIN + 16 : MAIN + 16 + ZE] for part in parts]
            main = [part[:MAIN].reshape(ZE, 32, 256) for part in parts]
            main[0] = main[0] + jnp.where(lines == 31, low[1][:, None, :], 0.0)
            main[1] = main[1] + jnp.where(lines == 0, high[0][:, None, :], 0.0)
            for q in range(2):
                span = slice(q * 32, q * 32 + 32)
                dn_ref[c, :, span, cols] = main[q][0:MZ].astype(jnp.bfloat16)
                mid_ref[c, :, span, cols] = main[q][MZ : MZ + ZD]
                up_ref[c, :, span, cols] = main[q][MZ + ZD :].astype(jnp.bfloat16)
            for j in range(3):
                halo_ref[j, c * ZD : (c + 1) * ZD, cols] = low[0][j * 4 : j * 4 + 4]
                halo_ref[3 + j, c * ZD : (c + 1) * ZD, cols] = high[1][j * 4 : j * 4 + 4]


def insert(count, weights, geometry, phases, payload):
    vmem = pl.BlockSpec(memory_space=pltpu.VMEM)
    return pl.pallas_call(
        functools.partial(insert_kernel, count),
        out_shape=(
            jax.ShapeDtypeStruct((count, ZD, LINES, GRID), jnp.float32),
            jax.ShapeDtypeStruct((count, ZD, LINES, GRID), jnp.bfloat16),
            jax.ShapeDtypeStruct((count, ZD, LINES, GRID), jnp.bfloat16),
            jax.ShapeDtypeStruct((6, 8, GRID), jnp.float32),
        ),
        in_specs=[pl.BlockSpec(memory_space=pltpu.SMEM), vmem, vmem, vmem],
        out_specs=(vmem, vmem, vmem, vmem),
        scratch_shapes=[
            pltpu.VMEM((2, count * KC, GRID), jnp.bfloat16),
            pltpu.VMEM((2, count * MROWS, count * KC), jnp.bfloat16),
        ],
        compiler_params=pltpu.CompilerParams(vmem_limit_bytes=60 << 20),
        cost_estimate=pl.CostEstimate(
            flops=count * count * 4 * MROWS * KC * GRID, bytes_accessed=count * 5 << 20,
            transcendentals=0,
        ),
        name=f"insert{count}",
    )(weights, geometry, phases, payload)


def exchange_kernel(
    signs, mid_ref, up_ref, dn_ref, halo_ref, out_ref,
    from_low, from_high, halos, half, mirror, perm, back, send, recv,
):
    count = len(signs)
    kz, ky = lax.axis_index("kz"), lax.axis_index("ky")
    above, below = lax.rem(kz + 1, 16), lax.rem(kz + 15, 16)
    after, before = lax.rem(ky + 1, 16), lax.rem(ky + 15, 16)
    partner = {"kz": 15 - kz, "ky": 15 - ky}
    slabs = (below, kz, above)
    peers = [{"kz": above, "ky": ky}, {"kz": below, "ky": ky}]
    peers += [{"kz": s, "ky": r} for s in slabs for r in (before, after)]
    peers += [partner]
    barrier = pltpu.get_barrier_semaphore()
    for peer in peers:
        pl.semaphore_signal(barrier, inc=1, device_id=peer, device_id_type=MESH)
    pl.semaphore_wait(barrier, len(peers))

    def copy(source, target, number, peer):
        return pltpu.make_async_remote_copy(
            src_ref=source, dst_ref=target, send_sem=send.at[number], recv_sem=recv.at[number],
            device_id=peer, device_id_type=MESH,
        )

    edges = []
    for j in range(3):
        for side, target in ((0, before), (1, after)):
            number = side * 3 + j
            edges.append(
                copy(
                    halo_ref.at[number], halos.at[number], number,
                    {"kz": slabs[j], "ky": target},
                )
            )
    margins = [
        (
            copy(up_ref.at[c], from_low.at[c], 6 + 2 * c, peers[0]),
            copy(dn_ref.at[c], from_high.at[c], 7 + 2 * c, peers[1]),
        )
        for c in range(count)
    ]
    for item in edges + [item for pair in margins for item in pair]:
        item.start()

    @pl.loop(0, GRID // 128)
    def _(tile):
        rows = pl.multiple_of(tile * 128, 128)
        k = lax.broadcasted_iota(jnp.int32, (128, GRID), 0) + rows
        x = lax.broadcasted_iota(jnp.int32, (128, GRID), 1)
        wanted = jnp.where(k < SLICE, 2 * k, 2 * (k - SLICE) + 1)
        perm[pl.ds(rows, 128), :] = (x == wanted).astype(jnp.float32).astype(jnp.bfloat16)
        back[pl.ds(rows, 128), :] = (GRID - 1 - x == wanted).astype(jnp.float32).astype(jnp.bfloat16)

    for item in edges:
        item.wait()

    lower = jnp.where(kz > 0, 1.0, 0.0)
    upper = jnp.where(kz < 15, 1.0, 0.0)
    lines = lax.broadcasted_iota(jnp.int32, (LINES, 1), 0)
    copies = []
    for c in range(count):
        for item in margins[c]:
            item.wait()

        @pl.loop(0, ZD)
        def _(p):
            row = pl.ds(c * ZD + p, 1)
            total = mid_ref[c, p] + lower * from_low[c, p].astype(jnp.float32)
            total = total + upper * from_high[c, p].astype(jnp.float32)
            last = upper * halos[0, row, :] + halos[1, row, :] + lower * halos[2, row, :]
            start = upper * halos[3, row, :] + halos[4, row, :] + lower * halos[5, row, :]
            total = total + jnp.where(lines == LINES - 1, last, 0.0)
            total = total + jnp.where(lines == 0, start, 0.0)
            half[c, pl.ds(pl.multiple_of(p * LINES, LINES), LINES), :] = total.astype(jnp.bfloat16)

        item = copy(half.at[c], mirror.at[c], 6 + 2 * count + c, partner)
        item.start()
        copies.append(item)

    for c in range(count):

        @pl.loop(0, GRID // 256)
        def _(tile):
            cols = pl.ds(pl.multiple_of(tile * 256, 256), 256)
            out_ref[c, :, cols] = jnp.dot(
                half[c], perm[:, cols], preferred_element_type=jnp.float32
            )

    i = lax.broadcasted_iota(jnp.int32, (256, 256), 0)
    j = lax.broadcasted_iota(jnp.int32, (256, 256), 1)
    flip = (i + j == 255).astype(jnp.float32).astype(jnp.bfloat16)
    for c, sign in enumerate(signs):
        copies[c].wait()
        turned = jnp.dot(flip, mirror[c], preferred_element_type=jnp.float32)
        mirror[c] = turned.astype(jnp.bfloat16)

        @pl.loop(0, GRID // 256)
        def _(tile):
            cols = pl.ds(pl.multiple_of(tile * 256, 256), 256)
            out_ref[c, :, cols] += sign * jnp.dot(
                mirror[c], back[:, cols], preferred_element_type=jnp.float32
            )


def exchange(signs, mid, up, dn, halo):
    count = len(signs)
    vmem = pl.BlockSpec(memory_space=pltpu.VMEM)
    return pl.pallas_call(
        functools.partial(exchange_kernel, signs),
        out_shape=jax.ShapeDtypeStruct((count, ZD * LINES, GRID), jnp.float32),
        in_specs=[vmem] * 4,
        out_specs=vmem,
        scratch_shapes=[
            pltpu.VMEM((count, ZD, LINES, GRID), jnp.bfloat16),
            pltpu.VMEM((count, ZD, LINES, GRID), jnp.bfloat16),
            pltpu.VMEM((6, 8, GRID), jnp.float32),
            pltpu.VMEM((count, ZD * LINES, GRID), jnp.bfloat16),
            pltpu.VMEM((count, ZD * LINES, GRID), jnp.bfloat16),
            pltpu.VMEM((GRID, GRID), jnp.bfloat16),
            pltpu.VMEM((GRID, GRID), jnp.bfloat16),
            pltpu.SemaphoreType.DMA((6 + 3 * count,)),
            pltpu.SemaphoreType.DMA((6 + 3 * count,)),
        ],
        compiler_params=pltpu.CompilerParams(
            collective_id=count, has_side_effects=True, vmem_limit_bytes=60 << 20
        ),
        cost_estimate=pl.CostEstimate(
            flops=count * 4 * 256 * GRID * GRID, bytes_accessed=count * 20 << 20, transcendentals=0
        ),
        name=f"exchange{count}",
    )(mid, up, dn, halo)


def padded(
    slice_re, slice_im, slice_ctf, slice_dest, slice_plane, helix_index, slice_tilt, slice_shift
):
    slab_index = lax.axis_index("kz")
    held_count = slice_re.shape[0]
    ctf = slice_ctf.astype(jnp.float32)
    square = (ctf * ctf).astype(jnp.bfloat16)[:, None]
    pair = jnp.stack(
        [ctf * slice_re.astype(jnp.float32), ctf * slice_im.astype(jnp.float32)], axis=1
    ).astype(jnp.bfloat16)
    ones = jnp.ones((held_count,), jnp.float32)
    zeros = jnp.zeros((held_count,), jnp.float32)
    geometry = jnp.stack(
        [
            slice_plane.astype(jnp.float32),
            helix_index.astype(jnp.float32),
            ones,
            slice_tilt.astype(jnp.float32),
            slice_shift[0].astype(jnp.float32),
            slice_shift[1].astype(jnp.float32),
            zeros,
            zeros,
        ],
        axis=1,
    ).astype(jnp.bfloat16)
    target = slice_dest[:, 0]
    onehot = (target[:, None] == jnp.arange(SLABS)[None, :]).astype(jnp.int32)
    ranking = jnp.sum((jnp.cumsum(onehot, axis=0) - 1) * onehot, axis=1)
    position = target * CAP + ranking
    matches = (jnp.arange(SLOTS)[:, None] == position[None, :]).astype(jnp.int32)
    occupied = jnp.sum(matches, axis=1) > 0
    source_row = jnp.sum(matches * jnp.arange(held_count)[None, :], axis=1)

    def dispatch(values):
        picked = jnp.take(values, source_row, axis=0, mode="clip")
        return lax.all_to_all(picked, "kz", split_axis=0, concat_axis=0, tiled=True)

    slots = jnp.where(occupied[:, None], jnp.take(geometry, source_row, axis=0, mode="clip"), 0)
    arrived = lax.all_to_all(slots, "kz", split_axis=0, concat_axis=0, tiled=True)
    square = dispatch(square)
    pair = dispatch(pair)
    arrived = arrived.astype(jnp.float32)
    offset = arrived[:, 5:6]
    weights = kaiser(jnp.array([[0.0, 2.0, 1.0, -1.0]]) - offset)
    weights = weights.astype(jnp.bfloat16).astype(jnp.float32)
    band = slab_index * ZD + jnp.arange(16) - MZ
    angle = twist_step * (arrived[:, 1].astype(jnp.int32)[None, :] * band[:, None]).astype(
        jnp.float32
    )
    phases = jnp.repeat(jnp.concatenate([jnp.cos(angle), jnp.sin(angle)], axis=0), HALF, axis=1)
    spread = jnp.repeat(arrived.T, HALF, axis=1)
    weight = exchange((1.0,), *insert(1, weights, spread, phases, square))
    signal = exchange((1.0, -1.0), *insert(2, weights, spread, phases, pair))
    return jnp.concatenate([signal, weight], axis=0)


PLANE, HELIX, VALID, TILT, SHIFT_Y, SHIFT_X, DEST, TAPS, EXTRA = 0, 1, 2, 3, 4, 5, 6, 8, 12


def plan_kernel(dest, plane, helix, tilt, shift, table, rows, seen):
    lane = lax.broadcasted_iota(jnp.int32, (1, 128), 1)
    table[...] = jnp.zeros_like(table)
    for d in range(SLABS):
        seen[d] = 0
        rows[d] = 0
        rows[SLABS + d] = 0
    extra = jnp.int32(0)
    for i in range(SLABS):
        d = dest[i, 0]
        fields = (
            (PLANE, plane[i].astype(jnp.float32)), (HELIX, helix[i].astype(jnp.float32)),
            (VALID, 1.0), (TILT, tilt[i]), (SHIFT_Y, shift[0, i]), (SHIFT_X, shift[1, i]),
            (DEST, d.astype(jnp.float32)),
        )
        row = jnp.zeros((1, 128), jnp.float32)
        for index, value in fields:
            row = jnp.where(lane == index, value, row)
        before = seen[d]

        @pl.when(before == 0)
        def _():
            table[d, 0:1, :] = row
            rows[d] = i

        @pl.when((before > 0) & (extra < SPARE))
        def _():
            rows[SLABS + extra] = i
            for other in range(SLABS):
                table[other, pl.ds(1 + extra, 1), :] = row

        seen[d] = before + 1
        extra = extra + jnp.where(before > 0, 1, 0)
    lags = jnp.where(lane == TAPS + 1, 2.0, jnp.where(lane == TAPS + 2, 1.0, 0.0))
    lags = jnp.where(lane == TAPS + 3, -1.0, lags)
    for d in range(SLABS):
        block = table[d]
        taps = kaiser(lags - block[:, SHIFT_X : SHIFT_X + 1])
        taps = taps.astype(jnp.bfloat16).astype(jnp.float32)
        block = jnp.where((lane >= TAPS) & (lane < TAPS + 4), taps, block)
        table[d] = jnp.where(lane == EXTRA, extra.astype(jnp.float32), block)


def plan(dest, plane, helix, tilt, shift):
    smem = pl.BlockSpec(memory_space=pltpu.SMEM)
    return pl.pallas_call(
        plan_kernel,
        out_shape=(
            jax.ShapeDtypeStruct((SLABS, 8, 128), jnp.float32),
            jax.ShapeDtypeStruct((2 * SLABS,), jnp.int32),
        ),
        in_specs=[smem] * 5,
        out_specs=(pl.BlockSpec(memory_space=pltpu.VMEM), smem),
        scratch_shapes=[pltpu.SMEM((SLABS,), jnp.int32)],
        name="plan",
    )(dest, plane, helix, tilt.astype(jnp.float32), shift.astype(jnp.float32))


def dispatch_kernel(
    rows, table, re_ref, im_ref, ctf_ref, cap, spare, tables, outbox,
    send, recv, cap_send, cap_recv, tab_send, tab_recv,
):
    me = lax.axis_index("kz")
    side, core = me // 8, lax.rem(me, 2)
    column = lax.rem(me, 8) // 2

    def at(other_side, x, c):
        return other_side * 8 + lax.rem(x + 4, 4) * 2 + c

    across, twin = at(1 - side, column, core), at(side, column, 1 - core)
    right, left = at(side, column + 1, core), at(side, column - 1, core)
    far = at(side, column + 2, core)
    right_across, left_across = at(1 - side, column + 1, core), at(1 - side, column - 1, core)
    far_across = at(1 - side, column + 2, core)
    barrier = pltpu.get_barrier_semaphore()
    for r in range(1, SLABS):
        pl.semaphore_signal(
            barrier, inc=1, device_id={"kz": lax.rem(me + r, SLABS)}, device_id_type=MESH
        )

    def pack(row, target, place):
        ctf = ctf_ref[row].astype(jnp.float32)
        target[place, 0] = (ctf * re_ref[row].astype(jnp.float32)).astype(jnp.bfloat16)
        target[place, 1] = (ctf * im_ref[row].astype(jnp.float32)).astype(jnp.bfloat16)
        target[place, 2] = (ctf * ctf).astype(jnp.bfloat16)

    for j in range(SPARE):
        pack(rows[SLABS + j], spare, me * SPARE + j)
    pl.semaphore_wait(barrier, SLABS - 1)

    def pass_on(number, origin, target, part=(0, SPARE)):
        block = spare.at[pl.ds(origin * SPARE + part[0], part[1] - part[0])]
        item = pltpu.make_async_remote_copy(
            src_ref=block, dst_ref=block, send_sem=send.at[number], recv_sem=recv.at[number],
            device_id={"kz": target}, device_id_type=MESH,
        )
        item.start()
        return item

    lower, upper = (0, SPARE // 2), (SPARE // 2, SPARE)
    sent = {}
    sent[0] = pass_on(0, me, across)
    sent[1] = pass_on(1, me, right)
    sent[2] = pass_on(2, me, left)
    sent[3] = pass_on(3, me, twin)
    copies = []
    for r in range(1, SLABS):
        d = lax.rem(me + r, SLABS)
        item = pltpu.make_async_remote_copy(
            src_ref=table.at[d], dst_ref=tables.at[me], send_sem=tab_send.at[r],
            recv_sem=tab_recv.at[r], device_id={"kz": d}, device_id_type=MESH,
        )
        item.start()
        copies.append(item)
        pack(rows[d], outbox, d)
        item = pltpu.make_async_remote_copy(
            src_ref=outbox.at[d], dst_ref=cap.at[me], send_sem=cap_send.at[r],
            recv_sem=cap_recv.at[r], device_id={"kz": d}, device_id_type=MESH,
        )
        item.start()
        copies.append(item)
    pack(rows[me], cap, me)
    tables[me] = table[me]

    sent[0].wait_recv()
    sent[4] = pass_on(4, across, right)
    sent[5] = pass_on(5, across, left)
    sent[6] = pass_on(6, across, twin)
    sent[1].wait_recv()
    sent[7] = pass_on(7, left, right, lower)
    sent[8] = pass_on(8, left, twin)
    sent[2].wait_recv()
    sent[9] = pass_on(9, right, left, upper)
    sent[10] = pass_on(10, right, twin)
    sent[4].wait_recv()
    sent[11] = pass_on(11, left_across, right, lower)
    sent[12] = pass_on(12, left_across, twin)
    sent[5].wait_recv()
    sent[13] = pass_on(13, right_across, left, upper)
    sent[14] = pass_on(14, right_across, twin)
    sent[7].wait_recv()
    sent[15] = pass_on(15, far, twin, lower)
    sent[9].wait_recv()
    sent[16] = pass_on(16, far, twin, upper)
    sent[11].wait_recv()
    sent[17] = pass_on(17, far_across, twin, lower)
    sent[13].wait_recv()
    sent[18] = pass_on(18, far_across, twin, upper)
    for number in (3, 6, 8, 10, 12, 14, 15, 16, 17, 18):
        sent[number].wait_recv()
    for number in range(19):
        sent[number].wait_send()
    for item in copies:
        item.wait()


def dispatch_all(rows, table, slice_re, slice_im, slice_ctf):
    vmem = pl.BlockSpec(memory_space=pltpu.VMEM)
    dma = pltpu.SemaphoreType.DMA
    return pl.pallas_call(
        dispatch_kernel,
        out_shape=(
            jax.ShapeDtypeStruct((SLABS, 3, STRIP, SLICE), jnp.bfloat16),
            jax.ShapeDtypeStruct((SLABS * SPARE, 3, STRIP, SLICE), jnp.bfloat16),
            jax.ShapeDtypeStruct((SLABS, 8, 128), jnp.float32),
        ),
        in_specs=[pl.BlockSpec(memory_space=pltpu.SMEM)] + [vmem] * 4,
        out_specs=(vmem,) * 3,
        scratch_shapes=[pltpu.VMEM((SLABS, 3, STRIP, SLICE), jnp.bfloat16)]
        + [dma((19,)), dma((19,))] + [dma((SLABS,))] * 4,
        compiler_params=pltpu.CompilerParams(
            collective_id=4, has_side_effects=True, vmem_limit_bytes=40 << 20
        ),
        name="dispatch",
    )(rows, table, slice_re, slice_im, slice_ctf)


def fused_kernel(
    table, trig, cap, spare, out_ref,
    b, a, mid, up, dn, edge, from_low, from_high, halos, half, mirror, perm, back, send, recv,
):
    kz, ky = lax.axis_index("kz"), lax.axis_index("ky")
    above, below = lax.rem(kz + 1, 16), lax.rem(kz + 15, 16)
    after, before = lax.rem(ky + 1, 16), lax.rem(ky + 15, 16)
    partner = {"kz": 15 - kz, "ky": 15 - ky}
    slabs = (below, kz, above)
    peers = [{"kz": above, "ky": ky}, {"kz": below, "ky": ky}]
    peers += [{"kz": s, "ky": r} for s in slabs for r in (before, after)]
    peers += [partner]
    barrier = pltpu.get_barrier_semaphore()
    for peer in peers:
        pl.semaphore_signal(barrier, inc=1, device_id=peer, device_id_type=MESH)

    def copy(source, target, number, peer):
        return pltpu.make_async_remote_copy(
            src_ref=source, dst_ref=target, send_sem=send.at[number], recv_sem=recv.at[number],
            device_id=peer, device_id_type=MESH,
        )

    k = lax.broadcasted_iota(jnp.int32, (1, KA), 1)
    slot, local = k // HALF, k % HALF
    other = slot - SLABS
    place = jnp.where(slot < SLABS, slot * 8, (other // SPARE) * 8 + 1 + other % SPARE)
    pick = (lax.broadcasted_iota(jnp.int32, (SLABS * 8, KA), 0) == place).astype(jnp.float32)
    spread = lax.dot_general(
        table[...].astype(jnp.bfloat16), pick.astype(jnp.bfloat16), (((0,), (0,)), ((), ())),
        preferred_element_type=jnp.float32,
    )

    def field(index):
        return spread[index : index + 1]

    plane, tilt, shift, helix = field(PLANE), field(TILT), field(SHIFT_Y), field(HELIX)
    live = jnp.where(field(DEST) == kz.astype(jnp.float32), field(VALID), 0.0)
    level = (lax.broadcasted_iota(jnp.int32, (16, 1), 0) - MZ).astype(jnp.float32)
    line = lax.broadcasted_iota(jnp.int32, (32, 1), 0)
    main_y = kaiser((line - 2 * local).astype(jnp.float32) - shift)
    low_y = kaiser((-1 - 2 * local).astype(jnp.float32) - shift)
    high_y = kaiser((32 - 2 * local).astype(jnp.float32) - shift)
    cosine = jnp.zeros((16, KA), jnp.float32)
    sine = jnp.zeros((16, KA), jnp.float32)
    for h in range(8):
        cosine = jnp.where(helix == float(h), trig[:, h : h + 1], cosine)
        sine = jnp.where(helix == float(h), trig[:, 8 + h : 9 + h], sine)

    def along_z(q):
        row = ky * STRIP + q * HALF + local - SLICE // 2
        centre = plane + tilt * row.astype(jnp.float32) / (SLICE // 2)
        return kaiser(level - centre) * live

    blocks = [(MAIN, slice(0, 16), low_y), (MAIN + 16, slice(0, 16), high_y)]
    blocks += [(z * 32, slice(z, z + 1), main_y) for z in range(ZE)]

    def spread_slot(source, n, tab_row, first, channels):
        taps = table[pl.ds(tab_row, 1), :]
        wa, wb = taps[:, TAPS : TAPS + 1], taps[:, TAPS + 1 : TAPS + 2]
        wc, wd = taps[:, TAPS + 2 : TAPS + 3], taps[:, TAPS + 3 : TAPS + 4]
        for index, c in enumerate(channels):
            d = source[n, c].astype(jnp.float32)
            even = (wa * d + wb * pltpu.roll(d, 1, 1)).astype(jnp.bfloat16)
            odd = (wc * d + wd * pltpu.roll(d, SLICE - 1, 1)).astype(jnp.bfloat16)
            rows = pl.ds(pl.multiple_of(index * KA + first, HALF), HALF)
            for q in range(2):
                b[q, rows, 0:SLICE] = even[q * HALF : (q + 1) * HALF]
                b[q, rows, SLICE:GRID] = odd[q * HALF : (q + 1) * HALF]

    def spread_all(channels):
        @pl.loop(0, SLABS)
        def _(n):
            spread_slot(cap, n, n * 8, n * HALF, channels)

        @pl.loop(0, SLABS)
        def _(n):
            for j in range(SPARE):
                m = n * SPARE + j
                spread_slot(spare, m, n * 8 + 1 + j, (SLABS + m) * HALF, channels)

    lines = lax.broadcasted_iota(jnp.int32, (1, 32, 1), 1)

    def multiply(c, rows, depth):
        @pl.loop(0, GRID // 256)
        def _(tile):
            cols = pl.ds(pl.multiple_of(tile * 256, 256), 256)
            parts = [
                jnp.dot(a[q, rows, 0:depth], b[q, 0:depth, cols], preferred_element_type=jnp.float32)
                for q in range(2)
            ]
            low = [part[MAIN : MAIN + ZE] for part in parts]
            high = [part[MAIN + 16 : MAIN + 16 + ZE] for part in parts]
            main = [part[:MAIN].reshape(ZE, 32, 256) for part in parts]
            main[0] = main[0] + jnp.where(lines == 31, low[1][:, None, :], 0.0)
            main[1] = main[1] + jnp.where(lines == 0, high[0][:, None, :], 0.0)
            for q in range(2):
                span = slice(q * 32, q * 32 + 32)
                dn[c, :, span, cols] = main[q][0:MZ].astype(jnp.bfloat16)
                mid[c, :, span, cols] = main[q][MZ : MZ + ZD]
                up[c, :, span, cols] = main[q][MZ + ZD :].astype(jnp.bfloat16)
            for j in range(3):
                edge[c, j, 0:ZD, cols] = low[0][j * 4 : j * 4 + 4]
                edge[c, 3 + j, 0:ZD, cols] = high[1][j * 4 : j * 4 + 4]

    def send_margins(c):
        items = [
            copy(up.at[c], from_low.at[c], 9 * c, peers[0]),
            copy(dn.at[c], from_high.at[c], 9 * c + 1, peers[1]),
        ]
        for j in range(3):
            for side, target in ((0, before), (1, after)):
                index = side * 3 + j
                items.append(
                    copy(
                        edge.at[c, index], halos.at[c, index], 9 * c + 2 + index,
                        {"kz": slabs[j], "ky": target},
                    )
                )
        for item in items:
            item.start()
        return items

    lower = jnp.where(kz > 0, 1.0, 0.0)
    upper = jnp.where(kz < 15, 1.0, 0.0)
    last_line = lax.broadcasted_iota(jnp.int32, (LINES, 1), 0)

    def finish(c, items):
        for item in items:
            item.wait()

        @pl.loop(0, ZD)
        def _(p):
            row = pl.ds(p, 1)
            total = mid[c, p] + lower * from_low[c, p].astype(jnp.float32)
            total = total + upper * from_high[c, p].astype(jnp.float32)
            last = upper * halos[c, 0, row, :] + halos[c, 1, row, :] + lower * halos[c, 2, row, :]
            start = upper * halos[c, 3, row, :] + halos[c, 4, row, :] + lower * halos[c, 5, row, :]
            total = total + jnp.where(last_line == LINES - 1, last, 0.0)
            total = total + jnp.where(last_line == 0, start, 0.0)
            half[c, pl.ds(pl.multiple_of(p * LINES, LINES), LINES), :] = total.astype(jnp.bfloat16)

        item = copy(half.at[c], mirror.at[c], 9 * c + 8, partner)
        item.start()
        return item

    spread_all((2,))
    for q in range(2):
        along = along_z(q)
        for first, levels, value_y in blocks:
            size = 16 if first >= MAIN else 32
            a[q, first : first + size, 0:KA] = (along[levels] * value_y).astype(jnp.bfloat16)
    multiply(2, slice(0, MROWS), KA)
    pl.semaphore_wait(barrier, len(peers))
    weight_items = send_margins(2)

    spread_all((0, 1))
    for q in range(2):
        along = along_z(q)
        real, imag = along * cosine, along * sine
        for first, levels, value_y in blocks:
            size = 16 if first >= MAIN else 32
            rows = slice(first, first + size)
            again = slice(MROWS + first, MROWS + first + size)
            kr = (real[levels] * value_y).astype(jnp.bfloat16)
            ki = imag[levels] * value_y
            a[q, rows, 0:KA] = kr
            a[q, rows, KA : 2 * KA] = (-ki).astype(jnp.bfloat16)
            a[q, again, 0:KA] = ki.astype(jnp.bfloat16)
            a[q, again, KA : 2 * KA] = kr
    copies = {2: finish(2, weight_items)}
    multiply(0, slice(0, MROWS), 2 * KA)
    real_items = send_margins(0)
    multiply(1, slice(MROWS, 2 * MROWS), 2 * KA)
    imag_items = send_margins(1)

    @pl.loop(0, GRID // 128)
    def _(tile):
        rows = pl.multiple_of(tile * 128, 128)
        k = lax.broadcasted_iota(jnp.int32, (128, GRID), 0) + rows
        x = lax.broadcasted_iota(jnp.int32, (128, GRID), 1)
        wanted = jnp.where(k < SLICE, 2 * k, 2 * (k - SLICE) + 1)
        perm[pl.ds(rows, 128), :] = (x == wanted).astype(jnp.float32).astype(jnp.bfloat16)
        back[pl.ds(rows, 128), :] = (GRID - 1 - x == wanted).astype(jnp.float32).astype(jnp.bfloat16)

    copies[0] = finish(0, real_items)
    copies[1] = finish(1, imag_items)

    for c in range(3):

        @pl.loop(0, GRID // 256)
        def _(tile):
            cols = pl.ds(pl.multiple_of(tile * 256, 256), 256)
            out_ref[c, :, cols] = jnp.dot(
                half[c], perm[:, cols], preferred_element_type=jnp.float32
            )

    i = lax.broadcasted_iota(jnp.int32, (256, 256), 0)
    j = lax.broadcasted_iota(jnp.int32, (256, 256), 1)
    flip = (i + j == 255).astype(jnp.float32).astype(jnp.bfloat16)
    for c, sign in ((2, 1.0), (0, 1.0), (1, -1.0)):
        copies[c].wait()
        turned = jnp.dot(flip, mirror[c], preferred_element_type=jnp.float32)
        mirror[c] = turned.astype(jnp.bfloat16)

        @pl.loop(0, GRID // 256)
        def _(tile):
            cols = pl.ds(pl.multiple_of(tile * 256, 256), 256)
            out_ref[c, :, cols] += sign * jnp.dot(
                mirror[c], back[:, cols], preferred_element_type=jnp.float32
            )


def fused(table, trig, cap, spare):
    vmem = pl.BlockSpec(memory_space=pltpu.VMEM)
    slab = (3, ZD, LINES, GRID)
    flat = (3, ZD * LINES, GRID)
    return pl.pallas_call(
        fused_kernel,
        out_shape=jax.ShapeDtypeStruct(flat, jnp.float32),
        in_specs=[vmem] * 4,
        out_specs=vmem,
        scratch_shapes=[
            pltpu.VMEM((2, 2 * KA, GRID), jnp.bfloat16),
            pltpu.VMEM((2, 2 * MROWS, 2 * KA), jnp.bfloat16),
            pltpu.VMEM(slab, jnp.float32),
            pltpu.VMEM(slab, jnp.bfloat16),
            pltpu.VMEM(slab, jnp.bfloat16),
            pltpu.VMEM((3, 6, 8, GRID), jnp.float32),
            pltpu.VMEM(slab, jnp.bfloat16),
            pltpu.VMEM(slab, jnp.bfloat16),
            pltpu.VMEM((3, 6, 8, GRID), jnp.float32),
            pltpu.VMEM(flat, jnp.bfloat16),
            pltpu.VMEM(flat, jnp.bfloat16),
            pltpu.VMEM((GRID, GRID), jnp.bfloat16),
            pltpu.VMEM((GRID, GRID), jnp.bfloat16),
            pltpu.SemaphoreType.DMA((27,)),
            pltpu.SemaphoreType.DMA((27,)),
        ],
        compiler_params=pltpu.CompilerParams(
            collective_id=3, has_side_effects=True, vmem_limit_bytes=62 << 20
        ),
        name="fused",
    )(table, trig, cap, spare)


def balanced(slice_re, slice_im, slice_ctf, dest, plane, helix, tilt, shift):
    table, rows = plan(dest, plane, helix, tilt, shift)
    cap, spare, tables = dispatch_all(rows, table, slice_re, slice_im, slice_ctf)
    band = lax.axis_index("kz") * ZD + jnp.arange(16) - MZ
    angle = twist_step * (jnp.arange(8)[None, :] * band[:, None]).astype(jnp.float32)
    trig = jnp.concatenate([jnp.cos(angle), jnp.sin(angle)], axis=1)
    fits = jnp.max(tables[:, 0, EXTRA]) <= SPARE
    return tables.reshape(SLABS * 8, 128), trig, cap, spare, fits


def per_device(*arguments):
    table, trig, cap, spare, fits = balanced(*arguments)
    out = lax.cond(
        fits,
        lambda: fused(table, trig, cap, spare),
        lambda: padded(*arguments),
    )
    return out.reshape(3, ZD, LINES, GRID)


def solution(mesh):
    placed = (
        P("kz", "ky", None),
        P("kz", "ky", None),
        P("kz", "ky", None),
        P("kz", None),
        P("kz"),
        P("kz"),
        P("kz"),
        P(None, "kz"),
    )
    return jax.shard_map(
        per_device, mesh=mesh, in_specs=placed, out_specs=P(None, "kz", "ky", None), check_vma=False
    )
```

```python
import functools
import math

import jax
import jax.numpy as jnp
from jax import lax
from jax.experimental import pallas as pl
from jax.experimental.pallas import tpu as pltpu
from jax.sharding import PartitionSpec as P

ZD = 4
MZ = 4
ZE = 12
CAP = 4
SLABS = 16
SLOTS = SLABS * CAP
SLICE = 512
GRID = 1024
SPARE = 4
ALL = SLABS * (1 + SPARE)
KA = ALL * 16
STRIP = 32
LINES = 64
HALF = 16
KC = SLOTS * HALF
MAIN = ZE * 32
MROWS = MAIN + 32

kernel_beta = 7.4
kernel_reach = 2.0
twist_step = 0.37

MESH = pl.DeviceIdType.MESH


def series(quarter):
    total = jnp.full_like(quarter, 1.0 / math.factorial(25) ** 2)
    for order in range(24, 0, -1):
        total = total * quarter + 1.0 / math.factorial(order) ** 2
    return total * quarter


SCALE = sum((kernel_beta * kernel_beta / 4) ** m / math.factorial(m) ** 2 for m in range(1, 26))


def kaiser(distance):
    inside = jnp.maximum(1.0 - distance * distance * 0.25, 0.0)
    return series(inside * (kernel_beta * kernel_beta * 0.25)) * (1.0 / SCALE)


def insert_kernel(count, w_ref, g_ref, cs_ref, pay_ref, mid_ref, up_ref, dn_ref, halo_ref, b, a):
    row_index = lax.axis_index("ky")

    @pl.loop(0, SLOTS)
    def _(n):
        wa, wb, wc, wd = w_ref[n, 0], w_ref[n, 1], w_ref[n, 2], w_ref[n, 3]
        for c in range(count):
            d = pay_ref[n, c].astype(jnp.float32)
            before = pltpu.roll(d, 1, 1)
            after = pltpu.roll(d, SLICE - 1, 1)
            even = (wa * d + wb * before).astype(jnp.bfloat16)
            odd = (wc * d + wd * after).astype(jnp.bfloat16)
            rows = pl.ds(pl.multiple_of(c * KC + n * HALF, HALF), HALF)
            for q in range(2):
                b[q, rows, 0:SLICE] = even[q * HALF : (q + 1) * HALF]
                b[q, rows, SLICE:GRID] = odd[q * HALF : (q + 1) * HALF]

    plane, live, tilt, shift = g_ref[0:1], g_ref[2:3], g_ref[3:4], g_ref[4:5]
    local = lax.broadcasted_iota(jnp.int32, (1, KC), 1) % HALF
    level = (lax.broadcasted_iota(jnp.int32, (16, 1), 0) - MZ).astype(jnp.float32)
    line = lax.broadcasted_iota(jnp.int32, (32, 1), 0)
    main_y = kaiser((line - 2 * local).astype(jnp.float32) - shift)
    low_y = kaiser((-1 - 2 * local).astype(jnp.float32) - shift)
    high_y = kaiser((32 - 2 * local).astype(jnp.float32) - shift)
    for q in range(2):
        row = row_index * STRIP + q * HALF + local - SLICE // 2
        centre = plane + tilt * row.astype(jnp.float32) / (SLICE // 2)
        along = kaiser(level - centre) * live
        parts = [(MAIN, slice(0, 16), low_y), (MAIN + 16, slice(0, 16), high_y)]
        parts += [(z * 32, slice(z, z + 1), main_y) for z in range(ZE)]
        if count == 2:
            real, imag = along * cs_ref[0:16], along * cs_ref[16:32]
        for first, levels, value_y in parts:
            size = 16 if first >= MAIN else 32
            rows = slice(first, first + size)
            again = slice(MROWS + first, MROWS + first + size)
            if count == 2:
                kr = (real[levels] * value_y).astype(jnp.bfloat16)
                ki = imag[levels] * value_y
                a[q, rows, 0:KC] = kr
                a[q, rows, KC : 2 * KC] = (-ki).astype(jnp.bfloat16)
                a[q, again, 0:KC] = ki.astype(jnp.bfloat16)
                a[q, again, KC : 2 * KC] = kr
            else:
                a[q, rows, :] = (along[levels] * value_y).astype(jnp.bfloat16)

    lines = lax.broadcasted_iota(jnp.int32, (1, 32, 1), 1)

    @pl.loop(0, GRID // 256)
    def _(tile):
        cols = pl.ds(pl.multiple_of(tile * 256, 256), 256)
        for c in range(count):
            parts = [
                jnp.dot(
                    a[q, c * MROWS : (c + 1) * MROWS, :],
                    b[q, :, cols],
                    preferred_element_type=jnp.float32,
                )
                for q in range(2)
            ]
            low = [part[MAIN : MAIN + ZE] for part in parts]
            high = [part[MAIN + 16 : MAIN + 16 + ZE] for part in parts]
            main = [part[:MAIN].reshape(ZE, 32, 256) for part in parts]
            main[0] = main[0] + jnp.where(lines == 31, low[1][:, None, :], 0.0)
            main[1] = main[1] + jnp.where(lines == 0, high[0][:, None, :], 0.0)
            for q in range(2):
                span = slice(q * 32, q * 32 + 32)
                dn_ref[c, :, span, cols] = main[q][0:MZ].astype(jnp.bfloat16)
                mid_ref[c, :, span, cols] = main[q][MZ : MZ + ZD]
                up_ref[c, :, span, cols] = main[q][MZ + ZD :].astype(jnp.bfloat16)
            for j in range(3):
                halo_ref[j, c * ZD : (c + 1) * ZD, cols] = low[0][j * 4 : j * 4 + 4]
                halo_ref[3 + j, c * ZD : (c + 1) * ZD, cols] = high[1][j * 4 : j * 4 + 4]


def insert(count, weights, geometry, phases, payload):
    vmem = pl.BlockSpec(memory_space=pltpu.VMEM)
    return pl.pallas_call(
        functools.partial(insert_kernel, count),
        out_shape=(
            jax.ShapeDtypeStruct((count, ZD, LINES, GRID), jnp.float32),
            jax.ShapeDtypeStruct((count, ZD, LINES, GRID), jnp.bfloat16),
            jax.ShapeDtypeStruct((count, ZD, LINES, GRID), jnp.bfloat16),
            jax.ShapeDtypeStruct((6, 8, GRID), jnp.float32),
        ),
        in_specs=[pl.BlockSpec(memory_space=pltpu.SMEM), vmem, vmem, vmem],
        out_specs=(vmem, vmem, vmem, vmem),
        scratch_shapes=[
            pltpu.VMEM((2, count * KC, GRID), jnp.bfloat16),
            pltpu.VMEM((2, count * MROWS, count * KC), jnp.bfloat16),
        ],
        compiler_params=pltpu.CompilerParams(vmem_limit_bytes=60 << 20),
        cost_estimate=pl.CostEstimate(
            flops=count * count * 4 * MROWS * KC * GRID, bytes_accessed=count * 5 << 20,
            transcendentals=0,
        ),
        name=f"insert{count}",
    )(weights, geometry, phases, payload)


def exchange_kernel(
    count, mid_ref, up_ref, dn_ref, halo_ref, own_ref, back_ref,
    from_low, from_high, halos, half, mirror, perm, back, send, recv,
):
    kz, ky = lax.axis_index("kz"), lax.axis_index("ky")
    above, below = lax.rem(kz + 1, 16), lax.rem(kz + 15, 16)
    after, before = lax.rem(ky + 1, 16), lax.rem(ky + 15, 16)
    partner = {"kz": 15 - kz, "ky": 15 - ky}
    slabs = (below, kz, above)
    peers = [{"kz": above, "ky": ky}, {"kz": below, "ky": ky}]
    peers += [{"kz": s, "ky": r} for s in slabs for r in (before, after)]
    peers += [partner]
    barrier = pltpu.get_barrier_semaphore()
    for peer in peers:
        pl.semaphore_signal(barrier, inc=1, device_id=peer, device_id_type=MESH)
    pl.semaphore_wait(barrier, len(peers))

    def copy(source, target, number, peer):
        return pltpu.make_async_remote_copy(
            src_ref=source, dst_ref=target, send_sem=send.at[number], recv_sem=recv.at[number],
            device_id=peer, device_id_type=MESH,
        )

    edges = []
    for j in range(3):
        for side, target in ((0, before), (1, after)):
            number = side * 3 + j
            edges.append(
                copy(
                    halo_ref.at[number], halos.at[number], number,
                    {"kz": slabs[j], "ky": target},
                )
            )
    margins = [
        (
            copy(up_ref.at[c], from_low.at[c], 6 + 2 * c, peers[0]),
            copy(dn_ref.at[c], from_high.at[c], 7 + 2 * c, peers[1]),
        )
        for c in range(count)
    ]
    for item in edges + [item for pair in margins for item in pair]:
        item.start()

    @pl.loop(0, GRID // 128)
    def _(tile):
        rows = pl.multiple_of(tile * 128, 128)
        k = lax.broadcasted_iota(jnp.int32, (128, GRID), 0) + rows
        x = lax.broadcasted_iota(jnp.int32, (128, GRID), 1)
        wanted = jnp.where(k < SLICE, 2 * k, 2 * (k - SLICE) + 1)
        perm[pl.ds(rows, 128), :] = (x == wanted).astype(jnp.float32).astype(jnp.bfloat16)
        back[pl.ds(rows, 128), :] = (GRID - 1 - x == wanted).astype(jnp.float32).astype(jnp.bfloat16)

    for item in edges:
        item.wait()

    lower = jnp.where(kz > 0, 1.0, 0.0)
    upper = jnp.where(kz < 15, 1.0, 0.0)
    lines = lax.broadcasted_iota(jnp.int32, (LINES, 1), 0)
    copies = []
    for c in range(count):
        for item in margins[c]:
            item.wait()

        @pl.loop(0, ZD)
        def _(p):
            row = pl.ds(c * ZD + p, 1)
            total = mid_ref[c, p] + lower * from_low[c, p].astype(jnp.float32)
            total = total + upper * from_high[c, p].astype(jnp.float32)
            last = upper * halos[0, row, :] + halos[1, row, :] + lower * halos[2, row, :]
            start = upper * halos[3, row, :] + halos[4, row, :] + lower * halos[5, row, :]
            total = total + jnp.where(lines == LINES - 1, last, 0.0)
            total = total + jnp.where(lines == 0, start, 0.0)
            half[c, pl.ds(pl.multiple_of(p * LINES, LINES), LINES), :] = total.astype(jnp.bfloat16)

        item = copy(half.at[c], mirror.at[c], 6 + 2 * count + c, partner)
        item.start()
        copies.append(item)

    for c in range(count):

        @pl.loop(0, GRID // 256)
        def _(tile):
            cols = pl.ds(pl.multiple_of(tile * 256, 256), 256)
            own = jnp.dot(half[c], perm[:, cols], preferred_element_type=jnp.float32)
            own_ref[c, :, cols] = own.astype(jnp.bfloat16)

    i = lax.broadcasted_iota(jnp.int32, (256, 256), 0)
    j = lax.broadcasted_iota(jnp.int32, (256, 256), 1)
    flip = (i + j == 255).astype(jnp.float32).astype(jnp.bfloat16)
    for c in range(count):
        copies[c].wait()
        turned = jnp.dot(flip, mirror[c], preferred_element_type=jnp.float32)
        mirror[c] = turned.astype(jnp.bfloat16)

        @pl.loop(0, GRID // 256)
        def _(tile):
            cols = pl.ds(pl.multiple_of(tile * 256, 256), 256)
            other = jnp.dot(mirror[c], back[:, cols], preferred_element_type=jnp.float32)
            back_ref[c, :, cols] = other.astype(jnp.bfloat16)


def exchange(mid, up, dn, halo):
    count = mid.shape[0]
    vmem = pl.BlockSpec(memory_space=pltpu.VMEM)
    return pl.pallas_call(
        functools.partial(exchange_kernel, count),
        out_shape=(jax.ShapeDtypeStruct((count, ZD * LINES, GRID), jnp.bfloat16),) * 2,
        in_specs=[vmem] * 4,
        out_specs=(vmem,) * 2,
        scratch_shapes=[
            pltpu.VMEM((count, ZD, LINES, GRID), jnp.bfloat16),
            pltpu.VMEM((count, ZD, LINES, GRID), jnp.bfloat16),
            pltpu.VMEM((6, 8, GRID), jnp.float32),
            pltpu.VMEM((count, ZD * LINES, GRID), jnp.bfloat16),
            pltpu.VMEM((count, ZD * LINES, GRID), jnp.bfloat16),
            pltpu.VMEM((GRID, GRID), jnp.bfloat16),
            pltpu.VMEM((GRID, GRID), jnp.bfloat16),
            pltpu.SemaphoreType.DMA((6 + 3 * count,)),
            pltpu.SemaphoreType.DMA((6 + 3 * count,)),
        ],
        compiler_params=pltpu.CompilerParams(
            collective_id=count, has_side_effects=True, vmem_limit_bytes=60 << 20
        ),
        cost_estimate=pl.CostEstimate(
            flops=count * 4 * 256 * GRID * GRID, bytes_accessed=count * 20 << 20, transcendentals=0
        ),
        name=f"exchange{count}",
    )(mid, up, dn, halo)


def padded(
    slice_re, slice_im, slice_ctf, slice_dest, slice_plane, helix_index, slice_tilt, slice_shift
):
    slab_index = lax.axis_index("kz")
    held_count = slice_re.shape[0]
    ctf = slice_ctf.astype(jnp.float32)
    square = (ctf * ctf).astype(jnp.bfloat16)[:, None]
    pair = jnp.stack(
        [ctf * slice_re.astype(jnp.float32), ctf * slice_im.astype(jnp.float32)], axis=1
    ).astype(jnp.bfloat16)
    ones = jnp.ones((held_count,), jnp.float32)
    zeros = jnp.zeros((held_count,), jnp.float32)
    geometry = jnp.stack(
        [
            slice_plane.astype(jnp.float32),
            helix_index.astype(jnp.float32),
            ones,
            slice_tilt.astype(jnp.float32),
            slice_shift[0].astype(jnp.float32),
            slice_shift[1].astype(jnp.float32),
            zeros,
            zeros,
        ],
        axis=1,
    ).astype(jnp.bfloat16)
    target = slice_dest[:, 0]
    onehot = (target[:, None] == jnp.arange(SLABS)[None, :]).astype(jnp.int32)
    ranking = jnp.sum((jnp.cumsum(onehot, axis=0) - 1) * onehot, axis=1)
    position = target * CAP + ranking
    matches = (jnp.arange(SLOTS)[:, None] == position[None, :]).astype(jnp.int32)
    occupied = jnp.sum(matches, axis=1) > 0
    source_row = jnp.sum(matches * jnp.arange(held_count)[None, :], axis=1)

    def dispatch(values):
        picked = jnp.take(values, source_row, axis=0, mode="clip")
        return lax.all_to_all(picked, "kz", split_axis=0, concat_axis=0, tiled=True)

    slots = jnp.where(occupied[:, None], jnp.take(geometry, source_row, axis=0, mode="clip"), 0)
    arrived = lax.all_to_all(slots, "kz", split_axis=0, concat_axis=0, tiled=True)
    square = dispatch(square)
    pair = dispatch(pair)
    arrived = arrived.astype(jnp.float32)
    offset = arrived[:, 5:6]
    weights = kaiser(jnp.array([[0.0, 2.0, 1.0, -1.0]]) - offset)
    weights = weights.astype(jnp.bfloat16).astype(jnp.float32)
    band = slab_index * ZD + jnp.arange(16) - MZ
    angle = twist_step * (arrived[:, 1].astype(jnp.int32)[None, :] * band[:, None]).astype(
        jnp.float32
    )
    phases = jnp.repeat(jnp.concatenate([jnp.cos(angle), jnp.sin(angle)], axis=0), HALF, axis=1)
    spread = jnp.repeat(arrived.T, HALF, axis=1)
    weight = exchange(*insert(1, weights, spread, phases, square))
    signal = exchange(*insert(2, weights, spread, phases, pair))
    return [jnp.concatenate(parts, axis=0) for parts in zip(signal, weight)]


PLANE, HELIX, VALID, TILT, SHIFT_Y, SHIFT_X, DEST, TAPS, EXTRA = 0, 1, 2, 3, 4, 5, 6, 8, 12


def plan_kernel(numbers, reals, table, rows, seen):
    lane = lax.broadcasted_iota(jnp.int32, (1, 128), 1)
    table[...] = jnp.zeros_like(table)
    for d in range(SLABS):
        seen[d] = 0
        rows[d] = 0
        rows[SLABS + d] = 0
    extra = jnp.int32(0)
    for i in range(SLABS):
        d = numbers[0, i]
        fields = (
            (PLANE, numbers[1, i].astype(jnp.float32)),
            (HELIX, numbers[2, i].astype(jnp.float32)),
            (VALID, 1.0), (TILT, reals[0, i]), (SHIFT_Y, reals[1, i]), (SHIFT_X, reals[2, i]),
            (DEST, d.astype(jnp.float32)),
        )
        row = jnp.zeros((1, 128), jnp.float32)
        for index, value in fields:
            row = jnp.where(lane == index, value, row)
        before = seen[d]

        @pl.when(before == 0)
        def _():
            table[d, 0:1, :] = row
            rows[d] = i

        @pl.when((before > 0) & (extra < SPARE))
        def _():
            rows[SLABS + extra] = i
            for other in range(SLABS):
                table[other, pl.ds(1 + extra, 1), :] = row

        seen[d] = before + 1
        extra = extra + jnp.where(before > 0, 1, 0)
    lags = jnp.where(lane == TAPS + 1, 2.0, jnp.where(lane == TAPS + 2, 1.0, 0.0))
    lags = jnp.where(lane == TAPS + 3, -1.0, lags)
    for d in range(SLABS):
        block = table[d]
        taps = kaiser(lags - block[:, SHIFT_X : SHIFT_X + 1])
        taps = taps.astype(jnp.bfloat16).astype(jnp.float32)
        block = jnp.where((lane >= TAPS) & (lane < TAPS + 4), taps, block)
        table[d] = jnp.where(lane == EXTRA, extra.astype(jnp.float32), block)


def plan(dest, plane, helix, tilt, shift):
    smem = pl.BlockSpec(memory_space=pltpu.SMEM)
    return pl.pallas_call(
        plan_kernel,
        out_shape=(
            jax.ShapeDtypeStruct((SLABS, 8, 128), jnp.float32),
            jax.ShapeDtypeStruct((2 * SLABS,), jnp.int32),
        ),
        in_specs=[smem] * 2,
        out_specs=(pl.BlockSpec(memory_space=pltpu.VMEM), smem),
        scratch_shapes=[pltpu.SMEM((SLABS,), jnp.int32)],
        name="plan",
    )(
        jnp.stack([dest[:, 0], plane, helix]),
        jnp.concatenate([tilt[None], shift], axis=0).astype(jnp.float32),
    )


def whole_kernel(
    rows, table, trig, re_ref, im_ref, ctf_ref, own_ref, back_ref, tables,
    outbox, cap, spare, b, bw, a, aw, mid, up, dn, edge, from_low, from_high, halos, half, mirror,
    perm, back, send, recv, hop_send, hop_recv, cap_send, cap_recv, tab_send, tab_recv,
):
    kz, ky = lax.axis_index("kz"), lax.axis_index("ky")
    side, core = kz // 8, lax.rem(kz, 2)
    column = lax.rem(kz, 8) // 2

    def at(other_side, x, c):
        return other_side * 8 + lax.rem(x + 4, 4) * 2 + c

    across, twin = at(1 - side, column, core), at(side, column, 1 - core)
    right, left = at(side, column + 1, core), at(side, column - 1, core)
    far = at(side, column + 2, core)
    right_across, left_across = at(1 - side, column + 1, core), at(1 - side, column - 1, core)
    far_across = at(1 - side, column + 2, core)

    above, below = lax.rem(kz + 1, 16), lax.rem(kz + 15, 16)
    after, before = lax.rem(ky + 1, 16), lax.rem(ky + 15, 16)
    partner = {"kz": 15 - kz, "ky": 15 - ky}
    slabs = (below, kz, above)
    peers = [{"kz": lax.rem(kz + r, SLABS), "ky": ky} for r in range(1, SLABS)]
    peers += [{"kz": s, "ky": r} for s in slabs for r in (before, after)]
    peers += [partner]
    barrier = pltpu.get_barrier_semaphore()
    for peer in peers:
        pl.semaphore_signal(barrier, inc=1, device_id=peer, device_id_type=MESH)

    def pack_signal(row, target, place):
        ctf = ctf_ref[row].astype(jnp.float32)
        target[place, 0] = (ctf * re_ref[row].astype(jnp.float32)).astype(jnp.bfloat16)
        target[place, 1] = (ctf * im_ref[row].astype(jnp.float32)).astype(jnp.bfloat16)

    def pack_weight(row, target, place):
        ctf = ctf_ref[row].astype(jnp.float32)
        target[place, 2] = (ctf * ctf).astype(jnp.bfloat16)

    for j in range(SPARE):
        pack_weight(rows[SLABS + j], spare, kz * SPARE + j)
    pl.semaphore_wait(barrier, len(peers))

    channels = (slice(2, 3), slice(0, 2))
    sent = {}

    def pass_on(group, number, origin, target, part=(0, SPARE)):
        block = spare.at[pl.ds(origin * SPARE + part[0], part[1] - part[0]), channels[group]]
        item = pltpu.make_async_remote_copy(
            src_ref=block, dst_ref=block, send_sem=hop_send.at[group, number],
            recv_sem=hop_recv.at[group, number], device_id={"kz": target}, device_id_type=MESH,
        )
        item.start()
        sent[group, number] = item

    def arrive(group, *numbers):
        for number in numbers:
            sent[group, number].wait_recv()

    halves = ((0, SPARE // 2), (SPARE // 2, SPARE))

    def hop_one(g):
        pass_on(g, 0, kz, across)
        pass_on(g, 1, kz, right)
        pass_on(g, 2, kz, left)
        pass_on(g, 3, kz, twin)

    def hop_two(g):
        arrive(g, 0)
        pass_on(g, 4, across, right)
        pass_on(g, 5, across, left)
        pass_on(g, 6, across, twin)
        arrive(g, 1)
        pass_on(g, 7, left, right, halves[0])
        pass_on(g, 8, left, twin)
        arrive(g, 2)
        pass_on(g, 9, right, left, halves[1])
        pass_on(g, 10, right, twin)

    def hop_three(g):
        arrive(g, 4)
        pass_on(g, 11, left_across, right, halves[0])
        pass_on(g, 12, left_across, twin)
        arrive(g, 5)
        pass_on(g, 13, right_across, left, halves[1])
        pass_on(g, 14, right_across, twin)
        arrive(g, 7)
        pass_on(g, 15, far, twin, halves[0])
        arrive(g, 9)
        pass_on(g, 16, far, twin, halves[1])

    def hop_four(g):
        arrive(g, 11)
        pass_on(g, 17, far_across, twin, halves[0])
        arrive(g, 13)
        pass_on(g, 18, far_across, twin, halves[1])

    direct = {0: [], 1: []}

    def send_caps(g, pack):
        for r in range(1, SLABS):
            d = lax.rem(kz + r, SLABS)
            pack(rows[d], outbox, d)
            item = pltpu.make_async_remote_copy(
                src_ref=outbox.at[d, channels[g]], dst_ref=cap.at[kz, channels[g]],
                send_sem=cap_send.at[g, r], recv_sem=cap_recv.at[g, r],
                device_id={"kz": d}, device_id_type=MESH,
            )
            item.start()
            direct[g].append(item)
        pack(rows[kz], cap, kz)

    hop_one(0)
    labels = []
    for r in range(1, SLABS):
        d = lax.rem(kz + r, SLABS)
        item = pltpu.make_async_remote_copy(
            src_ref=table.at[d], dst_ref=tables.at[kz], send_sem=tab_send.at[r],
            recv_sem=tab_recv.at[r], device_id={"kz": d}, device_id_type=MESH,
        )
        item.start()
        labels.append(item)
    tables[kz] = table[kz]
    send_caps(0, pack_weight)
    for j in range(SPARE):
        pack_signal(rows[SLABS + j], spare, kz * SPARE + j)
    hop_two(0)
    hop_one(1)
    send_caps(1, pack_signal)
    hop_three(0)
    for item in labels:
        item.wait()

    k = lax.broadcasted_iota(jnp.int32, (1, KA), 1)
    slot, local = k // HALF, k % HALF
    other = slot - SLABS
    place = jnp.where(slot < SLABS, slot * 8, (other // SPARE) * 8 + 1 + other % SPARE)
    pick = (lax.broadcasted_iota(jnp.int32, (SLABS * 8, KA), 0) == place).astype(jnp.float32)
    spread = lax.dot_general(
        tables[...].reshape(SLABS * 8, 128).astype(jnp.bfloat16), pick.astype(jnp.bfloat16),
        (((0,), (0,)), ((), ())), preferred_element_type=jnp.float32,
    )

    def field(index):
        return spread[index : index + 1]

    plane, tilt, shift, helix = field(PLANE), field(TILT), field(SHIFT_Y), field(HELIX)
    live = jnp.where(field(DEST) == kz.astype(jnp.float32), field(VALID), 0.0)
    level = (lax.broadcasted_iota(jnp.int32, (16, 1), 0) - MZ).astype(jnp.float32)
    line = lax.broadcasted_iota(jnp.int32, (32, 1), 0)
    main_y = kaiser((line - 2 * local).astype(jnp.float32) - shift)
    low_y = kaiser((-1 - 2 * local).astype(jnp.float32) - shift)
    high_y = kaiser((32 - 2 * local).astype(jnp.float32) - shift)
    cosine = jnp.zeros((16, KA), jnp.float32)
    sine = jnp.zeros((16, KA), jnp.float32)
    for h in range(8):
        cosine = jnp.where(helix == float(h), trig[:, h : h + 1], cosine)
        sine = jnp.where(helix == float(h), trig[:, 8 + h : 9 + h], sine)

    def along_z(q):
        row = ky * STRIP + q * HALF + local - SLICE // 2
        centre = plane + tilt * row.astype(jnp.float32) / (SLICE // 2)
        return kaiser(level - centre) * live

    blocks = [(MAIN, slice(0, 16), low_y), (MAIN + 16, slice(0, 16), high_y)]
    blocks += [(z * 32, slice(z, z + 1), main_y) for z in range(ZE)]

    def spread_slot(source, n, owner, index, first, group):
        taps = tables[owner, pl.ds(index, 1), :]
        wa, wb = taps[:, TAPS : TAPS + 1], taps[:, TAPS + 1 : TAPS + 2]
        wc, wd = taps[:, TAPS + 2 : TAPS + 3], taps[:, TAPS + 3 : TAPS + 4]
        for number, c in enumerate((2,) if group == 0 else (0, 1)):
            d = source[n, c].astype(jnp.float32)
            even = (wa * d + wb * pltpu.roll(d, 1, 1)).astype(jnp.bfloat16)
            odd = (wc * d + wd * pltpu.roll(d, SLICE - 1, 1)).astype(jnp.bfloat16)
            rows = pl.ds(pl.multiple_of(number * KA + first, HALF), HALF)
            target = bw if group == 0 else b
            for q in range(2):
                target[q, rows, 0:SLICE] = even[q * HALF : (q + 1) * HALF]
                target[q, rows, SLICE:GRID] = odd[q * HALF : (q + 1) * HALF]

    def spread_caps(group):
        for item in direct[group]:
            item.wait()

        @pl.loop(0, SLABS)
        def _(n):
            spread_slot(cap, n, n, 0, n * HALF, group)

    def spread_line(group, line_core):
        @pl.loop(0, SLABS // 2)
        def _(i):
            owner = 2 * i + line_core
            for j in range(SPARE):
                m = owner * SPARE + j
                spread_slot(spare, m, owner, 1 + j, (SLABS + m) * HALF, group)

    lines = lax.broadcasted_iota(jnp.int32, (1, 32, 1), 1)

    def multiply(c, left_side, right_side, rows):
        @pl.loop(0, GRID // 256)
        def _(tile):
            cols = pl.ds(pl.multiple_of(tile * 256, 256), 256)
            parts = [
                jnp.dot(
                    left_side[q, rows, :], right_side[q, :, cols],
                    preferred_element_type=jnp.float32,
                )
                for q in range(2)
            ]
            low = [part[MAIN : MAIN + ZE] for part in parts]
            high = [part[MAIN + 16 : MAIN + 16 + ZE] for part in parts]
            main = [part[:MAIN].reshape(ZE, 32, 256) for part in parts]
            main[0] = main[0] + jnp.where(lines == 31, low[1][:, None, :], 0.0)
            main[1] = main[1] + jnp.where(lines == 0, high[0][:, None, :], 0.0)
            for q in range(2):
                span = slice(q * 32, q * 32 + 32)
                dn[c, :, span, cols] = main[q][0:MZ].astype(jnp.bfloat16)
                mid[c, :, span, cols] = main[q][MZ : MZ + ZD]
                up[c, :, span, cols] = main[q][MZ + ZD :].astype(jnp.bfloat16)
            for j in range(3):
                edge[c, j, 0:ZD, cols] = low[0][j * 4 : j * 4 + 4]
                edge[c, 3 + j, 0:ZD, cols] = high[1][j * 4 : j * 4 + 4]

    def copy(source, target, number, peer):
        return pltpu.make_async_remote_copy(
            src_ref=source, dst_ref=target, send_sem=send.at[number], recv_sem=recv.at[number],
            device_id=peer, device_id_type=MESH,
        )

    def send_margins(c):
        items = [
            copy(up.at[c], from_low.at[c], 9 * c, {"kz": above, "ky": ky}),
            copy(dn.at[c], from_high.at[c], 9 * c + 1, {"kz": below, "ky": ky}),
        ]
        for j in range(3):
            for end, target in ((0, before), (1, after)):
                index = end * 3 + j
                items.append(
                    copy(
                        edge.at[c, index], halos.at[c, index], 9 * c + 2 + index,
                        {"kz": slabs[j], "ky": target},
                    )
                )
        for item in items:
            item.start()
        return items

    lower = jnp.where(kz > 0, 1.0, 0.0)
    upper = jnp.where(kz < 15, 1.0, 0.0)
    last_line = lax.broadcasted_iota(jnp.int32, (LINES, 1), 0)

    def finish(c, items):
        for item in items:
            item.wait()

        @pl.loop(0, ZD)
        def _(p):
            row = pl.ds(p, 1)
            total = mid[c, p] + lower * from_low[c, p].astype(jnp.float32)
            total = total + upper * from_high[c, p].astype(jnp.float32)
            last = upper * halos[c, 0, row, :] + halos[c, 1, row, :] + lower * halos[c, 2, row, :]
            start = upper * halos[c, 3, row, :] + halos[c, 4, row, :] + lower * halos[c, 5, row, :]
            total = total + jnp.where(last_line == LINES - 1, last, 0.0)
            total = total + jnp.where(last_line == 0, start, 0.0)
            half[c, pl.ds(pl.multiple_of(p * LINES, LINES), LINES), :] = total.astype(jnp.bfloat16)

        item = copy(half.at[c], mirror.at[c], 9 * c + 8, partner)
        item.start()
        return item

    for q in range(2):
        along = along_z(q)
        for first, levels, value_y in blocks:
            size = 16 if first >= MAIN else 32
            aw[q, first : first + size, :] = (along[levels] * value_y).astype(jnp.bfloat16)
    hop_four(0)
    hop_two(1)
    spread_caps(0)
    spread_line(0, core)
    arrive(0, 3, 6, 8, 10, 12, 14, 15, 16, 17, 18)
    spread_line(0, 1 - core)
    hop_three(1)
    multiply(2, aw, bw, slice(0, MROWS))
    weight_items = send_margins(2)
    hop_four(1)
    spread_caps(1)
    for q in range(2):
        along = along_z(q)
        real, imag = along * cosine, along * sine
        for first, levels, value_y in blocks:
            size = 16 if first >= MAIN else 32
            rows_re = slice(first, first + size)
            rows_im = slice(MROWS + first, MROWS + first + size)
            kr = (real[levels] * value_y).astype(jnp.bfloat16)
            ki = imag[levels] * value_y
            a[q, rows_re, 0:KA] = kr
            a[q, rows_re, KA : 2 * KA] = (-ki).astype(jnp.bfloat16)
            a[q, rows_im, 0:KA] = ki.astype(jnp.bfloat16)
            a[q, rows_im, KA : 2 * KA] = kr
    spread_line(1, core)
    copies = {2: finish(2, weight_items)}
    arrive(1, 3, 6, 8, 10, 12, 14, 15, 16, 17, 18)
    spread_line(1, 1 - core)
    multiply(0, a, b, slice(0, MROWS))
    real_items = send_margins(0)
    multiply(1, a, b, slice(MROWS, 2 * MROWS))
    imag_items = send_margins(1)
    for item in sent.values():
        item.wait_send()

    @pl.loop(0, GRID // 128)
    def _(tile):
        rows = pl.multiple_of(tile * 128, 128)
        k = lax.broadcasted_iota(jnp.int32, (128, GRID), 0) + rows
        x = lax.broadcasted_iota(jnp.int32, (128, GRID), 1)
        wanted = jnp.where(k < SLICE, 2 * k, 2 * (k - SLICE) + 1)
        perm[pl.ds(rows, 128), :] = (x == wanted).astype(jnp.float32).astype(jnp.bfloat16)
        back[pl.ds(rows, 128), :] = (GRID - 1 - x == wanted).astype(jnp.float32).astype(jnp.bfloat16)

    copies[0] = finish(0, real_items)
    copies[1] = finish(1, imag_items)

    for c in range(3):

        @pl.loop(0, GRID // 256)
        def _(tile):
            cols = pl.ds(pl.multiple_of(tile * 256, 256), 256)
            own = jnp.dot(half[c], perm[:, cols], preferred_element_type=jnp.float32)
            own_ref[c, :, cols] = own.astype(jnp.bfloat16)

    i = lax.broadcasted_iota(jnp.int32, (256, 256), 0)
    j = lax.broadcasted_iota(jnp.int32, (256, 256), 1)
    flip = (i + j == 255).astype(jnp.float32).astype(jnp.bfloat16)
    for c in (2, 0, 1):
        copies[c].wait()
        turned = jnp.dot(flip, mirror[c], preferred_element_type=jnp.float32)
        mirror[c] = turned.astype(jnp.bfloat16)

        @pl.loop(0, GRID // 256)
        def _(tile):
            cols = pl.ds(pl.multiple_of(tile * 256, 256), 256)
            other = jnp.dot(mirror[c], back[:, cols], preferred_element_type=jnp.float32)
            back_ref[c, :, cols] = other.astype(jnp.bfloat16)


def whole(rows, table, trig, slice_re, slice_im, slice_ctf):
    vmem = pl.BlockSpec(memory_space=pltpu.VMEM)
    dma = pltpu.SemaphoreType.DMA
    bf16 = jnp.bfloat16
    slab = (3, ZD, LINES, GRID)
    flat = (3, ZD * LINES, GRID)
    slots = (3, STRIP, SLICE)
    return pl.pallas_call(
        whole_kernel,
        out_shape=(
            jax.ShapeDtypeStruct(flat, bf16),
            jax.ShapeDtypeStruct(flat, bf16),
            jax.ShapeDtypeStruct((SLABS, 8, 128), jnp.float32),
        ),
        in_specs=[pl.BlockSpec(memory_space=pltpu.SMEM)] + [vmem] * 5,
        out_specs=(vmem,) * 3,
        scratch_shapes=[
            pltpu.VMEM((SLABS,) + slots, bf16),
            pltpu.VMEM((SLABS,) + slots, bf16),
            pltpu.VMEM((SLABS * SPARE,) + slots, bf16),
            pltpu.VMEM((2, 2 * KA, GRID), bf16),
            pltpu.VMEM((2, KA, GRID), bf16),
            pltpu.VMEM((2, 2 * MROWS, 2 * KA), bf16),
            pltpu.VMEM((2, MROWS, KA), bf16),
            pltpu.VMEM(slab, jnp.float32),
            pltpu.VMEM(slab, bf16),
            pltpu.VMEM(slab, bf16),
            pltpu.VMEM((3, 6, 8, GRID), jnp.float32),
            pltpu.VMEM(slab, bf16),
            pltpu.VMEM(slab, bf16),
            pltpu.VMEM((3, 6, 8, GRID), jnp.float32),
            pltpu.VMEM(flat, bf16),
            pltpu.VMEM(flat, bf16),
            pltpu.VMEM((GRID, GRID), bf16),
            pltpu.VMEM((GRID, GRID), bf16),
            dma((27,)), dma((27,)), dma((2, 19)), dma((2, 19)),
            dma((2, SLABS)), dma((2, SLABS)), dma((SLABS,)), dma((SLABS,)),
        ],
        compiler_params=pltpu.CompilerParams(
            collective_id=3, has_side_effects=True, vmem_limit_bytes=63 << 20
        ),
        name="whole",
    )(rows, table, trig, slice_re, slice_im, slice_ctf)


def per_device(*arguments):
    slice_re, slice_im, slice_ctf, dest, plane, helix, tilt, shift = arguments
    table, rows = plan(dest, plane, helix, tilt, shift)
    band = lax.axis_index("kz") * ZD + jnp.arange(16) - MZ
    angle = twist_step * (jnp.arange(8)[None, :] * band[:, None]).astype(jnp.float32)
    trig = jnp.concatenate([jnp.cos(angle), jnp.sin(angle)], axis=1)
    own, back, tables = whole(rows, table, trig, slice_re, slice_im, slice_ctf)
    signs = jnp.array([1.0, -1.0, 1.0], jnp.float32).reshape(3, 1, 1)

    def fold(own, back):
        out = own.astype(jnp.float32) + signs * back.astype(jnp.float32)
        return out.reshape(3, ZD, LINES, GRID)

    return lax.cond(
        jnp.max(tables[:, 0, EXTRA]) <= SPARE,
        lambda: fold(own, back),
        lambda: fold(*padded(*arguments)),
    )


def solution(mesh):
    placed = (
        P("kz", "ky", None),
        P("kz", "ky", None),
        P("kz", "ky", None),
        P("kz", None),
        P("kz"),
        P("kz"),
        P("kz"),
        P(None, "kz"),
    )
    return jax.shard_map(
        per_device, mesh=mesh, in_specs=placed, out_specs=P(None, "kz", "ky", None), check_vma=False
    )
```

```python
import functools
import math

import jax
import jax.numpy as jnp
from jax import lax
from jax.experimental import pallas as pl
from jax.experimental.pallas import tpu as pltpu
from jax.sharding import PartitionSpec as P

ZD = 4
MZ = 4
ZE = 12
CAP = 4
SLABS = 16
SLOTS = SLABS * CAP
SLICE = 512
GRID = 1024
SPARE = 4
ALL = SLABS * (1 + SPARE)
KA = ALL * 16
STRIP = 32
LINES = 64
HALF = 16
KC = SLOTS * HALF
MAIN = ZE * 32
MROWS = MAIN + 32

kernel_beta = 7.4
kernel_reach = 2.0
twist_step = 0.37

MESH = pl.DeviceIdType.MESH


def series(quarter):
    total = jnp.full_like(quarter, 1.0 / math.factorial(25) ** 2)
    for order in range(24, 0, -1):
        total = total * quarter + 1.0 / math.factorial(order) ** 2
    return total * quarter


SCALE = sum((kernel_beta * kernel_beta / 4) ** m / math.factorial(m) ** 2 for m in range(1, 26))


def kaiser(distance):
    inside = jnp.maximum(1.0 - distance * distance * 0.25, 0.0)
    return series(inside * (kernel_beta * kernel_beta * 0.25)) * (1.0 / SCALE)


def insert_kernel(count, w_ref, g_ref, cs_ref, pay_ref, mid_ref, up_ref, dn_ref, halo_ref, b, a):
    row_index = lax.axis_index("ky")

    @pl.loop(0, SLOTS)
    def _(n):
        wa, wb, wc, wd = w_ref[n, 0], w_ref[n, 1], w_ref[n, 2], w_ref[n, 3]
        for c in range(count):
            d = pay_ref[n, c].astype(jnp.float32)
            before = pltpu.roll(d, 1, 1)
            after = pltpu.roll(d, SLICE - 1, 1)
            even = (wa * d + wb * before).astype(jnp.bfloat16)
            odd = (wc * d + wd * after).astype(jnp.bfloat16)
            rows = pl.ds(pl.multiple_of(c * KC + n * HALF, HALF), HALF)
            for q in range(2):
                b[q, rows, 0:SLICE] = even[q * HALF : (q + 1) * HALF]
                b[q, rows, SLICE:GRID] = odd[q * HALF : (q + 1) * HALF]

    plane, live, tilt, shift = g_ref[0:1], g_ref[2:3], g_ref[3:4], g_ref[4:5]
    local = lax.broadcasted_iota(jnp.int32, (1, KC), 1) % HALF
    level = (lax.broadcasted_iota(jnp.int32, (16, 1), 0) - MZ).astype(jnp.float32)
    line = lax.broadcasted_iota(jnp.int32, (32, 1), 0)
    main_y = kaiser((line - 2 * local).astype(jnp.float32) - shift)
    low_y = kaiser((-1 - 2 * local).astype(jnp.float32) - shift)
    high_y = kaiser((32 - 2 * local).astype(jnp.float32) - shift)
    for q in range(2):
        row = row_index * STRIP + q * HALF + local - SLICE // 2
        centre = plane + tilt * row.astype(jnp.float32) / (SLICE // 2)
        along = kaiser(level - centre) * live
        parts = [(MAIN, slice(0, 16), low_y), (MAIN + 16, slice(0, 16), high_y)]
        parts += [(z * 32, slice(z, z + 1), main_y) for z in range(ZE)]
        if count == 2:
            real, imag = along * cs_ref[0:16], along * cs_ref[16:32]
        for first, levels, value_y in parts:
            size = 16 if first >= MAIN else 32
            rows = slice(first, first + size)
            again = slice(MROWS + first, MROWS + first + size)
            if count == 2:
                kr = (real[levels] * value_y).astype(jnp.bfloat16)
                ki = imag[levels] * value_y
                a[q, rows, 0:KC] = kr
                a[q, rows, KC : 2 * KC] = (-ki).astype(jnp.bfloat16)
                a[q, again, 0:KC] = ki.astype(jnp.bfloat16)
                a[q, again, KC : 2 * KC] = kr
            else:
                a[q, rows, :] = (along[levels] * value_y).astype(jnp.bfloat16)

    lines = lax.broadcasted_iota(jnp.int32, (1, 32, 1), 1)

    @pl.loop(0, GRID // 256)
    def _(tile):
        cols = pl.ds(pl.multiple_of(tile * 256, 256), 256)
        for c in range(count):
            parts = [
                jnp.dot(
                    a[q, c * MROWS : (c + 1) * MROWS, :],
                    b[q, :, cols],
                    preferred_element_type=jnp.float32,
                )
                for q in range(2)
            ]
            low = [part[MAIN : MAIN + ZE] for part in parts]
            high = [part[MAIN + 16 : MAIN + 16 + ZE] for part in parts]
            main = [part[:MAIN].reshape(ZE, 32, 256) for part in parts]
            main[0] = main[0] + jnp.where(lines == 31, low[1][:, None, :], 0.0)
            main[1] = main[1] + jnp.where(lines == 0, high[0][:, None, :], 0.0)
            for q in range(2):
                span = slice(q * 32, q * 32 + 32)
                dn_ref[c, :, span, cols] = main[q][0:MZ].astype(jnp.bfloat16)
                mid_ref[c, :, span, cols] = main[q][MZ : MZ + ZD]
                up_ref[c, :, span, cols] = main[q][MZ + ZD :].astype(jnp.bfloat16)
            for j in range(3):
                halo_ref[j, c * ZD : (c + 1) * ZD, cols] = low[0][j * 4 : j * 4 + 4]
                halo_ref[3 + j, c * ZD : (c + 1) * ZD, cols] = high[1][j * 4 : j * 4 + 4]


def insert(count, weights, geometry, phases, payload):
    vmem = pl.BlockSpec(memory_space=pltpu.VMEM)
    return pl.pallas_call(
        functools.partial(insert_kernel, count),
        out_shape=(
            jax.ShapeDtypeStruct((count, ZD, LINES, GRID), jnp.float32),
            jax.ShapeDtypeStruct((count, ZD, LINES, GRID), jnp.bfloat16),
            jax.ShapeDtypeStruct((count, ZD, LINES, GRID), jnp.bfloat16),
            jax.ShapeDtypeStruct((6, 8, GRID), jnp.float32),
        ),
        in_specs=[pl.BlockSpec(memory_space=pltpu.SMEM), vmem, vmem, vmem],
        out_specs=(vmem, vmem, vmem, vmem),
        scratch_shapes=[
            pltpu.VMEM((2, count * KC, GRID), jnp.bfloat16),
            pltpu.VMEM((2, count * MROWS, count * KC), jnp.bfloat16),
        ],
        compiler_params=pltpu.CompilerParams(vmem_limit_bytes=60 << 20),
        cost_estimate=pl.CostEstimate(
            flops=count * count * 4 * MROWS * KC * GRID, bytes_accessed=count * 5 << 20,
            transcendentals=0,
        ),
        name=f"insert{count}",
    )(weights, geometry, phases, payload)


def exchange_kernel(
    count, mid_ref, up_ref, dn_ref, halo_ref, own_ref, back_ref,
    from_low, from_high, halos, half, mirror, perm, back, send, recv,
):
    kz, ky = lax.axis_index("kz"), lax.axis_index("ky")
    above, below = lax.rem(kz + 1, 16), lax.rem(kz + 15, 16)
    after, before = lax.rem(ky + 1, 16), lax.rem(ky + 15, 16)
    partner = {"kz": 15 - kz, "ky": 15 - ky}
    slabs = (below, kz, above)
    peers = [{"kz": above, "ky": ky}, {"kz": below, "ky": ky}]
    peers += [{"kz": s, "ky": r} for s in slabs for r in (before, after)]
    peers += [partner]
    barrier = pltpu.get_barrier_semaphore()
    for peer in peers:
        pl.semaphore_signal(barrier, inc=1, device_id=peer, device_id_type=MESH)
    pl.semaphore_wait(barrier, len(peers))

    def copy(source, target, number, peer):
        return pltpu.make_async_remote_copy(
            src_ref=source, dst_ref=target, send_sem=send.at[number], recv_sem=recv.at[number],
            device_id=peer, device_id_type=MESH,
        )

    edges = []
    for j in range(3):
        for side, target in ((0, before), (1, after)):
            number = side * 3 + j
            edges.append(
                copy(
                    halo_ref.at[number], halos.at[number], number,
                    {"kz": slabs[j], "ky": target},
                )
            )
    margins = [
        (
            copy(up_ref.at[c], from_low.at[c], 6 + 2 * c, peers[0]),
            copy(dn_ref.at[c], from_high.at[c], 7 + 2 * c, peers[1]),
        )
        for c in range(count)
    ]
    for item in edges + [item for pair in margins for item in pair]:
        item.start()

    @pl.loop(0, GRID // 128)
    def _(tile):
        rows = pl.multiple_of(tile * 128, 128)
        k = lax.broadcasted_iota(jnp.int32, (128, GRID), 0) + rows
        x = lax.broadcasted_iota(jnp.int32, (128, GRID), 1)
        wanted = jnp.where(k < SLICE, 2 * k, 2 * (k - SLICE) + 1)
        perm[pl.ds(rows, 128), :] = (x == wanted).astype(jnp.float32).astype(jnp.bfloat16)
        back[pl.ds(rows, 128), :] = (GRID - 1 - x == wanted).astype(jnp.float32).astype(jnp.bfloat16)

    for item in edges:
        item.wait()

    lower = jnp.where(kz > 0, 1.0, 0.0)
    upper = jnp.where(kz < 15, 1.0, 0.0)
    lines = lax.broadcasted_iota(jnp.int32, (LINES, 1), 0)
    copies = []
    for c in range(count):
        for item in margins[c]:
            item.wait()

        @pl.loop(0, ZD)
        def _(p):
            row = pl.ds(c * ZD + p, 1)
            total = mid_ref[c, p] + lower * from_low[c, p].astype(jnp.float32)
            total = total + upper * from_high[c, p].astype(jnp.float32)
            last = upper * halos[0, row, :] + halos[1, row, :] + lower * halos[2, row, :]
            start = upper * halos[3, row, :] + halos[4, row, :] + lower * halos[5, row, :]
            total = total + jnp.where(lines == LINES - 1, last, 0.0)
            total = total + jnp.where(lines == 0, start, 0.0)
            half[c, pl.ds(pl.multiple_of(p * LINES, LINES), LINES), :] = total.astype(jnp.bfloat16)

        item = copy(half.at[c], mirror.at[c], 6 + 2 * count + c, partner)
        item.start()
        copies.append(item)

    for c in range(count):

        @pl.loop(0, GRID // 256)
        def _(tile):
            cols = pl.ds(pl.multiple_of(tile * 256, 256), 256)
            own = jnp.dot(half[c], perm[:, cols], preferred_element_type=jnp.float32)
            own_ref[c, :, cols] = own.astype(jnp.bfloat16)

    i = lax.broadcasted_iota(jnp.int32, (256, 256), 0)
    j = lax.broadcasted_iota(jnp.int32, (256, 256), 1)
    flip = (i + j == 255).astype(jnp.float32).astype(jnp.bfloat16)
    for c in range(count):
        copies[c].wait()
        turned = jnp.dot(flip, mirror[c], preferred_element_type=jnp.float32)
        mirror[c] = turned.astype(jnp.bfloat16)

        @pl.loop(0, GRID // 256)
        def _(tile):
            cols = pl.ds(pl.multiple_of(tile * 256, 256), 256)
            other = jnp.dot(mirror[c], back[:, cols], preferred_element_type=jnp.float32)
            back_ref[c, :, cols] = other.astype(jnp.bfloat16)


def exchange(mid, up, dn, halo):
    count = mid.shape[0]
    vmem = pl.BlockSpec(memory_space=pltpu.VMEM)
    return pl.pallas_call(
        functools.partial(exchange_kernel, count),
        out_shape=(jax.ShapeDtypeStruct((count, ZD * LINES, GRID), jnp.bfloat16),) * 2,
        in_specs=[vmem] * 4,
        out_specs=(vmem,) * 2,
        scratch_shapes=[
            pltpu.VMEM((count, ZD, LINES, GRID), jnp.bfloat16),
            pltpu.VMEM((count, ZD, LINES, GRID), jnp.bfloat16),
            pltpu.VMEM((6, 8, GRID), jnp.float32),
            pltpu.VMEM((count, ZD * LINES, GRID), jnp.bfloat16),
            pltpu.VMEM((count, ZD * LINES, GRID), jnp.bfloat16),
            pltpu.VMEM((GRID, GRID), jnp.bfloat16),
            pltpu.VMEM((GRID, GRID), jnp.bfloat16),
            pltpu.SemaphoreType.DMA((6 + 3 * count,)),
            pltpu.SemaphoreType.DMA((6 + 3 * count,)),
        ],
        compiler_params=pltpu.CompilerParams(
            collective_id=count, has_side_effects=True, vmem_limit_bytes=60 << 20
        ),
        cost_estimate=pl.CostEstimate(
            flops=count * 4 * 256 * GRID * GRID, bytes_accessed=count * 20 << 20, transcendentals=0
        ),
        name=f"exchange{count}",
    )(mid, up, dn, halo)


def padded(
    slice_re, slice_im, slice_ctf, slice_dest, slice_plane, helix_index, slice_tilt, slice_shift
):
    slab_index = lax.axis_index("kz")
    held_count = slice_re.shape[0]
    ctf = slice_ctf.astype(jnp.float32)
    square = (ctf * ctf).astype(jnp.bfloat16)[:, None]
    pair = jnp.stack(
        [ctf * slice_re.astype(jnp.float32), ctf * slice_im.astype(jnp.float32)], axis=1
    ).astype(jnp.bfloat16)
    ones = jnp.ones((held_count,), jnp.float32)
    zeros = jnp.zeros((held_count,), jnp.float32)
    geometry = jnp.stack(
        [
            slice_plane.astype(jnp.float32),
            helix_index.astype(jnp.float32),
            ones,
            slice_tilt.astype(jnp.float32),
            slice_shift[0].astype(jnp.float32),
            slice_shift[1].astype(jnp.float32),
            zeros,
            zeros,
        ],
        axis=1,
    ).astype(jnp.bfloat16)
    target = slice_dest[:, 0]
    onehot = (target[:, None] == jnp.arange(SLABS)[None, :]).astype(jnp.int32)
    ranking = jnp.sum((jnp.cumsum(onehot, axis=0) - 1) * onehot, axis=1)
    position = target * CAP + ranking
    matches = (jnp.arange(SLOTS)[:, None] == position[None, :]).astype(jnp.int32)
    occupied = jnp.sum(matches, axis=1) > 0
    source_row = jnp.sum(matches * jnp.arange(held_count)[None, :], axis=1)

    def dispatch(values):
        picked = jnp.take(values, source_row, axis=0, mode="clip")
        return lax.all_to_all(picked, "kz", split_axis=0, concat_axis=0, tiled=True)

    slots = jnp.where(occupied[:, None], jnp.take(geometry, source_row, axis=0, mode="clip"), 0)
    arrived = lax.all_to_all(slots, "kz", split_axis=0, concat_axis=0, tiled=True)
    square = dispatch(square)
    pair = dispatch(pair)
    arrived = arrived.astype(jnp.float32)
    offset = arrived[:, 5:6]
    weights = kaiser(jnp.array([[0.0, 2.0, 1.0, -1.0]]) - offset)
    weights = weights.astype(jnp.bfloat16).astype(jnp.float32)
    band = slab_index * ZD + jnp.arange(16) - MZ
    angle = twist_step * (arrived[:, 1].astype(jnp.int32)[None, :] * band[:, None]).astype(
        jnp.float32
    )
    phases = jnp.repeat(jnp.concatenate([jnp.cos(angle), jnp.sin(angle)], axis=0), HALF, axis=1)
    spread = jnp.repeat(arrived.T, HALF, axis=1)
    weight = exchange(*insert(1, weights, spread, phases, square))
    signal = exchange(*insert(2, weights, spread, phases, pair))
    return [jnp.concatenate(parts, axis=0) for parts in zip(signal, weight)]


PLANE, HELIX, VALID, TILT, SHIFT_Y, SHIFT_X, DEST, TAPS, EXTRA = 0, 1, 2, 3, 4, 5, 6, 8, 12


def whole_kernel(
    dest, dest_line, plane_line, helix_line, tilt_line, shift_lines, re_ref, im_ref, ctf_ref,
    own_ref, back_ref, flag_ref, tables, table, held, rows, outbox, cap, spare, b, bw, a, aw, mid, up, dn, edge, from_low, from_high, halos, half, mirror,
    perm, back, send, recv, hop_send, hop_recv, cap_send, cap_recv, tab_send, tab_recv,
):
    kz, ky = lax.axis_index("kz"), lax.axis_index("ky")
    side, core = kz // 8, lax.rem(kz, 2)
    column = lax.rem(kz, 8) // 2

    def at(other_side, x, c):
        return other_side * 8 + lax.rem(x + 4, 4) * 2 + c

    across, twin = at(1 - side, column, core), at(side, column, 1 - core)
    right, left = at(side, column + 1, core), at(side, column - 1, core)
    far = at(side, column + 2, core)
    right_across, left_across = at(1 - side, column + 1, core), at(1 - side, column - 1, core)
    far_across = at(1 - side, column + 2, core)

    above, below = lax.rem(kz + 1, 16), lax.rem(kz + 15, 16)
    after, before = lax.rem(ky + 1, 16), lax.rem(ky + 15, 16)
    partner = {"kz": 15 - kz, "ky": 15 - ky}
    slabs = (below, kz, above)
    peers = [{"kz": lax.rem(kz + r, SLABS), "ky": ky} for r in range(1, SLABS)]
    peers += [{"kz": s, "ky": r} for s in slabs for r in (before, after)]
    peers += [partner]
    barrier = pltpu.get_barrier_semaphore()
    for peer in peers:
        pl.semaphore_signal(barrier, inc=1, device_id=peer, device_id_type=MESH)

    first = []
    for d in range(SLABS):
        found = jnp.int32(SLABS)
        for i in reversed(range(SLABS)):
            found = jnp.where(dest[i] == d, i, found)
        first.append(found)
    extra = jnp.int32(0)
    spare_rows = [jnp.int32(0)] * SPARE
    for i in range(1, SLABS):
        again = dest[i] == dest[0]
        for earlier in range(1, i):
            again = again | (dest[i] == dest[earlier])
        for j in range(SPARE):
            spare_rows[j] = jnp.where(again & (extra == j), i, spare_rows[j])
        extra = extra + jnp.where(again, 1, 0)

    def pack_signal(row, target, place):
        ctf = ctf_ref[row].astype(jnp.float32)
        target[place, 0] = (ctf * re_ref[row].astype(jnp.float32)).astype(jnp.bfloat16)
        target[place, 1] = (ctf * im_ref[row].astype(jnp.float32)).astype(jnp.bfloat16)

    def pack_weight(row, target, place):
        ctf = ctf_ref[row].astype(jnp.float32)
        target[place, 2] = (ctf * ctf).astype(jnp.bfloat16)

    for j in range(SPARE):
        pack_weight(spare_rows[j], spare, kz * SPARE + j)

    lane = lax.broadcasted_iota(jnp.int32, (1, 128), 1)
    kind = lax.broadcasted_iota(jnp.int32, (8, SLABS), 0)
    fields = jnp.where(kind == VALID, 1.0, 0.0)
    shifts = shift_lines[...].astype(jnp.float32)
    for index, value in (
        (PLANE, plane_line[...].astype(jnp.float32)),
        (HELIX, helix_line[...].astype(jnp.float32)),
        (TILT, tilt_line[...].astype(jnp.float32)), (SHIFT_Y, shifts[0:1]),
        (SHIFT_X, shifts[1:2]), (DEST, dest_line[...].astype(jnp.float32)),
    ):
        fields = jnp.where(kind == index, value, fields)
    same = lax.broadcasted_iota(jnp.int32, (8, 128), 0) == lax.broadcasted_iota(
        jnp.int32, (8, 128), 1
    )
    notes = lax.dot_general(
        fields.astype(jnp.bfloat16), same.astype(jnp.float32).astype(jnp.bfloat16),
        (((0,), (0,)), ((), ())), preferred_element_type=jnp.float32,
    )
    lags = jnp.where(lane == TAPS + 1, 2.0, jnp.where(lane == TAPS + 2, 1.0, 0.0))
    lags = jnp.where(lane == TAPS + 3, -1.0, lags)
    taps = kaiser(lags - notes[:, SHIFT_X : SHIFT_X + 1])
    taps = taps.astype(jnp.bfloat16).astype(jnp.float32)
    held[...] = jnp.where((lane >= TAPS) & (lane < TAPS + 4), taps, notes)
    count = extra.astype(jnp.float32)
    shared = [jnp.zeros((1, 128), jnp.float32)]
    for j in range(SPARE):
        shared.append(jnp.where(extra > j, 1.0, 0.0) * held[pl.ds(spare_rows[j], 1), :])
    for d in range(SLABS):
        there = jnp.where(first[d] < SLABS, 1.0, 0.0)
        first[d] = jnp.where(first[d] < SLABS, first[d], 0)
        shared[0] = there * held[pl.ds(first[d], 1), :]
        for j in range(1 + SPARE):
            table[d, j : j + 1, :] = jnp.where(lane == EXTRA, count, shared[j])
        table[d, 1 + SPARE : 8, :] = jnp.zeros((7 - SPARE, 128), jnp.float32)
        rows[d] = first[d]
    pl.semaphore_wait(barrier, len(peers))

    channels = (slice(2, 3), slice(0, 2))
    sent = {}

    def pass_on(group, number, origin, target, part=(0, SPARE)):
        block = spare.at[pl.ds(origin * SPARE + part[0], part[1] - part[0]), channels[group]]
        item = pltpu.make_async_remote_copy(
            src_ref=block, dst_ref=block, send_sem=hop_send.at[group, number],
            recv_sem=hop_recv.at[group, number], device_id={"kz": target}, device_id_type=MESH,
        )
        item.start()
        sent[group, number] = item

    def arrive(group, *numbers):
        for number in numbers:
            sent[group, number].wait_recv()

    halves = ((0, SPARE // 2), (SPARE // 2, SPARE))

    def hop_one(g):
        pass_on(g, 0, kz, across)
        pass_on(g, 1, kz, right)
        pass_on(g, 2, kz, left)
        pass_on(g, 3, kz, twin)

    def hop_two(g):
        arrive(g, 0)
        pass_on(g, 4, across, right)
        pass_on(g, 5, across, left)
        pass_on(g, 6, across, twin)
        arrive(g, 1)
        pass_on(g, 7, left, right, halves[0])
        pass_on(g, 8, left, twin)
        arrive(g, 2)
        pass_on(g, 9, right, left, halves[1])
        pass_on(g, 10, right, twin)

    def hop_three(g):
        arrive(g, 4)
        pass_on(g, 11, left_across, right, halves[0])
        pass_on(g, 12, left_across, twin)
        arrive(g, 5)
        pass_on(g, 13, right_across, left, halves[1])
        pass_on(g, 14, right_across, twin)
        arrive(g, 7)
        pass_on(g, 15, far, twin, halves[0])
        arrive(g, 9)
        pass_on(g, 16, far, twin, halves[1])

    def hop_four(g):
        arrive(g, 11)
        pass_on(g, 17, far_across, twin, halves[0])
        arrive(g, 13)
        pass_on(g, 18, far_across, twin, halves[1])

    direct = {0: [], 1: []}

    def send_caps(g, pack):
        for r in range(1, SLABS):
            d = lax.rem(kz + r, SLABS)
            pack(rows[d], outbox, d)
            item = pltpu.make_async_remote_copy(
                src_ref=outbox.at[d, channels[g]], dst_ref=cap.at[kz, channels[g]],
                send_sem=cap_send.at[g, r], recv_sem=cap_recv.at[g, r],
                device_id={"kz": d}, device_id_type=MESH,
            )
            item.start()
            direct[g].append(item)
        pack(rows[kz], cap, kz)

    hop_one(0)
    labels = []
    for r in range(1, SLABS):
        d = lax.rem(kz + r, SLABS)
        item = pltpu.make_async_remote_copy(
            src_ref=table.at[d], dst_ref=tables.at[kz], send_sem=tab_send.at[r],
            recv_sem=tab_recv.at[r], device_id={"kz": d}, device_id_type=MESH,
        )
        item.start()
        labels.append(item)
    tables[kz] = table[kz]
    for j in range(SPARE):
        pack_signal(spare_rows[j], spare, kz * SPARE + j)
    hop_two(0)
    send_caps(0, pack_weight)
    hop_one(1)
    hop_three(0)
    for item in labels:
        item.wait()
    flag_ref[...] = jnp.max(tables[...], axis=0)

    k = lax.broadcasted_iota(jnp.int32, (1, KA), 1)
    slot, local = k // HALF, k % HALF
    other = slot - SLABS
    place = jnp.where(slot < SLABS, slot * 8, (other // SPARE) * 8 + 1 + other % SPARE)
    pick = (lax.broadcasted_iota(jnp.int32, (SLABS * 8, KA), 0) == place).astype(jnp.float32)
    spread = lax.dot_general(
        tables[...].reshape(SLABS * 8, 128).astype(jnp.bfloat16), pick.astype(jnp.bfloat16),
        (((0,), (0,)), ((), ())), preferred_element_type=jnp.float32,
    )

    def field(index):
        return spread[index : index + 1]

    plane, tilt, shift, helix = field(PLANE), field(TILT), field(SHIFT_Y), field(HELIX)
    live = jnp.where(field(DEST) == kz.astype(jnp.float32), field(VALID), 0.0)
    level = (lax.broadcasted_iota(jnp.int32, (16, 1), 0) - MZ).astype(jnp.float32)
    line = lax.broadcasted_iota(jnp.int32, (32, 1), 0)
    main_y = kaiser((line - 2 * local).astype(jnp.float32) - shift)
    low_y = kaiser((-1 - 2 * local).astype(jnp.float32) - shift)
    high_y = kaiser((32 - 2 * local).astype(jnp.float32) - shift)
    helices = lax.broadcasted_iota(jnp.int32, (16, 128), 1)
    bands = lax.broadcasted_iota(jnp.int32, (16, 128), 0) + kz * ZD - MZ
    angle = twist_step * (helices * bands).astype(jnp.float32)
    cos_of, sin_of = jnp.cos(angle), jnp.sin(angle)
    cosine = jnp.zeros((16, KA), jnp.float32)
    sine = jnp.zeros((16, KA), jnp.float32)
    for h in range(8):
        cosine = jnp.where(helix == float(h), cos_of[:, h : h + 1], cosine)
        sine = jnp.where(helix == float(h), sin_of[:, h : h + 1], sine)

    def along_z(q):
        row = ky * STRIP + q * HALF + local - SLICE // 2
        centre = plane + tilt * row.astype(jnp.float32) / (SLICE // 2)
        return kaiser(level - centre) * live

    blocks = [(MAIN, slice(0, 16), low_y), (MAIN + 16, slice(0, 16), high_y)]
    blocks += [(z * 32, slice(z, z + 1), main_y) for z in range(ZE)]

    def spread_slot(source, n, owner, index, first, group):
        taps = tables[owner, pl.ds(index, 1), :]
        wa, wb = taps[:, TAPS : TAPS + 1], taps[:, TAPS + 1 : TAPS + 2]
        wc, wd = taps[:, TAPS + 2 : TAPS + 3], taps[:, TAPS + 3 : TAPS + 4]
        for number, c in enumerate((2,) if group == 0 else (0, 1)):
            d = source[n, c].astype(jnp.float32)
            even = (wa * d + wb * pltpu.roll(d, 1, 1)).astype(jnp.bfloat16)
            odd = (wc * d + wd * pltpu.roll(d, SLICE - 1, 1)).astype(jnp.bfloat16)
            rows = pl.ds(pl.multiple_of(number * KA + first, HALF), HALF)
            target = bw if group == 0 else b
            for q in range(2):
                target[q, rows, 0:SLICE] = even[q * HALF : (q + 1) * HALF]
                target[q, rows, SLICE:GRID] = odd[q * HALF : (q + 1) * HALF]

    def spread_caps(group):
        for item in direct[group]:
            item.wait()

        @pl.loop(0, SLABS)
        def _(n):
            spread_slot(cap, n, n, 0, n * HALF, group)

    def spread_line(group, line_core):
        @pl.loop(0, SLABS // 2)
        def _(i):
            owner = 2 * i + line_core
            for j in range(SPARE):
                m = owner * SPARE + j
                spread_slot(spare, m, owner, 1 + j, (SLABS + m) * HALF, group)

    lines = lax.broadcasted_iota(jnp.int32, (1, 32, 1), 1)

    def multiply(c, left_side, right_side, rows):
        @pl.loop(0, GRID // 256)
        def _(tile):
            cols = pl.ds(pl.multiple_of(tile * 256, 256), 256)
            parts = [
                jnp.dot(
                    left_side[q, rows, :], right_side[q, :, cols],
                    preferred_element_type=jnp.float32,
                )
                for q in range(2)
            ]
            low = [part[MAIN : MAIN + ZE] for part in parts]
            high = [part[MAIN + 16 : MAIN + 16 + ZE] for part in parts]
            main = [part[:MAIN].reshape(ZE, 32, 256) for part in parts]
            main[0] = main[0] + jnp.where(lines == 31, low[1][:, None, :], 0.0)
            main[1] = main[1] + jnp.where(lines == 0, high[0][:, None, :], 0.0)
            for q in range(2):
                span = slice(q * 32, q * 32 + 32)
                dn[c, :, span, cols] = main[q][0:MZ].astype(jnp.bfloat16)
                mid[c, :, span, cols] = main[q][MZ : MZ + ZD]
                up[c, :, span, cols] = main[q][MZ + ZD :].astype(jnp.bfloat16)
            for j in range(3):
                edge[c, j, 0:ZD, cols] = low[0][j * 4 : j * 4 + 4]
                edge[c, 3 + j, 0:ZD, cols] = high[1][j * 4 : j * 4 + 4]

    def copy(source, target, number, peer):
        return pltpu.make_async_remote_copy(
            src_ref=source, dst_ref=target, send_sem=send.at[number], recv_sem=recv.at[number],
            device_id=peer, device_id_type=MESH,
        )

    def send_margins(c):
        items = [
            copy(up.at[c], from_low.at[c], 9 * c, {"kz": above, "ky": ky}),
            copy(dn.at[c], from_high.at[c], 9 * c + 1, {"kz": below, "ky": ky}),
        ]
        for j in range(3):
            for end, target in ((0, before), (1, after)):
                index = end * 3 + j
                items.append(
                    copy(
                        edge.at[c, index], halos.at[c, index], 9 * c + 2 + index,
                        {"kz": slabs[j], "ky": target},
                    )
                )
        for item in items:
            item.start()
        return items

    lower = jnp.where(kz > 0, 1.0, 0.0)
    upper = jnp.where(kz < 15, 1.0, 0.0)
    last_line = lax.broadcasted_iota(jnp.int32, (LINES, 1), 0)

    def finish(c, items):
        for item in items:
            item.wait()

        @pl.loop(0, ZD)
        def _(p):
            row = pl.ds(p, 1)
            total = mid[c, p] + lower * from_low[c, p].astype(jnp.float32)
            total = total + upper * from_high[c, p].astype(jnp.float32)
            last = upper * halos[c, 0, row, :] + halos[c, 1, row, :] + lower * halos[c, 2, row, :]
            start = upper * halos[c, 3, row, :] + halos[c, 4, row, :] + lower * halos[c, 5, row, :]
            total = total + jnp.where(last_line == LINES - 1, last, 0.0)
            total = total + jnp.where(last_line == 0, start, 0.0)
            half[c, pl.ds(pl.multiple_of(p * LINES, LINES), LINES), :] = total.astype(jnp.bfloat16)

        item = copy(half.at[c], mirror.at[c], 9 * c + 8, partner)
        item.start()
        return item

    for q in range(2):
        along = along_z(q)
        for first, levels, value_y in blocks:
            size = 16 if first >= MAIN else 32
            aw[q, first : first + size, :] = (along[levels] * value_y).astype(jnp.bfloat16)
    hop_four(0)
    hop_two(1)
    send_caps(1, pack_signal)
    spread_caps(0)
    spread_line(0, core)
    arrive(0, 3, 6, 8, 10, 12, 14, 15, 16, 17, 18)
    spread_line(0, 1 - core)
    hop_three(1)
    multiply(2, aw, bw, slice(0, MROWS))
    weight_items = send_margins(2)
    hop_four(1)
    spread_caps(1)
    for q in range(2):
        along = along_z(q)
        real, imag = along * cosine, along * sine
        for first, levels, value_y in blocks:
            size = 16 if first >= MAIN else 32
            rows_re = slice(first, first + size)
            rows_im = slice(MROWS + first, MROWS + first + size)
            kr = (real[levels] * value_y).astype(jnp.bfloat16)
            ki = imag[levels] * value_y
            a[q, rows_re, 0:KA] = kr
            a[q, rows_re, KA : 2 * KA] = (-ki).astype(jnp.bfloat16)
            a[q, rows_im, 0:KA] = ki.astype(jnp.bfloat16)
            a[q, rows_im, KA : 2 * KA] = kr
    spread_line(1, core)
    copies = {2: finish(2, weight_items)}
    arrive(1, 3, 6, 8, 10, 12, 14, 15, 16, 17, 18)
    spread_line(1, 1 - core)
    multiply(0, a, b, slice(0, MROWS))
    real_items = send_margins(0)
    multiply(1, a, b, slice(MROWS, 2 * MROWS))
    imag_items = send_margins(1)
    for item in sent.values():
        item.wait_send()

    @pl.loop(0, GRID // 128)
    def _(tile):
        rows = pl.multiple_of(tile * 128, 128)
        k = lax.broadcasted_iota(jnp.int32, (128, GRID), 0) + rows
        x = lax.broadcasted_iota(jnp.int32, (128, GRID), 1)
        wanted = jnp.where(k < SLICE, 2 * k, 2 * (k - SLICE) + 1)
        perm[pl.ds(rows, 128), :] = (x == wanted).astype(jnp.float32).astype(jnp.bfloat16)
        back[pl.ds(rows, 128), :] = (GRID - 1 - x == wanted).astype(jnp.float32).astype(jnp.bfloat16)

    copies[0] = finish(0, real_items)
    copies[1] = finish(1, imag_items)

    for c in range(3):

        @pl.loop(0, GRID // 256)
        def _(tile):
            cols = pl.ds(pl.multiple_of(tile * 256, 256), 256)
            own = jnp.dot(half[c], perm[:, cols], preferred_element_type=jnp.float32)
            own_ref[c, :, cols] = own.astype(jnp.bfloat16)

    i = lax.broadcasted_iota(jnp.int32, (256, 256), 0)
    j = lax.broadcasted_iota(jnp.int32, (256, 256), 1)
    flip = (i + j == 255).astype(jnp.float32).astype(jnp.bfloat16)
    for c in (2, 0, 1):
        copies[c].wait()
        turned = jnp.dot(flip, mirror[c], preferred_element_type=jnp.float32)
        mirror[c] = turned.astype(jnp.bfloat16)

        @pl.loop(0, GRID // 256)
        def _(tile):
            cols = pl.ds(pl.multiple_of(tile * 256, 256), 256)
            other = jnp.dot(mirror[c], back[:, cols], preferred_element_type=jnp.float32)
            back_ref[c, :, cols] = other.astype(jnp.bfloat16)


def whole(dest, plane, helix, tilt, shift, slice_re, slice_im, slice_ctf):
    vmem = pl.BlockSpec(memory_space=pltpu.VMEM)
    dma = pltpu.SemaphoreType.DMA
    bf16 = jnp.bfloat16
    slab = (3, ZD, LINES, GRID)
    flat = (3, ZD * LINES, GRID)
    slots = (3, STRIP, SLICE)
    return pl.pallas_call(
        whole_kernel,
        out_shape=(
            jax.ShapeDtypeStruct(flat, bf16),
            jax.ShapeDtypeStruct(flat, bf16),
            jax.ShapeDtypeStruct((8, 128), jnp.float32),
        ),
        in_specs=[pl.BlockSpec(memory_space=pltpu.SMEM)] + [vmem] * 8,
        out_specs=(vmem,) * 3,
        scratch_shapes=[
            pltpu.VMEM((SLABS, 8, 128), jnp.float32),
            pltpu.VMEM((SLABS, 8, 128), jnp.float32),
            pltpu.VMEM((SLABS, 128), jnp.float32),
            pltpu.SMEM((SLABS,), jnp.int32),
            pltpu.VMEM((SLABS,) + slots, bf16),
            pltpu.VMEM((SLABS,) + slots, bf16),
            pltpu.VMEM((SLABS * SPARE,) + slots, bf16),
            pltpu.VMEM((2, 2 * KA, GRID), bf16),
            pltpu.VMEM((2, KA, GRID), bf16),
            pltpu.VMEM((2, 2 * MROWS, 2 * KA), bf16),
            pltpu.VMEM((2, MROWS, KA), bf16),
            pltpu.VMEM(slab, jnp.float32),
            pltpu.VMEM(slab, bf16),
            pltpu.VMEM(slab, bf16),
            pltpu.VMEM((3, 6, 8, GRID), jnp.float32),
            pltpu.VMEM(slab, bf16),
            pltpu.VMEM(slab, bf16),
            pltpu.VMEM((3, 6, 8, GRID), jnp.float32),
            pltpu.VMEM(flat, bf16),
            pltpu.VMEM(flat, bf16),
            pltpu.VMEM((GRID, GRID), bf16),
            pltpu.VMEM((GRID, GRID), bf16),
            dma((27,)), dma((27,)), dma((2, 19)), dma((2, 19)),
            dma((2, SLABS)), dma((2, SLABS)), dma((SLABS,)), dma((SLABS,)),
        ],
        compiler_params=pltpu.CompilerParams(
            collective_id=3, has_side_effects=True, vmem_limit_bytes=63 << 20
        ),
        name="whole",
    )(
        dest.reshape(SLABS), dest.reshape(1, SLABS), plane.reshape(1, SLABS),
        helix.reshape(1, SLABS), tilt.reshape(1, SLABS), shift, slice_re, slice_im, slice_ctf,
    )


def per_device(*arguments):
    slice_re, slice_im, slice_ctf, dest, plane, helix, tilt, shift = arguments
    own, back, flag = whole(dest, plane, helix, tilt, shift, slice_re, slice_im, slice_ctf)
    signs = jnp.array([1.0, -1.0, 1.0], jnp.float32).reshape(3, 1, 1)

    def fold(own, back):
        out = own.astype(jnp.float32) + signs * back.astype(jnp.float32)
        return out.reshape(3, ZD, LINES, GRID)

    return lax.cond(
        flag[0, EXTRA] <= SPARE,
        lambda: fold(own, back),
        lambda: fold(*padded(*arguments)),
    )


def solution(mesh):
    placed = (
        P("kz", "ky", None),
        P("kz", "ky", None),
        P("kz", "ky", None),
        P("kz", None),
        P("kz"),
        P("kz"),
        P("kz"),
        P(None, "kz"),
    )
    return jax.shard_map(
        per_device, mesh=mesh, in_specs=placed, out_specs=P(None, "kz", "ky", None), check_vma=False
    )
```

```python
import functools
import math

import jax
import jax.numpy as jnp
from jax import lax
from jax.experimental import pallas as pl
from jax.experimental.pallas import tpu as pltpu
from jax.sharding import PartitionSpec as P

ZD = 4
MZ = 4
ZE = 12
CAP = 4
SLABS = 16
SLOTS = SLABS * CAP
SLICE = 512
GRID = 1024
SPARE = 4
ALL = SLABS * (1 + SPARE)
KA = ALL * 16
STRIP = 32
LINES = 64
HALF = 16
KC = SLOTS * HALF
MAIN = ZE * 32
MROWS = MAIN + 32

kernel_beta = 7.4
kernel_reach = 2.0
twist_step = 0.37

MESH = pl.DeviceIdType.MESH


def series(quarter):
    total = jnp.full_like(quarter, 1.0 / math.factorial(25) ** 2)
    for order in range(24, 0, -1):
        total = total * quarter + 1.0 / math.factorial(order) ** 2
    return total * quarter


SCALE = sum((kernel_beta * kernel_beta / 4) ** m / math.factorial(m) ** 2 for m in range(1, 26))


def kaiser(distance):
    inside = jnp.maximum(1.0 - distance * distance * 0.25, 0.0)
    return series(inside * (kernel_beta * kernel_beta * 0.25)) * (1.0 / SCALE)


def insert_kernel(count, w_ref, g_ref, cs_ref, pay_ref, mid_ref, up_ref, dn_ref, halo_ref, b, a):
    row_index = lax.axis_index("ky")

    @pl.loop(0, SLOTS)
    def _(n):
        wa, wb, wc, wd = w_ref[n, 0], w_ref[n, 1], w_ref[n, 2], w_ref[n, 3]
        for c in range(count):
            d = pay_ref[n, c].astype(jnp.float32)
            before = pltpu.roll(d, 1, 1)
            after = pltpu.roll(d, SLICE - 1, 1)
            even = (wa * d + wb * before).astype(jnp.bfloat16)
            odd = (wc * d + wd * after).astype(jnp.bfloat16)
            rows = pl.ds(pl.multiple_of(c * KC + n * HALF, HALF), HALF)
            for q in range(2):
                b[q, rows, 0:SLICE] = even[q * HALF : (q + 1) * HALF]
                b[q, rows, SLICE:GRID] = odd[q * HALF : (q + 1) * HALF]

    plane, live, tilt, shift = g_ref[0:1], g_ref[2:3], g_ref[3:4], g_ref[4:5]
    local = lax.broadcasted_iota(jnp.int32, (1, KC), 1) % HALF
    level = (lax.broadcasted_iota(jnp.int32, (16, 1), 0) - MZ).astype(jnp.float32)
    line = lax.broadcasted_iota(jnp.int32, (32, 1), 0)
    main_y = kaiser((line - 2 * local).astype(jnp.float32) - shift)
    low_y = kaiser((-1 - 2 * local).astype(jnp.float32) - shift)
    high_y = kaiser((32 - 2 * local).astype(jnp.float32) - shift)
    for q in range(2):
        row = row_index * STRIP + q * HALF + local - SLICE // 2
        centre = plane + tilt * row.astype(jnp.float32) / (SLICE // 2)
        along = kaiser(level - centre) * live
        parts = [(MAIN, slice(0, 16), low_y), (MAIN + 16, slice(0, 16), high_y)]
        parts += [(z * 32, slice(z, z + 1), main_y) for z in range(ZE)]
        if count == 2:
            real, imag = along * cs_ref[0:16], along * cs_ref[16:32]
        for first, levels, value_y in parts:
            size = 16 if first >= MAIN else 32
            rows = slice(first, first + size)
            again = slice(MROWS + first, MROWS + first + size)
            if count == 2:
                kr = (real[levels] * value_y).astype(jnp.bfloat16)
                ki = imag[levels] * value_y
                a[q, rows, 0:KC] = kr
                a[q, rows, KC : 2 * KC] = (-ki).astype(jnp.bfloat16)
                a[q, again, 0:KC] = ki.astype(jnp.bfloat16)
                a[q, again, KC : 2 * KC] = kr
            else:
                a[q, rows, :] = (along[levels] * value_y).astype(jnp.bfloat16)

    lines = lax.broadcasted_iota(jnp.int32, (1, 32, 1), 1)

    @pl.loop(0, GRID // 256)
    def _(tile):
        cols = pl.ds(pl.multiple_of(tile * 256, 256), 256)
        for c in range(count):
            parts = [
                jnp.dot(
                    a[q, c * MROWS : (c + 1) * MROWS, :],
                    b[q, :, cols],
                    preferred_element_type=jnp.float32,
                )
                for q in range(2)
            ]
            low = [part[MAIN : MAIN + ZE] for part in parts]
            high = [part[MAIN + 16 : MAIN + 16 + ZE] for part in parts]
            main = [part[:MAIN].reshape(ZE, 32, 256) for part in parts]
            main[0] = main[0] + jnp.where(lines == 31, low[1][:, None, :], 0.0)
            main[1] = main[1] + jnp.where(lines == 0, high[0][:, None, :], 0.0)
            for q in range(2):
                span = slice(q * 32, q * 32 + 32)
                dn_ref[c, :, span, cols] = main[q][0:MZ].astype(jnp.bfloat16)
                mid_ref[c, :, span, cols] = main[q][MZ : MZ + ZD]
                up_ref[c, :, span, cols] = main[q][MZ + ZD :].astype(jnp.bfloat16)
            for j in range(3):
                halo_ref[j, c * ZD : (c + 1) * ZD, cols] = low[0][j * 4 : j * 4 + 4]
                halo_ref[3 + j, c * ZD : (c + 1) * ZD, cols] = high[1][j * 4 : j * 4 + 4]


def insert(count, weights, geometry, phases, payload):
    vmem = pl.BlockSpec(memory_space=pltpu.VMEM)
    return pl.pallas_call(
        functools.partial(insert_kernel, count),
        out_shape=(
            jax.ShapeDtypeStruct((count, ZD, LINES, GRID), jnp.float32),
            jax.ShapeDtypeStruct((count, ZD, LINES, GRID), jnp.bfloat16),
            jax.ShapeDtypeStruct((count, ZD, LINES, GRID), jnp.bfloat16),
            jax.ShapeDtypeStruct((6, 8, GRID), jnp.float32),
        ),
        in_specs=[pl.BlockSpec(memory_space=pltpu.SMEM), vmem, vmem, vmem],
        out_specs=(vmem, vmem, vmem, vmem),
        scratch_shapes=[
            pltpu.VMEM((2, count * KC, GRID), jnp.bfloat16),
            pltpu.VMEM((2, count * MROWS, count * KC), jnp.bfloat16),
        ],
        compiler_params=pltpu.CompilerParams(vmem_limit_bytes=60 << 20),
        cost_estimate=pl.CostEstimate(
            flops=count * count * 4 * MROWS * KC * GRID, bytes_accessed=count * 5 << 20,
            transcendentals=0,
        ),
        name=f"insert{count}",
    )(weights, geometry, phases, payload)


def exchange_kernel(
    count, mid_ref, up_ref, dn_ref, halo_ref, own_ref, back_ref,
    from_low, from_high, halos, half, mirror, perm, back, send, recv,
):
    kz, ky = lax.axis_index("kz"), lax.axis_index("ky")
    above, below = lax.rem(kz + 1, 16), lax.rem(kz + 15, 16)
    after, before = lax.rem(ky + 1, 16), lax.rem(ky + 15, 16)
    partner = {"kz": 15 - kz, "ky": 15 - ky}
    slabs = (below, kz, above)
    peers = [{"kz": above, "ky": ky}, {"kz": below, "ky": ky}]
    peers += [{"kz": s, "ky": r} for s in slabs for r in (before, after)]
    peers += [partner]
    barrier = pltpu.get_barrier_semaphore()
    for peer in peers:
        pl.semaphore_signal(barrier, inc=1, device_id=peer, device_id_type=MESH)
    pl.semaphore_wait(barrier, len(peers))

    def copy(source, target, number, peer):
        return pltpu.make_async_remote_copy(
            src_ref=source, dst_ref=target, send_sem=send.at[number], recv_sem=recv.at[number],
            device_id=peer, device_id_type=MESH,
        )

    edges = []
    for j in range(3):
        for side, target in ((0, before), (1, after)):
            number = side * 3 + j
            edges.append(
                copy(
                    halo_ref.at[number], halos.at[number], number,
                    {"kz": slabs[j], "ky": target},
                )
            )
    margins = [
        (
            copy(up_ref.at[c], from_low.at[c], 6 + 2 * c, peers[0]),
            copy(dn_ref.at[c], from_high.at[c], 7 + 2 * c, peers[1]),
        )
        for c in range(count)
    ]
    for item in edges + [item for pair in margins for item in pair]:
        item.start()

    @pl.loop(0, GRID // 128)
    def _(tile):
        rows = pl.multiple_of(tile * 128, 128)
        k = lax.broadcasted_iota(jnp.int32, (128, GRID), 0) + rows
        x = lax.broadcasted_iota(jnp.int32, (128, GRID), 1)
        wanted = jnp.where(k < SLICE, 2 * k, 2 * (k - SLICE) + 1)
        perm[pl.ds(rows, 128), :] = (x == wanted).astype(jnp.float32).astype(jnp.bfloat16)
        back[pl.ds(rows, 128), :] = (GRID - 1 - x == wanted).astype(jnp.float32).astype(jnp.bfloat16)

    for item in edges:
        item.wait()

    lower = jnp.where(kz > 0, 1.0, 0.0)
    upper = jnp.where(kz < 15, 1.0, 0.0)
    lines = lax.broadcasted_iota(jnp.int32, (LINES, 1), 0)
    copies = []
    for c in range(count):
        for item in margins[c]:
            item.wait()

        @pl.loop(0, ZD)
        def _(p):
            row = pl.ds(c * ZD + p, 1)
            total = mid_ref[c, p] + lower * from_low[c, p].astype(jnp.float32)
            total = total + upper * from_high[c, p].astype(jnp.float32)
            last = upper * halos[0, row, :] + halos[1, row, :] + lower * halos[2, row, :]
            start = upper * halos[3, row, :] + halos[4, row, :] + lower * halos[5, row, :]
            total = total + jnp.where(lines == LINES - 1, last, 0.0)
            total = total + jnp.where(lines == 0, start, 0.0)
            half[c, pl.ds(pl.multiple_of(p * LINES, LINES), LINES), :] = total.astype(jnp.bfloat16)

        item = copy(half.at[c], mirror.at[c], 6 + 2 * count + c, partner)
        item.start()
        copies.append(item)

    for c in range(count):

        @pl.loop(0, GRID // 256)
        def _(tile):
            cols = pl.ds(pl.multiple_of(tile * 256, 256), 256)
            own = jnp.dot(half[c], perm[:, cols], preferred_element_type=jnp.float32)
            own_ref[c, :, cols] = own.astype(jnp.bfloat16)

    i = lax.broadcasted_iota(jnp.int32, (256, 256), 0)
    j = lax.broadcasted_iota(jnp.int32, (256, 256), 1)
    flip = (i + j == 255).astype(jnp.float32).astype(jnp.bfloat16)
    for c in range(count):
        copies[c].wait()
        turned = jnp.dot(flip, mirror[c], preferred_element_type=jnp.float32)
        mirror[c] = turned.astype(jnp.bfloat16)

        @pl.loop(0, GRID // 256)
        def _(tile):
            cols = pl.ds(pl.multiple_of(tile * 256, 256), 256)
            other = jnp.dot(mirror[c], back[:, cols], preferred_element_type=jnp.float32)
            back_ref[c, :, cols] = other.astype(jnp.bfloat16)


def exchange(mid, up, dn, halo):
    count = mid.shape[0]
    vmem = pl.BlockSpec(memory_space=pltpu.VMEM)
    return pl.pallas_call(
        functools.partial(exchange_kernel, count),
        out_shape=(jax.ShapeDtypeStruct((count, ZD * LINES, GRID), jnp.bfloat16),) * 2,
        in_specs=[vmem] * 4,
        out_specs=(vmem,) * 2,
        scratch_shapes=[
            pltpu.VMEM((count, ZD, LINES, GRID), jnp.bfloat16),
            pltpu.VMEM((count, ZD, LINES, GRID), jnp.bfloat16),
            pltpu.VMEM((6, 8, GRID), jnp.float32),
            pltpu.VMEM((count, ZD * LINES, GRID), jnp.bfloat16),
            pltpu.VMEM((count, ZD * LINES, GRID), jnp.bfloat16),
            pltpu.VMEM((GRID, GRID), jnp.bfloat16),
            pltpu.VMEM((GRID, GRID), jnp.bfloat16),
            pltpu.SemaphoreType.DMA((6 + 3 * count,)),
            pltpu.SemaphoreType.DMA((6 + 3 * count,)),
        ],
        compiler_params=pltpu.CompilerParams(
            collective_id=count, has_side_effects=True, vmem_limit_bytes=60 << 20
        ),
        cost_estimate=pl.CostEstimate(
            flops=count * 4 * 256 * GRID * GRID, bytes_accessed=count * 20 << 20, transcendentals=0
        ),
        name=f"exchange{count}",
    )(mid, up, dn, halo)


def padded(
    slice_re, slice_im, slice_ctf, slice_dest, slice_plane, helix_index, slice_tilt, slice_shift
):
    slab_index = lax.axis_index("kz")
    held_count = slice_re.shape[0]
    ctf = slice_ctf.astype(jnp.float32)
    square = (ctf * ctf).astype(jnp.bfloat16)[:, None]
    pair = jnp.stack(
        [ctf * slice_re.astype(jnp.float32), ctf * slice_im.astype(jnp.float32)], axis=1
    ).astype(jnp.bfloat16)
    ones = jnp.ones((held_count,), jnp.float32)
    zeros = jnp.zeros((held_count,), jnp.float32)
    geometry = jnp.stack(
        [
            slice_plane.astype(jnp.float32),
            helix_index.astype(jnp.float32),
            ones,
            slice_tilt.astype(jnp.float32),
            slice_shift[0].astype(jnp.float32),
            slice_shift[1].astype(jnp.float32),
            zeros,
            zeros,
        ],
        axis=1,
    ).astype(jnp.bfloat16)
    target = slice_dest[:, 0]
    onehot = (target[:, None] == jnp.arange(SLABS)[None, :]).astype(jnp.int32)
    ranking = jnp.sum((jnp.cumsum(onehot, axis=0) - 1) * onehot, axis=1)
    position = target * CAP + ranking
    matches = (jnp.arange(SLOTS)[:, None] == position[None, :]).astype(jnp.int32)
    occupied = jnp.sum(matches, axis=1) > 0
    source_row = jnp.sum(matches * jnp.arange(held_count)[None, :], axis=1)

    def dispatch(values):
        picked = jnp.take(values, source_row, axis=0, mode="clip")
        return lax.all_to_all(picked, "kz", split_axis=0, concat_axis=0, tiled=True)

    slots = jnp.where(occupied[:, None], jnp.take(geometry, source_row, axis=0, mode="clip"), 0)
    arrived = lax.all_to_all(slots, "kz", split_axis=0, concat_axis=0, tiled=True)
    square = dispatch(square)
    pair = dispatch(pair)
    arrived = arrived.astype(jnp.float32)
    offset = arrived[:, 5:6]
    weights = kaiser(jnp.array([[0.0, 2.0, 1.0, -1.0]]) - offset)
    weights = weights.astype(jnp.bfloat16).astype(jnp.float32)
    band = slab_index * ZD + jnp.arange(16) - MZ
    angle = twist_step * (arrived[:, 1].astype(jnp.int32)[None, :] * band[:, None]).astype(
        jnp.float32
    )
    phases = jnp.repeat(jnp.concatenate([jnp.cos(angle), jnp.sin(angle)], axis=0), HALF, axis=1)
    spread = jnp.repeat(arrived.T, HALF, axis=1)
    weight = exchange(*insert(1, weights, spread, phases, square))
    signal = exchange(*insert(2, weights, spread, phases, pair))
    return [jnp.concatenate(parts, axis=0) for parts in zip(signal, weight)]


PLANE, HELIX, VALID, TILT, SHIFT_Y, SHIFT_X, DEST, TAPS, EXTRA = 0, 1, 2, 3, 4, 5, 6, 8, 12


def whole_kernel(
    dest, dest_line, plane_line, helix_line, tilt_line, shift_lines, re_ref, im_ref, ctf_ref,
    own_ref, back_ref, flag_ref, tables, table, held, rows, outbox, cap, spare, b, bw, a, aw, mid, up, dn, edge, from_low, from_high, halos, half, mirror,
    perm, back, send, recv, hop_send, hop_recv, cap_send, cap_recv, tab_send, tab_recv,
):
    kz, ky = lax.axis_index("kz"), lax.axis_index("ky")
    side, core = kz // 8, lax.rem(kz, 2)
    column = lax.rem(kz, 8) // 2

    def at(other_side, x, c):
        return other_side * 8 + lax.rem(x + 4, 4) * 2 + c

    across, twin = at(1 - side, column, core), at(side, column, 1 - core)
    right, left = at(side, column + 1, core), at(side, column - 1, core)
    far = at(side, column + 2, core)
    right_across, left_across = at(1 - side, column + 1, core), at(1 - side, column - 1, core)
    far_across = at(1 - side, column + 2, core)

    above, below = lax.rem(kz + 1, 16), lax.rem(kz + 15, 16)
    after, before = lax.rem(ky + 1, 16), lax.rem(ky + 15, 16)
    partner = {"kz": 15 - kz, "ky": 15 - ky}
    slabs = (below, kz, above)
    peers = [{"kz": lax.rem(kz + r, SLABS), "ky": ky} for r in range(1, SLABS)]
    peers += [{"kz": s, "ky": r} for s in slabs for r in (before, after)]
    peers += [partner]
    barrier = pltpu.get_barrier_semaphore()
    for peer in peers:
        pl.semaphore_signal(barrier, inc=1, device_id=peer, device_id_type=MESH)

    first = []
    for d in range(SLABS):
        found = jnp.int32(SLABS)
        for i in reversed(range(SLABS)):
            found = jnp.where(dest[i] == d, i, found)
        first.append(found)
    extra = jnp.int32(0)
    spare_rows = [jnp.int32(0)] * SPARE
    for i in range(1, SLABS):
        again = dest[i] == dest[0]
        for earlier in range(1, i):
            again = again | (dest[i] == dest[earlier])
        for j in range(SPARE):
            spare_rows[j] = jnp.where(again & (extra == j), i, spare_rows[j])
        extra = extra + jnp.where(again, 1, 0)

    def pack_signal(row, target, place):
        ctf = ctf_ref[row].astype(jnp.float32)
        target[place, 0] = (ctf * re_ref[row].astype(jnp.float32)).astype(jnp.bfloat16)
        target[place, 1] = (ctf * im_ref[row].astype(jnp.float32)).astype(jnp.bfloat16)

    def pack_weight(row, target, place):
        ctf = ctf_ref[row].astype(jnp.float32)
        target[place, 2] = (ctf * ctf).astype(jnp.bfloat16)

    for j in range(SPARE):
        pack_weight(spare_rows[j], spare, kz * SPARE + j)

    lane = lax.broadcasted_iota(jnp.int32, (1, 128), 1)
    kind = lax.broadcasted_iota(jnp.int32, (8, SLABS), 0)
    fields = jnp.where(kind == VALID, 1.0, 0.0)
    shifts = shift_lines[...].astype(jnp.float32)
    for index, value in (
        (PLANE, plane_line[...].astype(jnp.float32)),
        (HELIX, helix_line[...].astype(jnp.float32)),
        (TILT, tilt_line[...].astype(jnp.float32)), (SHIFT_Y, shifts[0:1]),
        (SHIFT_X, shifts[1:2]), (DEST, dest_line[...].astype(jnp.float32)),
    ):
        fields = jnp.where(kind == index, value, fields)
    same = lax.broadcasted_iota(jnp.int32, (8, 128), 0) == lax.broadcasted_iota(
        jnp.int32, (8, 128), 1
    )
    notes = lax.dot_general(
        fields.astype(jnp.bfloat16), same.astype(jnp.float32).astype(jnp.bfloat16),
        (((0,), (0,)), ((), ())), preferred_element_type=jnp.float32,
    )
    lags = jnp.where(lane == TAPS + 1, 2.0, jnp.where(lane == TAPS + 2, 1.0, 0.0))
    lags = jnp.where(lane == TAPS + 3, -1.0, lags)
    taps = kaiser(lags - notes[:, SHIFT_X : SHIFT_X + 1])
    taps = taps.astype(jnp.bfloat16).astype(jnp.float32)
    held[...] = jnp.where((lane >= TAPS) & (lane < TAPS + 4), taps, notes)
    count = extra.astype(jnp.float32)
    shared = [jnp.zeros((1, 128), jnp.float32)]
    for j in range(SPARE):
        shared.append(jnp.where(extra > j, 1.0, 0.0) * held[pl.ds(spare_rows[j], 1), :])
    for d in range(SLABS):
        there = jnp.where(first[d] < SLABS, 1.0, 0.0)
        first[d] = jnp.where(first[d] < SLABS, first[d], 0)
        shared[0] = there * held[pl.ds(first[d], 1), :]
        for j in range(1 + SPARE):
            table[d, j : j + 1, :] = jnp.where(lane == EXTRA, count, shared[j])
        table[d, 1 + SPARE : 8, :] = jnp.zeros((7 - SPARE, 128), jnp.float32)
        rows[d] = first[d]
    pl.semaphore_wait(barrier, len(peers))

    channels = (slice(2, 3), slice(0, 2))
    sent = {}

    def pass_on(group, number, origin, target, part=(0, SPARE)):
        block = spare.at[pl.ds(origin * SPARE + part[0], part[1] - part[0]), channels[group]]
        item = pltpu.make_async_remote_copy(
            src_ref=block, dst_ref=block, send_sem=hop_send.at[group, number],
            recv_sem=hop_recv.at[group, number], device_id={"kz": target}, device_id_type=MESH,
        )
        item.start()
        sent[group, number] = item

    def arrive(group, *numbers):
        for number in numbers:
            sent[group, number].wait_recv()

    halves = ((0, SPARE // 2), (SPARE // 2, SPARE))

    def hop_one(g):
        pass_on(g, 0, kz, across)
        pass_on(g, 1, kz, right)
        pass_on(g, 2, kz, left)
        pass_on(g, 3, kz, twin)

    def hop_two(g):
        arrive(g, 0)
        pass_on(g, 4, across, right)
        pass_on(g, 5, across, left)
        pass_on(g, 6, across, twin)
        arrive(g, 1)
        pass_on(g, 7, left, right, halves[0])
        pass_on(g, 8, left, twin)
        arrive(g, 2)
        pass_on(g, 9, right, left, halves[1])
        pass_on(g, 10, right, twin)

    def hop_three(g):
        arrive(g, 4)
        pass_on(g, 11, left_across, right, halves[0])
        pass_on(g, 12, left_across, twin)
        arrive(g, 5)
        pass_on(g, 13, right_across, left, halves[1])
        pass_on(g, 14, right_across, twin)
        arrive(g, 7)
        pass_on(g, 15, far, twin, halves[0])
        arrive(g, 9)
        pass_on(g, 16, far, twin, halves[1])

    def hop_four(g):
        arrive(g, 11)
        pass_on(g, 17, far_across, twin, halves[0])
        arrive(g, 13)
        pass_on(g, 18, far_across, twin, halves[1])

    direct = {0: [], 1: []}

    def send_caps(g, pack):
        for r in range(1, SLABS):
            d = lax.rem(kz + r, SLABS)
            pack(rows[d], outbox, d)
            item = pltpu.make_async_remote_copy(
                src_ref=outbox.at[d, channels[g]], dst_ref=cap.at[kz, channels[g]],
                send_sem=cap_send.at[g, r], recv_sem=cap_recv.at[g, r],
                device_id={"kz": d}, device_id_type=MESH,
            )
            item.start()
            direct[g].append(item)
        pack(rows[kz], cap, kz)

    hop_one(0)
    labels = []
    for r in range(1, SLABS):
        d = lax.rem(kz + r, SLABS)
        item = pltpu.make_async_remote_copy(
            src_ref=table.at[d], dst_ref=tables.at[kz], send_sem=tab_send.at[r],
            recv_sem=tab_recv.at[r], device_id={"kz": d}, device_id_type=MESH,
        )
        item.start()
        labels.append(item)
    tables[kz] = table[kz]
    for j in range(SPARE):
        pack_signal(spare_rows[j], spare, kz * SPARE + j)
    hop_two(0)
    send_caps(0, pack_weight)
    hop_one(1)
    hop_three(0)
    for item in labels:
        item.wait()
    flag_ref[...] = jnp.max(tables[...], axis=0)

    k = lax.broadcasted_iota(jnp.int32, (1, KA), 1)
    slot, local = k // HALF, k % HALF
    other = slot - SLABS
    place = jnp.where(slot < SLABS, slot * 8, (other // SPARE) * 8 + 1 + other % SPARE)
    pick = (lax.broadcasted_iota(jnp.int32, (SLABS * 8, KA), 0) == place).astype(jnp.float32)
    spread = lax.dot_general(
        tables[...].reshape(SLABS * 8, 128).astype(jnp.bfloat16), pick.astype(jnp.bfloat16),
        (((0,), (0,)), ((), ())), preferred_element_type=jnp.float32,
    )

    def field(index):
        return spread[index : index + 1]

    plane, tilt, shift, helix = field(PLANE), field(TILT), field(SHIFT_Y), field(HELIX)
    live = jnp.where(field(DEST) == kz.astype(jnp.float32), field(VALID), 0.0)
    level = (lax.broadcasted_iota(jnp.int32, (16, 1), 0) - MZ).astype(jnp.float32)
    line = lax.broadcasted_iota(jnp.int32, (32, 1), 0)
    main_y = kaiser((line - 2 * local).astype(jnp.float32) - shift)
    low_y = kaiser((-1 - 2 * local).astype(jnp.float32) - shift)
    high_y = kaiser((32 - 2 * local).astype(jnp.float32) - shift)
    helices = lax.broadcasted_iota(jnp.int32, (16, 128), 1)
    bands = lax.broadcasted_iota(jnp.int32, (16, 128), 0) + kz * ZD - MZ
    angle = twist_step * (helices * bands).astype(jnp.float32)
    cos_of, sin_of = jnp.cos(angle), jnp.sin(angle)
    cosine = jnp.zeros((16, KA), jnp.float32)
    sine = jnp.zeros((16, KA), jnp.float32)
    for h in range(8):
        cosine = jnp.where(helix == float(h), cos_of[:, h : h + 1], cosine)
        sine = jnp.where(helix == float(h), sin_of[:, h : h + 1], sine)

    def along_z(q):
        row = ky * STRIP + q * HALF + local - SLICE // 2
        centre = plane + tilt * row.astype(jnp.float32) / (SLICE // 2)
        return kaiser(level - centre) * live

    blocks = [(MAIN, slice(0, 16), low_y), (MAIN + 16, slice(0, 16), high_y)]
    blocks += [(z * 32, slice(z, z + 1), main_y) for z in range(ZE)]

    def spread_slot(source, n, owner, index, first, group):
        taps = tables[owner, pl.ds(index, 1), :]
        wa, wb = taps[:, TAPS : TAPS + 1], taps[:, TAPS + 1 : TAPS + 2]
        wc, wd = taps[:, TAPS + 2 : TAPS + 3], taps[:, TAPS + 3 : TAPS + 4]
        for number, c in enumerate((2,) if group == 0 else (0, 1)):
            d = source[n, c].astype(jnp.float32)
            even = (wa * d + wb * pltpu.roll(d, 1, 1)).astype(jnp.bfloat16)
            odd = (wc * d + wd * pltpu.roll(d, SLICE - 1, 1)).astype(jnp.bfloat16)
            rows = pl.ds(pl.multiple_of(number * KA + first, HALF), HALF)
            target = bw if group == 0 else b
            for q in range(2):
                target[q, rows, 0:SLICE] = even[q * HALF : (q + 1) * HALF]
                target[q, rows, SLICE:GRID] = odd[q * HALF : (q + 1) * HALF]

    def spread_caps(group):
        for item in direct[group]:
            item.wait()

        @pl.loop(0, SLABS)
        def _(n):
            spread_slot(cap, n, n, 0, n * HALF, group)

    def spread_line(group, line_core):
        @pl.loop(0, SLABS // 2)
        def _(i):
            owner = 2 * i + line_core
            for j in range(SPARE):
                m = owner * SPARE + j
                spread_slot(spare, m, owner, 1 + j, (SLABS + m) * HALF, group)

    lines = lax.broadcasted_iota(jnp.int32, (1, 32, 1), 1)

    def multiply(c, left_side, right_side, rows):
        @pl.loop(0, GRID // 256)
        def _(tile):
            cols = pl.ds(pl.multiple_of(tile * 256, 256), 256)
            parts = [
                jnp.dot(
                    left_side[q, rows, :], right_side[q, :, cols],
                    preferred_element_type=jnp.float32,
                )
                for q in range(2)
            ]
            low = [part[MAIN : MAIN + ZE] for part in parts]
            high = [part[MAIN + 16 : MAIN + 16 + ZE] for part in parts]
            main = [part[:MAIN].reshape(ZE, 32, 256) for part in parts]
            main[0] = main[0] + jnp.where(lines == 31, low[1][:, None, :], 0.0)
            main[1] = main[1] + jnp.where(lines == 0, high[0][:, None, :], 0.0)
            for q in range(2):
                span = slice(q * 32, q * 32 + 32)
                dn[c, :, span, cols] = main[q][0:MZ].astype(jnp.bfloat16)
                mid[c, :, span, cols] = main[q][MZ : MZ + ZD]
                up[c, :, span, cols] = main[q][MZ + ZD :].astype(jnp.bfloat16)
            for j in range(3):
                edge[c, j, 0:ZD, cols] = low[0][j * 4 : j * 4 + 4]
                edge[c, 3 + j, 0:ZD, cols] = high[1][j * 4 : j * 4 + 4]

    def copy(source, target, number, peer):
        return pltpu.make_async_remote_copy(
            src_ref=source, dst_ref=target, send_sem=send.at[number], recv_sem=recv.at[number],
            device_id=peer, device_id_type=MESH,
        )

    def send_margins(c):
        items = [
            copy(up.at[c], from_low.at[c], 9 * c, {"kz": above, "ky": ky}),
            copy(dn.at[c], from_high.at[c], 9 * c + 1, {"kz": below, "ky": ky}),
        ]
        for j in range(3):
            for end, target in ((0, before), (1, after)):
                index = end * 3 + j
                items.append(
                    copy(
                        edge.at[c, index], halos.at[c, index], 9 * c + 2 + index,
                        {"kz": slabs[j], "ky": target},
                    )
                )
        for item in items:
            item.start()
        return items

    lower = jnp.where(kz > 0, 1.0, 0.0)
    upper = jnp.where(kz < 15, 1.0, 0.0)
    last_line = lax.broadcasted_iota(jnp.int32, (LINES, 1), 0)

    def finish(c, items):
        for item in items:
            item.wait()

        @pl.loop(0, ZD)
        def _(p):
            row = pl.ds(p, 1)
            total = mid[c, p] + lower * from_low[c, p].astype(jnp.float32)
            total = total + upper * from_high[c, p].astype(jnp.float32)
            last = upper * halos[c, 0, row, :] + halos[c, 1, row, :] + lower * halos[c, 2, row, :]
            start = upper * halos[c, 3, row, :] + halos[c, 4, row, :] + lower * halos[c, 5, row, :]
            total = total + jnp.where(last_line == LINES - 1, last, 0.0)
            total = total + jnp.where(last_line == 0, start, 0.0)
            half[c, pl.ds(pl.multiple_of(p * LINES, LINES), LINES), :] = total.astype(jnp.bfloat16)

        item = copy(half.at[c], mirror.at[c], 9 * c + 8, partner)
        item.start()
        return item

    for q in range(2):
        along = along_z(q)
        for first, levels, value_y in blocks:
            size = 16 if first >= MAIN else 32
            aw[q, first : first + size, :] = (along[levels] * value_y).astype(jnp.bfloat16)
    hop_four(0)
    hop_two(1)
    send_caps(1, pack_signal)
    spread_caps(0)
    spread_line(0, core)
    arrive(0, 3, 6, 8, 10, 12, 14, 15, 16, 17, 18)
    spread_line(0, 1 - core)
    hop_three(1)
    multiply(2, aw, bw, slice(0, MROWS))
    weight_items = send_margins(2)
    hop_four(1)
    copies = {2: finish(2, weight_items)}
    spread_caps(1)
    for q in range(2):
        along = along_z(q)
        real, imag = along * cosine, along * sine
        for first, levels, value_y in blocks:
            size = 16 if first >= MAIN else 32
            rows_re = slice(first, first + size)
            rows_im = slice(MROWS + first, MROWS + first + size)
            kr = (real[levels] * value_y).astype(jnp.bfloat16)
            ki = imag[levels] * value_y
            a[q, rows_re, 0:KA] = kr
            a[q, rows_re, KA : 2 * KA] = (-ki).astype(jnp.bfloat16)
            a[q, rows_im, 0:KA] = ki.astype(jnp.bfloat16)
            a[q, rows_im, KA : 2 * KA] = kr
    spread_line(1, core)
    arrive(1, 3, 6, 8, 10, 12, 14, 15, 16, 17, 18)
    spread_line(1, 1 - core)
    multiply(0, a, b, slice(0, MROWS))
    real_items = send_margins(0)
    multiply(1, a, b, slice(MROWS, 2 * MROWS))
    imag_items = send_margins(1)
    for item in sent.values():
        item.wait_send()

    @pl.loop(0, GRID // 128)
    def _(tile):
        rows = pl.multiple_of(tile * 128, 128)
        k = lax.broadcasted_iota(jnp.int32, (128, GRID), 0) + rows
        x = lax.broadcasted_iota(jnp.int32, (128, GRID), 1)
        wanted = jnp.where(k < SLICE, 2 * k, 2 * (k - SLICE) + 1)
        perm[pl.ds(rows, 128), :] = (x == wanted).astype(jnp.float32).astype(jnp.bfloat16)
        back[pl.ds(rows, 128), :] = (GRID - 1 - x == wanted).astype(jnp.float32).astype(jnp.bfloat16)

    copies[0] = finish(0, real_items)
    copies[1] = finish(1, imag_items)

    for c in range(3):

        @pl.loop(0, GRID // 256)
        def _(tile):
            cols = pl.ds(pl.multiple_of(tile * 256, 256), 256)
            own = jnp.dot(half[c], perm[:, cols], preferred_element_type=jnp.float32)
            own_ref[c, :, cols] = own.astype(jnp.bfloat16)

    i = lax.broadcasted_iota(jnp.int32, (256, 256), 0)
    j = lax.broadcasted_iota(jnp.int32, (256, 256), 1)
    flip = (i + j == 255).astype(jnp.float32).astype(jnp.bfloat16)
    for c in (2, 0, 1):
        copies[c].wait()
        turned = jnp.dot(flip, mirror[c], preferred_element_type=jnp.float32)
        mirror[c] = turned.astype(jnp.bfloat16)

        @pl.loop(0, GRID // 256)
        def _(tile):
            cols = pl.ds(pl.multiple_of(tile * 256, 256), 256)
            other = jnp.dot(mirror[c], back[:, cols], preferred_element_type=jnp.float32)
            back_ref[c, :, cols] = other.astype(jnp.bfloat16)


def whole(dest, plane, helix, tilt, shift, slice_re, slice_im, slice_ctf):
    vmem = pl.BlockSpec(memory_space=pltpu.VMEM)
    dma = pltpu.SemaphoreType.DMA
    bf16 = jnp.bfloat16
    slab = (3, ZD, LINES, GRID)
    flat = (3, ZD * LINES, GRID)
    slots = (3, STRIP, SLICE)
    return pl.pallas_call(
        whole_kernel,
        out_shape=(
            jax.ShapeDtypeStruct(flat, bf16),
            jax.ShapeDtypeStruct(flat, bf16),
            jax.ShapeDtypeStruct((8, 128), jnp.float32),
        ),
        in_specs=[pl.BlockSpec(memory_space=pltpu.SMEM)] + [vmem] * 8,
        out_specs=(vmem,) * 3,
        scratch_shapes=[
            pltpu.VMEM((SLABS, 8, 128), jnp.float32),
            pltpu.VMEM((SLABS, 8, 128), jnp.float32),
            pltpu.VMEM((SLABS, 128), jnp.float32),
            pltpu.SMEM((SLABS,), jnp.int32),
            pltpu.VMEM((SLABS,) + slots, bf16),
            pltpu.VMEM((SLABS,) + slots, bf16),
            pltpu.VMEM((SLABS * SPARE,) + slots, bf16),
            pltpu.VMEM((2, 2 * KA, GRID), bf16),
            pltpu.VMEM((2, KA, GRID), bf16),
            pltpu.VMEM((2, 2 * MROWS, 2 * KA), bf16),
            pltpu.VMEM((2, MROWS, KA), bf16),
            pltpu.VMEM(slab, jnp.float32),
            pltpu.VMEM(slab, bf16),
            pltpu.VMEM(slab, bf16),
            pltpu.VMEM((3, 6, 8, GRID), jnp.float32),
            pltpu.VMEM(slab, bf16),
            pltpu.VMEM(slab, bf16),
            pltpu.VMEM((3, 6, 8, GRID), jnp.float32),
            pltpu.VMEM(flat, bf16),
            pltpu.VMEM(flat, bf16),
            pltpu.VMEM((GRID, GRID), bf16),
            pltpu.VMEM((GRID, GRID), bf16),
            dma((27,)), dma((27,)), dma((2, 19)), dma((2, 19)),
            dma((2, SLABS)), dma((2, SLABS)), dma((SLABS,)), dma((SLABS,)),
        ],
        compiler_params=pltpu.CompilerParams(
            collective_id=3, has_side_effects=True, vmem_limit_bytes=63 << 20
        ),
        name="whole",
    )(
        dest.reshape(SLABS), dest.reshape(1, SLABS), plane.reshape(1, SLABS),
        helix.reshape(1, SLABS), tilt.reshape(1, SLABS), shift, slice_re, slice_im, slice_ctf,
    )


def per_device(*arguments):
    slice_re, slice_im, slice_ctf, dest, plane, helix, tilt, shift = arguments
    own, back, flag = whole(dest, plane, helix, tilt, shift, slice_re, slice_im, slice_ctf)
    signs = jnp.array([1.0, -1.0, 1.0], jnp.float32).reshape(3, 1, 1)

    def fold(own, back):
        out = own.astype(jnp.float32) + signs * back.astype(jnp.float32)
        return out.reshape(3, ZD, LINES, GRID)

    return lax.cond(
        flag[0, EXTRA] <= SPARE,
        lambda: fold(own, back),
        lambda: fold(*padded(*arguments)),
    )


def solution(mesh):
    placed = (
        P("kz", "ky", None),
        P("kz", "ky", None),
        P("kz", "ky", None),
        P("kz", None),
        P("kz"),
        P("kz"),
        P("kz"),
        P(None, "kz"),
    )
    return jax.shard_map(
        per_device, mesh=mesh, in_specs=placed, out_specs=P(None, "kz", "ky", None), check_vma=False
    )
```

```python
import functools
import math

import jax
import jax.numpy as jnp
from jax import lax
from jax.experimental import pallas as pl
from jax.experimental.pallas import tpu as pltpu
from jax.sharding import PartitionSpec as P

ZD = 4
MZ = 4
ZE = 12
CAP = 4
SLABS = 16
SLOTS = SLABS * CAP
SLICE = 512
GRID = 1024
SPARE = 4
ALL = SLABS * (1 + SPARE)
KA = ALL * 16
STRIP = 32
LINES = 64
HALF = 16
KC = SLOTS * HALF
MAIN = ZE * 32
MROWS = MAIN + 32

kernel_beta = 7.4
kernel_reach = 2.0
twist_step = 0.37

MESH = pl.DeviceIdType.MESH


def series(quarter):
    total = jnp.full_like(quarter, 1.0 / math.factorial(25) ** 2)
    for order in range(24, 0, -1):
        total = total * quarter + 1.0 / math.factorial(order) ** 2
    return total * quarter


SCALE = sum((kernel_beta * kernel_beta / 4) ** m / math.factorial(m) ** 2 for m in range(1, 26))


def kaiser(distance):
    inside = jnp.maximum(1.0 - distance * distance * 0.25, 0.0)
    return series(inside * (kernel_beta * kernel_beta * 0.25)) * (1.0 / SCALE)


def insert_kernel(count, w_ref, g_ref, cs_ref, pay_ref, mid_ref, up_ref, dn_ref, halo_ref, b, a):
    row_index = lax.axis_index("ky")

    @pl.loop(0, SLOTS)
    def _(n):
        wa, wb, wc, wd = w_ref[n, 0], w_ref[n, 1], w_ref[n, 2], w_ref[n, 3]
        for c in range(count):
            d = pay_ref[n, c].astype(jnp.float32)
            before = pltpu.roll(d, 1, 1)
            after = pltpu.roll(d, SLICE - 1, 1)
            even = (wa * d + wb * before).astype(jnp.bfloat16)
            odd = (wc * d + wd * after).astype(jnp.bfloat16)
            rows = pl.ds(pl.multiple_of(c * KC + n * HALF, HALF), HALF)
            for q in range(2):
                b[q, rows, 0:SLICE] = even[q * HALF : (q + 1) * HALF]
                b[q, rows, SLICE:GRID] = odd[q * HALF : (q + 1) * HALF]

    plane, live, tilt, shift = g_ref[0:1], g_ref[2:3], g_ref[3:4], g_ref[4:5]
    local = lax.broadcasted_iota(jnp.int32, (1, KC), 1) % HALF
    level = (lax.broadcasted_iota(jnp.int32, (16, 1), 0) - MZ).astype(jnp.float32)
    line = lax.broadcasted_iota(jnp.int32, (32, 1), 0)
    main_y = kaiser((line - 2 * local).astype(jnp.float32) - shift)
    low_y = kaiser((-1 - 2 * local).astype(jnp.float32) - shift)
    high_y = kaiser((32 - 2 * local).astype(jnp.float32) - shift)
    for q in range(2):
        row = row_index * STRIP + q * HALF + local - SLICE // 2
        centre = plane + tilt * row.astype(jnp.float32) / (SLICE // 2)
        along = kaiser(level - centre) * live
        parts = [(MAIN, slice(0, 16), low_y), (MAIN + 16, slice(0, 16), high_y)]
        parts += [(z * 32, slice(z, z + 1), main_y) for z in range(ZE)]
        if count == 2:
            real, imag = along * cs_ref[0:16], along * cs_ref[16:32]
        for first, levels, value_y in parts:
            size = 16 if first >= MAIN else 32
            rows = slice(first, first + size)
            again = slice(MROWS + first, MROWS + first + size)
            if count == 2:
                kr = (real[levels] * value_y).astype(jnp.bfloat16)
                ki = imag[levels] * value_y
                a[q, rows, 0:KC] = kr
                a[q, rows, KC : 2 * KC] = (-ki).astype(jnp.bfloat16)
                a[q, again, 0:KC] = ki.astype(jnp.bfloat16)
                a[q, again, KC : 2 * KC] = kr
            else:
                a[q, rows, :] = (along[levels] * value_y).astype(jnp.bfloat16)

    lines = lax.broadcasted_iota(jnp.int32, (1, 32, 1), 1)

    @pl.loop(0, GRID // 256)
    def _(tile):
        cols = pl.ds(pl.multiple_of(tile * 256, 256), 256)
        for c in range(count):
            parts = [
                jnp.dot(
                    a[q, c * MROWS : (c + 1) * MROWS, :],
                    b[q, :, cols],
                    preferred_element_type=jnp.float32,
                )
                for q in range(2)
            ]
            low = [part[MAIN : MAIN + ZE] for part in parts]
            high = [part[MAIN + 16 : MAIN + 16 + ZE] for part in parts]
            main = [part[:MAIN].reshape(ZE, 32, 256) for part in parts]
            main[0] = main[0] + jnp.where(lines == 31, low[1][:, None, :], 0.0)
            main[1] = main[1] + jnp.where(lines == 0, high[0][:, None, :], 0.0)
            for q in range(2):
                span = slice(q * 32, q * 32 + 32)
                dn_ref[c, :, span, cols] = main[q][0:MZ].astype(jnp.bfloat16)
                mid_ref[c, :, span, cols] = main[q][MZ : MZ + ZD]
                up_ref[c, :, span, cols] = main[q][MZ + ZD :].astype(jnp.bfloat16)
            for j in range(3):
                halo_ref[j, c * ZD : (c + 1) * ZD, cols] = low[0][j * 4 : j * 4 + 4]
                halo_ref[3 + j, c * ZD : (c + 1) * ZD, cols] = high[1][j * 4 : j * 4 + 4]


def insert(count, weights, geometry, phases, payload):
    vmem = pl.BlockSpec(memory_space=pltpu.VMEM)
    return pl.pallas_call(
        functools.partial(insert_kernel, count),
        out_shape=(
            jax.ShapeDtypeStruct((count, ZD, LINES, GRID), jnp.float32),
            jax.ShapeDtypeStruct((count, ZD, LINES, GRID), jnp.bfloat16),
            jax.ShapeDtypeStruct((count, ZD, LINES, GRID), jnp.bfloat16),
            jax.ShapeDtypeStruct((6, 8, GRID), jnp.float32),
        ),
        in_specs=[pl.BlockSpec(memory_space=pltpu.SMEM), vmem, vmem, vmem],
        out_specs=(vmem, vmem, vmem, vmem),
        scratch_shapes=[
            pltpu.VMEM((2, count * KC, GRID), jnp.bfloat16),
            pltpu.VMEM((2, count * MROWS, count * KC), jnp.bfloat16),
        ],
        compiler_params=pltpu.CompilerParams(vmem_limit_bytes=60 << 20),
        cost_estimate=pl.CostEstimate(
            flops=count * count * 4 * MROWS * KC * GRID, bytes_accessed=count * 5 << 20,
            transcendentals=0,
        ),
        name=f"insert{count}",
    )(weights, geometry, phases, payload)


def exchange_kernel(
    count, mid_ref, up_ref, dn_ref, halo_ref, own_ref, back_ref,
    from_low, from_high, halos, half, mirror, perm, back, send, recv,
):
    kz, ky = lax.axis_index("kz"), lax.axis_index("ky")
    above, below = lax.rem(kz + 1, 16), lax.rem(kz + 15, 16)
    after, before = lax.rem(ky + 1, 16), lax.rem(ky + 15, 16)
    partner = {"kz": 15 - kz, "ky": 15 - ky}
    slabs = (below, kz, above)
    peers = [{"kz": above, "ky": ky}, {"kz": below, "ky": ky}]
    peers += [{"kz": s, "ky": r} for s in slabs for r in (before, after)]
    peers += [partner]
    barrier = pltpu.get_barrier_semaphore()
    for peer in peers:
        pl.semaphore_signal(barrier, inc=1, device_id=peer, device_id_type=MESH)
    pl.semaphore_wait(barrier, len(peers))

    def copy(source, target, number, peer):
        return pltpu.make_async_remote_copy(
            src_ref=source, dst_ref=target, send_sem=send.at[number], recv_sem=recv.at[number],
            device_id=peer, device_id_type=MESH,
        )

    edges = []
    for j in range(3):
        for side, target in ((0, before), (1, after)):
            number = side * 3 + j
            edges.append(
                copy(
                    halo_ref.at[number], halos.at[number], number,
                    {"kz": slabs[j], "ky": target},
                )
            )
    margins = [
        (
            copy(up_ref.at[c], from_low.at[c], 6 + 2 * c, peers[0]),
            copy(dn_ref.at[c], from_high.at[c], 7 + 2 * c, peers[1]),
        )
        for c in range(count)
    ]
    for item in edges + [item for pair in margins for item in pair]:
        item.start()

    @pl.loop(0, GRID // 128)
    def _(tile):
        rows = pl.multiple_of(tile * 128, 128)
        k = lax.broadcasted_iota(jnp.int32, (128, GRID), 0) + rows
        x = lax.broadcasted_iota(jnp.int32, (128, GRID), 1)
        wanted = jnp.where(k < SLICE, 2 * k, 2 * (k - SLICE) + 1)
        perm[pl.ds(rows, 128), :] = (x == wanted).astype(jnp.float32).astype(jnp.bfloat16)
        back[pl.ds(rows, 128), :] = (GRID - 1 - x == wanted).astype(jnp.float32).astype(jnp.bfloat16)

    for item in edges:
        item.wait()

    lower = jnp.where(kz > 0, 1.0, 0.0)
    upper = jnp.where(kz < 15, 1.0, 0.0)
    lines = lax.broadcasted_iota(jnp.int32, (LINES, 1), 0)
    copies = []
    for c in range(count):
        for item in margins[c]:
            item.wait()

        @pl.loop(0, ZD)
        def _(p):
            row = pl.ds(c * ZD + p, 1)
            total = mid_ref[c, p] + lower * from_low[c, p].astype(jnp.float32)
            total = total + upper * from_high[c, p].astype(jnp.float32)
            last = upper * halos[0, row, :] + halos[1, row, :] + lower * halos[2, row, :]
            start = upper * halos[3, row, :] + halos[4, row, :] + lower * halos[5, row, :]
            total = total + jnp.where(lines == LINES - 1, last, 0.0)
            total = total + jnp.where(lines == 0, start, 0.0)
            half[c, pl.ds(pl.multiple_of(p * LINES, LINES), LINES), :] = total.astype(jnp.bfloat16)

        item = copy(half.at[c], mirror.at[c], 6 + 2 * count + c, partner)
        item.start()
        copies.append(item)

    for c in range(count):

        @pl.loop(0, GRID // 256)
        def _(tile):
            cols = pl.ds(pl.multiple_of(tile * 256, 256), 256)
            own = jnp.dot(half[c], perm[:, cols], preferred_element_type=jnp.float32)
            own_ref[c, :, cols] = own.astype(jnp.bfloat16)

    i = lax.broadcasted_iota(jnp.int32, (256, 256), 0)
    j = lax.broadcasted_iota(jnp.int32, (256, 256), 1)
    flip = (i + j == 255).astype(jnp.float32).astype(jnp.bfloat16)
    for c in range(count):
        copies[c].wait()
        turned = jnp.dot(flip, mirror[c], preferred_element_type=jnp.float32)
        mirror[c] = turned.astype(jnp.bfloat16)

        @pl.loop(0, GRID // 256)
        def _(tile):
            cols = pl.ds(pl.multiple_of(tile * 256, 256), 256)
            other = jnp.dot(mirror[c], back[:, cols], preferred_element_type=jnp.float32)
            back_ref[c, :, cols] = other.astype(jnp.bfloat16)


def exchange(mid, up, dn, halo):
    count = mid.shape[0]
    vmem = pl.BlockSpec(memory_space=pltpu.VMEM)
    return pl.pallas_call(
        functools.partial(exchange_kernel, count),
        out_shape=(jax.ShapeDtypeStruct((count, ZD * LINES, GRID), jnp.bfloat16),) * 2,
        in_specs=[vmem] * 4,
        out_specs=(vmem,) * 2,
        scratch_shapes=[
            pltpu.VMEM((count, ZD, LINES, GRID), jnp.bfloat16),
            pltpu.VMEM((count, ZD, LINES, GRID), jnp.bfloat16),
            pltpu.VMEM((6, 8, GRID), jnp.float32),
            pltpu.VMEM((count, ZD * LINES, GRID), jnp.bfloat16),
            pltpu.VMEM((count, ZD * LINES, GRID), jnp.bfloat16),
            pltpu.VMEM((GRID, GRID), jnp.bfloat16),
            pltpu.VMEM((GRID, GRID), jnp.bfloat16),
            pltpu.SemaphoreType.DMA((6 + 3 * count,)),
            pltpu.SemaphoreType.DMA((6 + 3 * count,)),
        ],
        compiler_params=pltpu.CompilerParams(
            collective_id=count, has_side_effects=True, vmem_limit_bytes=60 << 20
        ),
        cost_estimate=pl.CostEstimate(
            flops=count * 4 * 256 * GRID * GRID, bytes_accessed=count * 20 << 20, transcendentals=0
        ),
        name=f"exchange{count}",
    )(mid, up, dn, halo)


def padded(
    slice_re, slice_im, slice_ctf, slice_dest, slice_plane, helix_index, slice_tilt, slice_shift
):
    slab_index = lax.axis_index("kz")
    held_count = slice_re.shape[0]
    ctf = slice_ctf.astype(jnp.float32)
    square = (ctf * ctf).astype(jnp.bfloat16)[:, None]
    pair = jnp.stack(
        [ctf * slice_re.astype(jnp.float32), ctf * slice_im.astype(jnp.float32)], axis=1
    ).astype(jnp.bfloat16)
    ones = jnp.ones((held_count,), jnp.float32)
    zeros = jnp.zeros((held_count,), jnp.float32)
    geometry = jnp.stack(
        [
            slice_plane.astype(jnp.float32),
            helix_index.astype(jnp.float32),
            ones,
            slice_tilt.astype(jnp.float32),
            slice_shift[0].astype(jnp.float32),
            slice_shift[1].astype(jnp.float32),
            zeros,
            zeros,
        ],
        axis=1,
    ).astype(jnp.bfloat16)
    target = slice_dest[:, 0]
    onehot = (target[:, None] == jnp.arange(SLABS)[None, :]).astype(jnp.int32)
    ranking = jnp.sum((jnp.cumsum(onehot, axis=0) - 1) * onehot, axis=1)
    position = target * CAP + ranking
    matches = (jnp.arange(SLOTS)[:, None] == position[None, :]).astype(jnp.int32)
    occupied = jnp.sum(matches, axis=1) > 0
    source_row = jnp.sum(matches * jnp.arange(held_count)[None, :], axis=1)

    def dispatch(values):
        picked = jnp.take(values, source_row, axis=0, mode="clip")
        return lax.all_to_all(picked, "kz", split_axis=0, concat_axis=0, tiled=True)

    slots = jnp.where(occupied[:, None], jnp.take(geometry, source_row, axis=0, mode="clip"), 0)
    arrived = lax.all_to_all(slots, "kz", split_axis=0, concat_axis=0, tiled=True)
    square = dispatch(square)
    pair = dispatch(pair)
    arrived = arrived.astype(jnp.float32)
    offset = arrived[:, 5:6]
    weights = kaiser(jnp.array([[0.0, 2.0, 1.0, -1.0]]) - offset)
    weights = weights.astype(jnp.bfloat16).astype(jnp.float32)
    band = slab_index * ZD + jnp.arange(16) - MZ
    angle = twist_step * (arrived[:, 1].astype(jnp.int32)[None, :] * band[:, None]).astype(
        jnp.float32
    )
    phases = jnp.repeat(jnp.concatenate([jnp.cos(angle), jnp.sin(angle)], axis=0), HALF, axis=1)
    spread = jnp.repeat(arrived.T, HALF, axis=1)
    weight = exchange(*insert(1, weights, spread, phases, square))
    signal = exchange(*insert(2, weights, spread, phases, pair))
    return [jnp.concatenate(parts, axis=0) for parts in zip(signal, weight)]


PLANE, HELIX, VALID, TILT, SHIFT_Y, SHIFT_X, DEST, TAPS, EXTRA = 0, 1, 2, 3, 4, 5, 6, 8, 12


def whole_kernel(
    dest, dest_line, plane_line, helix_line, tilt_line, shift_lines, re_ref, im_ref, ctf_ref,
    own_ref, back_ref, flag_ref, tables, table, held, rows, outbox, cap, spare, b, bw, a, aw, mid, up, dn, edge, from_low, from_high, halos, half, mirror,
    perm, back, send, recv, hop_send, hop_recv, cap_send, cap_recv, tab_send, tab_recv,
):
    kz, ky = lax.axis_index("kz"), lax.axis_index("ky")
    side, core = kz // 8, lax.rem(kz, 2)
    column = lax.rem(kz, 8) // 2

    def at(other_side, x, c):
        return other_side * 8 + lax.rem(x + 4, 4) * 2 + c

    across, twin = at(1 - side, column, core), at(side, column, 1 - core)
    right, left = at(side, column + 1, core), at(side, column - 1, core)
    far = at(side, column + 2, core)
    right_across, left_across = at(1 - side, column + 1, core), at(1 - side, column - 1, core)
    far_across = at(1 - side, column + 2, core)

    above, below = lax.rem(kz + 1, 16), lax.rem(kz + 15, 16)
    after, before = lax.rem(ky + 1, 16), lax.rem(ky + 15, 16)
    partner = {"kz": 15 - kz, "ky": 15 - ky}
    slabs = (below, kz, above)
    peers = [{"kz": lax.rem(kz + r, SLABS), "ky": ky} for r in range(1, SLABS)]
    peers += [{"kz": s, "ky": r} for s in slabs for r in (before, after)]
    peers += [partner]
    barrier = pltpu.get_barrier_semaphore()
    for peer in peers:
        pl.semaphore_signal(barrier, inc=1, device_id=peer, device_id_type=MESH)

    first = []
    for d in range(SLABS):
        found = jnp.int32(SLABS)
        for i in reversed(range(SLABS)):
            found = jnp.where(dest[i] == d, i, found)
        first.append(found)
    extra = jnp.int32(0)
    spare_rows = [jnp.int32(0)] * SPARE
    for i in range(1, SLABS):
        again = dest[i] == dest[0]
        for earlier in range(1, i):
            again = again | (dest[i] == dest[earlier])
        for j in range(SPARE):
            spare_rows[j] = jnp.where(again & (extra == j), i, spare_rows[j])
        extra = extra + jnp.where(again, 1, 0)

    def pack_signal(row, target, place):
        ctf = ctf_ref[row].astype(jnp.float32)
        target[place, 0] = (ctf * re_ref[row].astype(jnp.float32)).astype(jnp.bfloat16)
        target[place, 1] = (ctf * im_ref[row].astype(jnp.float32)).astype(jnp.bfloat16)

    def pack_weight(row, target, place):
        ctf = ctf_ref[row].astype(jnp.float32)
        target[place, 2] = (ctf * ctf).astype(jnp.bfloat16)

    for j in range(SPARE):
        pack_weight(spare_rows[j], spare, kz * SPARE + j)

    lane = lax.broadcasted_iota(jnp.int32, (1, 128), 1)
    kind = lax.broadcasted_iota(jnp.int32, (8, SLABS), 0)
    fields = jnp.where(kind == VALID, 1.0, 0.0)
    shifts = shift_lines[...].astype(jnp.float32)
    for index, value in (
        (PLANE, plane_line[...].astype(jnp.float32)),
        (HELIX, helix_line[...].astype(jnp.float32)),
        (TILT, tilt_line[...].astype(jnp.float32)), (SHIFT_Y, shifts[0:1]),
        (SHIFT_X, shifts[1:2]), (DEST, dest_line[...].astype(jnp.float32)),
    ):
        fields = jnp.where(kind == index, value, fields)
    same = lax.broadcasted_iota(jnp.int32, (8, 128), 0) == lax.broadcasted_iota(
        jnp.int32, (8, 128), 1
    )
    notes = lax.dot_general(
        fields.astype(jnp.bfloat16), same.astype(jnp.float32).astype(jnp.bfloat16),
        (((0,), (0,)), ((), ())), preferred_element_type=jnp.float32,
    )
    lags = jnp.where(lane == TAPS + 1, 2.0, jnp.where(lane == TAPS + 2, 1.0, 0.0))
    lags = jnp.where(lane == TAPS + 3, -1.0, lags)
    taps = kaiser(lags - notes[:, SHIFT_X : SHIFT_X + 1])
    taps = taps.astype(jnp.bfloat16).astype(jnp.float32)
    held[...] = jnp.where((lane >= TAPS) & (lane < TAPS + 4), taps, notes)
    count = extra.astype(jnp.float32)
    shared = [jnp.zeros((1, 128), jnp.float32)]
    for j in range(SPARE):
        shared.append(jnp.where(extra > j, 1.0, 0.0) * held[pl.ds(spare_rows[j], 1), :])
    for d in range(SLABS):
        there = jnp.where(first[d] < SLABS, 1.0, 0.0)
        first[d] = jnp.where(first[d] < SLABS, first[d], 0)
        shared[0] = there * held[pl.ds(first[d], 1), :]
        for j in range(1 + SPARE):
            table[d, j : j + 1, :] = jnp.where(lane == EXTRA, count, shared[j])
        table[d, 1 + SPARE : 8, :] = jnp.zeros((7 - SPARE, 128), jnp.float32)
        rows[d] = first[d]
    pl.semaphore_wait(barrier, len(peers))

    channels = (slice(2, 3), slice(0, 2))
    sent = {}

    def pass_on(group, number, origin, target, part=(0, SPARE)):
        block = spare.at[pl.ds(origin * SPARE + part[0], part[1] - part[0]), channels[group]]
        item = pltpu.make_async_remote_copy(
            src_ref=block, dst_ref=block, send_sem=hop_send.at[group, number],
            recv_sem=hop_recv.at[group, number], device_id={"kz": target}, device_id_type=MESH,
        )
        item.start()
        sent[group, number] = item

    def arrive(group, *numbers):
        for number in numbers:
            sent[group, number].wait_recv()

    halves = ((0, SPARE // 2), (SPARE // 2, SPARE))

    def hop_one(g):
        pass_on(g, 0, kz, across)
        pass_on(g, 1, kz, right)
        pass_on(g, 2, kz, left)
        pass_on(g, 3, kz, twin)

    def hop_two(g):
        arrive(g, 0)
        pass_on(g, 4, across, right)
        pass_on(g, 5, across, left)
        pass_on(g, 6, across, twin)
        arrive(g, 1)
        pass_on(g, 7, left, right, halves[0])
        pass_on(g, 8, left, twin)
        arrive(g, 2)
        pass_on(g, 9, right, left, halves[1])
        pass_on(g, 10, right, twin)

    def hop_three(g):
        arrive(g, 4)
        pass_on(g, 11, left_across, right, halves[0])
        pass_on(g, 12, left_across, twin)
        arrive(g, 5)
        pass_on(g, 13, right_across, left, halves[1])
        pass_on(g, 14, right_across, twin)
        arrive(g, 7)
        pass_on(g, 15, far, twin, halves[0])
        arrive(g, 9)
        pass_on(g, 16, far, twin, halves[1])

    def hop_four(g):
        arrive(g, 11)
        pass_on(g, 17, far_across, twin, halves[0])
        arrive(g, 13)
        pass_on(g, 18, far_across, twin, halves[1])

    direct = {0: [], 1: []}

    def send_caps(g, pack):
        for r in range(1, SLABS):
            d = lax.rem(kz + r, SLABS)
            pack(rows[d], outbox, d)
            item = pltpu.make_async_remote_copy(
                src_ref=outbox.at[d, channels[g]], dst_ref=cap.at[kz, channels[g]],
                send_sem=cap_send.at[g, r], recv_sem=cap_recv.at[g, r],
                device_id={"kz": d}, device_id_type=MESH,
            )
            item.start()
            direct[g].append(item)
        pack(rows[kz], cap, kz)

    hop_one(0)
    labels = []
    for r in range(1, SLABS):
        d = lax.rem(kz + r, SLABS)
        item = pltpu.make_async_remote_copy(
            src_ref=table.at[d], dst_ref=tables.at[kz], send_sem=tab_send.at[r],
            recv_sem=tab_recv.at[r], device_id={"kz": d}, device_id_type=MESH,
        )
        item.start()
        labels.append(item)
    tables[kz] = table[kz]
    for j in range(SPARE):
        pack_signal(spare_rows[j], spare, kz * SPARE + j)
    hop_two(0)
    send_caps(0, pack_weight)
    hop_one(1)
    hop_three(0)
    for item in labels:
        item.wait()
    flag_ref[...] = jnp.max(tables[...], axis=0)

    k = lax.broadcasted_iota(jnp.int32, (1, KA), 1)
    slot, local = k // HALF, k % HALF
    other = slot - SLABS
    place = jnp.where(slot < SLABS, slot * 8, (other // SPARE) * 8 + 1 + other % SPARE)
    pick = (lax.broadcasted_iota(jnp.int32, (SLABS * 8, KA), 0) == place).astype(jnp.float32)
    spread = lax.dot_general(
        tables[...].reshape(SLABS * 8, 128).astype(jnp.bfloat16), pick.astype(jnp.bfloat16),
        (((0,), (0,)), ((), ())), preferred_element_type=jnp.float32,
    )

    def field(index):
        return spread[index : index + 1]

    plane, tilt, shift, helix = field(PLANE), field(TILT), field(SHIFT_Y), field(HELIX)
    live = jnp.where(field(DEST) == kz.astype(jnp.float32), field(VALID), 0.0)
    level = (lax.broadcasted_iota(jnp.int32, (16, 1), 0) - MZ).astype(jnp.float32)
    line = lax.broadcasted_iota(jnp.int32, (32, 1), 0)
    main_y = kaiser((line - 2 * local).astype(jnp.float32) - shift)
    low_y = kaiser((-1 - 2 * local).astype(jnp.float32) - shift)
    high_y = kaiser((32 - 2 * local).astype(jnp.float32) - shift)
    helices = lax.broadcasted_iota(jnp.int32, (16, 128), 1)
    bands = lax.broadcasted_iota(jnp.int32, (16, 128), 0) + kz * ZD - MZ
    angle = twist_step * (helices * bands).astype(jnp.float32)
    cos_of, sin_of = jnp.cos(angle), jnp.sin(angle)
    cosine = jnp.zeros((16, KA), jnp.float32)
    sine = jnp.zeros((16, KA), jnp.float32)
    for h in range(8):
        cosine = jnp.where(helix == float(h), cos_of[:, h : h + 1], cosine)
        sine = jnp.where(helix == float(h), sin_of[:, h : h + 1], sine)

    def along_z(q):
        row = ky * STRIP + q * HALF + local - SLICE // 2
        centre = plane + tilt * row.astype(jnp.float32) / (SLICE // 2)
        return kaiser(level - centre) * live

    blocks = [(MAIN, slice(0, 16), low_y), (MAIN + 16, slice(0, 16), high_y)]
    blocks += [(z * 32, slice(z, z + 1), main_y) for z in range(ZE)]

    def spread_slot(source, n, owner, index, first, group):
        taps = tables[owner, pl.ds(index, 1), :]
        wa, wb = taps[:, TAPS : TAPS + 1], taps[:, TAPS + 1 : TAPS + 2]
        wc, wd = taps[:, TAPS + 2 : TAPS + 3], taps[:, TAPS + 3 : TAPS + 4]
        for number, c in enumerate((2,) if group == 0 else (0, 1)):
            d = source[n, c].astype(jnp.float32)
            even = (wa * d + wb * pltpu.roll(d, 1, 1)).astype(jnp.bfloat16)
            odd = (wc * d + wd * pltpu.roll(d, SLICE - 1, 1)).astype(jnp.bfloat16)
            rows = pl.ds(pl.multiple_of(number * KA + first, HALF), HALF)
            target = bw if group == 0 else b
            for q in range(2):
                target[q, rows, 0:SLICE] = even[q * HALF : (q + 1) * HALF]
                target[q, rows, SLICE:GRID] = odd[q * HALF : (q + 1) * HALF]

    def spread_caps(group):
        for item in direct[group]:
            item.wait()

        @pl.loop(0, SLABS)
        def _(n):
            spread_slot(cap, n, n, 0, n * HALF, group)

    def spread_line(group, line_core):
        @pl.loop(0, SLABS // 2)
        def _(i):
            owner = 2 * i + line_core
            for j in range(SPARE):
                m = owner * SPARE + j
                spread_slot(spare, m, owner, 1 + j, (SLABS + m) * HALF, group)

    lines = lax.broadcasted_iota(jnp.int32, (1, 32, 1), 1)

    def multiply(c, left_side, right_side, rows):
        @pl.loop(0, GRID // 256)
        def _(tile):
            cols = pl.ds(pl.multiple_of(tile * 256, 256), 256)
            parts = [
                jnp.dot(
                    left_side[q, rows, :], right_side[q, :, cols],
                    preferred_element_type=jnp.float32,
                )
                for q in range(2)
            ]
            low = [part[MAIN : MAIN + ZE] for part in parts]
            high = [part[MAIN + 16 : MAIN + 16 + ZE] for part in parts]
            main = [part[:MAIN].reshape(ZE, 32, 256) for part in parts]
            main[0] = main[0] + jnp.where(lines == 31, low[1][:, None, :], 0.0)
            main[1] = main[1] + jnp.where(lines == 0, high[0][:, None, :], 0.0)
            for q in range(2):
                span = slice(q * 32, q * 32 + 32)
                dn[c, :, span, cols] = main[q][0:MZ].astype(jnp.bfloat16)
                mid[c, :, span, cols] = main[q][MZ : MZ + ZD]
                up[c, :, span, cols] = main[q][MZ + ZD :].astype(jnp.bfloat16)
            for j in range(3):
                edge[c, j, 0:ZD, cols] = low[0][j * 4 : j * 4 + 4]
                edge[c, 3 + j, 0:ZD, cols] = high[1][j * 4 : j * 4 + 4]

    def copy(source, target, number, peer):
        return pltpu.make_async_remote_copy(
            src_ref=source, dst_ref=target, send_sem=send.at[number], recv_sem=recv.at[number],
            device_id=peer, device_id_type=MESH,
        )

    def send_margins(c):
        items = [
            copy(up.at[c], from_low.at[c], 9 * c, {"kz": above, "ky": ky}),
            copy(dn.at[c], from_high.at[c], 9 * c + 1, {"kz": below, "ky": ky}),
        ]
        for j in range(3):
            for end, target in ((0, before), (1, after)):
                index = end * 3 + j
                items.append(
                    copy(
                        edge.at[c, index], halos.at[c, index], 9 * c + 2 + index,
                        {"kz": slabs[j], "ky": target},
                    )
                )
        for item in items:
            item.start()
        return items

    lower = jnp.where(kz > 0, 1.0, 0.0)
    upper = jnp.where(kz < 15, 1.0, 0.0)
    last_line = lax.broadcasted_iota(jnp.int32, (LINES, 1), 0)

    def finish(c, items):
        for item in items:
            item.wait()

        @pl.loop(0, ZD)
        def _(p):
            row = pl.ds(p, 1)
            total = mid[c, p] + lower * from_low[c, p].astype(jnp.float32)
            total = total + upper * from_high[c, p].astype(jnp.float32)
            last = upper * halos[c, 0, row, :] + halos[c, 1, row, :] + lower * halos[c, 2, row, :]
            start = upper * halos[c, 3, row, :] + halos[c, 4, row, :] + lower * halos[c, 5, row, :]
            total = total + jnp.where(last_line == LINES - 1, last, 0.0)
            total = total + jnp.where(last_line == 0, start, 0.0)
            half[c, pl.ds(pl.multiple_of(p * LINES, LINES), LINES), :] = total.astype(jnp.bfloat16)

        item = copy(half.at[c], mirror.at[c], 9 * c + 8, partner)
        item.start()
        return item

    for q in range(2):
        along = along_z(q)
        for first, levels, value_y in blocks:
            size = 16 if first >= MAIN else 32
            aw[q, first : first + size, :] = (along[levels] * value_y).astype(jnp.bfloat16)
    hop_four(0)
    hop_two(1)
    send_caps(1, pack_signal)
    spread_caps(0)
    spread_line(0, core)
    arrive(0, 3, 6, 8, 10, 12, 14, 15, 16, 17, 18)
    spread_line(0, 1 - core)
    hop_three(1)
    multiply(2, aw, bw, slice(0, MROWS))
    weight_items = send_margins(2)
    hop_four(1)
    copies = {2: finish(2, weight_items)}
    spread_caps(1)
    for q in range(2):
        along = along_z(q)
        real, imag = along * cosine, along * sine
        for first, levels, value_y in blocks:
            size = 16 if first >= MAIN else 32
            rows_re = slice(first, first + size)
            rows_im = slice(MROWS + first, MROWS + first + size)
            kr = (real[levels] * value_y).astype(jnp.bfloat16)
            ki = imag[levels] * value_y
            a[q, rows_re, 0:KA] = kr
            a[q, rows_re, KA : 2 * KA] = (-ki).astype(jnp.bfloat16)
            a[q, rows_im, 0:KA] = ki.astype(jnp.bfloat16)
            a[q, rows_im, KA : 2 * KA] = kr
    spread_line(1, core)

    @pl.loop(0, GRID // 128)
    def _(tile):
        rows = pl.multiple_of(tile * 128, 128)
        k = lax.broadcasted_iota(jnp.int32, (128, GRID), 0) + rows
        x = lax.broadcasted_iota(jnp.int32, (128, GRID), 1)
        wanted = jnp.where(k < SLICE, 2 * k, 2 * (k - SLICE) + 1)
        perm[pl.ds(rows, 128), :] = (x == wanted).astype(jnp.float32).astype(jnp.bfloat16)
        back[pl.ds(rows, 128), :] = (GRID - 1 - x == wanted).astype(jnp.float32).astype(jnp.bfloat16)

    arrive(1, 3, 6, 8, 10, 12, 14, 15, 16, 17, 18)
    spread_line(1, 1 - core)
    multiply(0, a, b, slice(0, MROWS))
    real_items = send_margins(0)
    multiply(1, a, b, slice(MROWS, 2 * MROWS))
    imag_items = send_margins(1)
    for item in sent.values():
        item.wait_send()

    copies[0] = finish(0, real_items)
    copies[1] = finish(1, imag_items)

    for c in range(3):

        @pl.loop(0, GRID // 256)
        def _(tile):
            cols = pl.ds(pl.multiple_of(tile * 256, 256), 256)
            own = jnp.dot(half[c], perm[:, cols], preferred_element_type=jnp.float32)
            own_ref[c, :, cols] = own.astype(jnp.bfloat16)

    i = lax.broadcasted_iota(jnp.int32, (256, 256), 0)
    j = lax.broadcasted_iota(jnp.int32, (256, 256), 1)
    flip = (i + j == 255).astype(jnp.float32).astype(jnp.bfloat16)
    for c in (2, 0, 1):
        copies[c].wait()
        turned = jnp.dot(flip, mirror[c], preferred_element_type=jnp.float32)
        mirror[c] = turned.astype(jnp.bfloat16)

        @pl.loop(0, GRID // 256)
        def _(tile):
            cols = pl.ds(pl.multiple_of(tile * 256, 256), 256)
            other = jnp.dot(mirror[c], back[:, cols], preferred_element_type=jnp.float32)
            back_ref[c, :, cols] = other.astype(jnp.bfloat16)


def whole(dest, plane, helix, tilt, shift, slice_re, slice_im, slice_ctf):
    vmem = pl.BlockSpec(memory_space=pltpu.VMEM)
    dma = pltpu.SemaphoreType.DMA
    bf16 = jnp.bfloat16
    slab = (3, ZD, LINES, GRID)
    flat = (3, ZD * LINES, GRID)
    slots = (3, STRIP, SLICE)
    return pl.pallas_call(
        whole_kernel,
        out_shape=(
            jax.ShapeDtypeStruct(flat, bf16),
            jax.ShapeDtypeStruct(flat, bf16),
            jax.ShapeDtypeStruct((8, 128), jnp.float32),
        ),
        in_specs=[pl.BlockSpec(memory_space=pltpu.SMEM)] + [vmem] * 8,
        out_specs=(vmem,) * 3,
        scratch_shapes=[
            pltpu.VMEM((SLABS, 8, 128), jnp.float32),
            pltpu.VMEM((SLABS, 8, 128), jnp.float32),
            pltpu.VMEM((SLABS, 128), jnp.float32),
            pltpu.SMEM((SLABS,), jnp.int32),
            pltpu.VMEM((SLABS,) + slots, bf16),
            pltpu.VMEM((SLABS,) + slots, bf16),
            pltpu.VMEM((SLABS * SPARE,) + slots, bf16),
            pltpu.VMEM((2, 2 * KA, GRID), bf16),
            pltpu.VMEM((2, KA, GRID), bf16),
            pltpu.VMEM((2, 2 * MROWS, 2 * KA), bf16),
            pltpu.VMEM((2, MROWS, KA), bf16),
            pltpu.VMEM(slab, jnp.float32),
            pltpu.VMEM(slab, bf16),
            pltpu.VMEM(slab, bf16),
            pltpu.VMEM((3, 6, 8, GRID), jnp.float32),
            pltpu.VMEM(slab, bf16),
            pltpu.VMEM(slab, bf16),
            pltpu.VMEM((3, 6, 8, GRID), jnp.float32),
            pltpu.VMEM(flat, bf16),
            pltpu.VMEM(flat, bf16),
            pltpu.VMEM((GRID, GRID), bf16),
            pltpu.VMEM((GRID, GRID), bf16),
            dma((27,)), dma((27,)), dma((2, 19)), dma((2, 19)),
            dma((2, SLABS)), dma((2, SLABS)), dma((SLABS,)), dma((SLABS,)),
        ],
        compiler_params=pltpu.CompilerParams(
            collective_id=3, has_side_effects=True, vmem_limit_bytes=63 << 20
        ),
        name="whole",
    )(
        dest.reshape(SLABS), dest.reshape(1, SLABS), plane.reshape(1, SLABS),
        helix.reshape(1, SLABS), tilt.reshape(1, SLABS), shift, slice_re, slice_im, slice_ctf,
    )


def per_device(*arguments):
    slice_re, slice_im, slice_ctf, dest, plane, helix, tilt, shift = arguments
    own, back, flag = whole(dest, plane, helix, tilt, shift, slice_re, slice_im, slice_ctf)
    signs = jnp.array([1.0, -1.0, 1.0], jnp.float32).reshape(3, 1, 1)

    def fold(own, back):
        out = own.astype(jnp.float32) + signs * back.astype(jnp.float32)
        return out.reshape(3, ZD, LINES, GRID)

    return lax.cond(
        flag[0, EXTRA] <= SPARE,
        lambda: fold(own, back),
        lambda: fold(*padded(*arguments)),
    )


def solution(mesh):
    placed = (
        P("kz", "ky", None),
        P("kz", "ky", None),
        P("kz", "ky", None),
        P("kz", None),
        P("kz"),
        P("kz"),
        P("kz"),
        P(None, "kz"),
    )
    return jax.shard_map(
        per_device, mesh=mesh, in_specs=placed, out_specs=P(None, "kz", "ky", None), check_vma=False
    )
```
